128 devices in a mesh: band: 16 (over x, z_lo, core), grid: 8 (over y, z_hi).
Axes of the slice: x: 4, y: 4, z: 4 (z_hi: 2, z_lo: 2; z = z_hi * 2 + z_lo), core: 2. Of those that a mesh axis runs over, the one named last changes fastest.
Arguments:
- valence: bfloat16 [32, 2, 160, 160, 160], P('band', None, 'grid'), may hold values from -6 to 6
- conduction: bfloat16 [16, 2, 160, 160, 160], P('band', None, 'grid'), may hold values from -6 to 6
- val_energy: float32 [32], replicated, may hold values from -12 to -1
- cond_energy: float32 [16], replicated, may hold values from 1 to 16
- cond_band: int32 [16], P('band'), may hold values from 0 to 15, each once
- owners: int32 [2], replicated, may hold values from 0 to 15
- gvectors: int32 [3, 4096], replicated, may hold values from 0 to 159, as said below
Outputs:
- chi0: float32 [2, 4096, 4096], P(None, 'grid', 'band')
The draws below stay inside these ranges and needn't reach their ends.
Inputs may be any that keep to these rules, and one draw needn't show every extreme that they name: `gvectors`: the G-vectors are distinct; each component, read between -80 and 80, lies within -10 to 10. `owners`: each entry is an index along band. `cond_band`: A permutation of the global conduction band numbers.
All inputs are finite; a program needn't handle non-finite values.
Results may differ from the reference program's by a relative error of at most 0.0092.
Values may be sent and summed in bfloat16 or wider, within the bound.
No kernel may reach another device: no remote copies, remote signals or barrier semaphores. Data moves between devices by JAX's collectives and lax.ppermute only.
A program may use at most 192 MiB of HBM per device.

```python
import math
import jax
import jax.numpy as jnp
from jax import lax

NFFT = 160
NGS = 4096
GMAX = 10
VAL_DEV = 2
ROUNDS = 2
VAL = 32
COND = 16
PAIRS = 64
N_BAND = 16


def draw_gvectors(key, part):
    side = 2 * GMAX + 1
    chosen = jax.random.permutation(key, side * side * side)[:NGS].astype(jnp.int32)
    comp_first = chosen // (side * side) - GMAX
    comp_second = chosen // side % side - GMAX
    comp_third = chosen % side - GMAX
    return (jnp.stack([comp_first, comp_second, comp_third]) % NFFT).astype(jnp.int32)


def block_levels(stream_key, dims, pieces, least, largest):
    gain = 1.0
    for dim, parts in pieces:
        draws = jax.random.uniform(jax.random.fold_in(jax.random.fold_in(stream_key, 6), dim), (parts,), jnp.float32, least / len(pieces), largest / len(pieces))
        gain = gain * jnp.repeat(jnp.exp(draws), dims[dim] // parts).reshape((-1,) + (1,) * (len(dims) - 1 - dim))
    return gain


def noise(key, shape, deviation, limit, split=(), held_as=jnp.bfloat16):
    array = deviation * jax.random.normal(key, shape, jnp.float32)
    if split:
        array = array * block_levels(key, shape, split, -0.22, 0.18)
    return jnp.clip(array, -limit, limit).astype(held_as)


def setup_inputs(seed: int = 0) -> dict:
    seeds = jax.random.split(jax.random.key(seed), 8)
    valence = noise(seeds[0], (VAL, 2, NFFT, NFFT, NFFT), 1.0, 6.0, ((0, 16), (2, 8)))
    conduction = noise(seeds[1], (COND, 2, NFFT, NFFT, NFFT), 1.0, 6.0, ((0, 16), (2, 8)))
    val_energy = jnp.clip(jax.random.uniform(seeds[2], (VAL,), jnp.float32, -12.0, -1.0), -12.0, -1.0)
    cond_energy = jnp.clip(jax.random.uniform(seeds[3], (COND,), jnp.float32, 1.0, 16.0), 1.0, 16.0)
    cond_band = jax.random.permutation(seeds[4], COND).astype(jnp.int32)
    owners = jax.random.randint(seeds[5], (ROUNDS,), 0, N_BAND).astype(jnp.int32)
    gvectors = draw_gvectors(jax.random.fold_in(seeds[7], 71), 0)
    return dict(valence=valence, conduction=conduction, val_energy=val_energy, cond_energy=cond_energy, cond_band=cond_band, owners=owners, gvectors=gvectors)


def dft_tables(length):
    positions = jnp.arange(length, dtype=jnp.int32)
    phase_index = (positions[:, None] * positions[None, :]) % length
    angles = phase_index.astype(jnp.float32) * (2.0 * math.pi / length)
    return jnp.cos(angles).astype(jnp.bfloat16), jnp.sin(angles).astype(jnp.bfloat16)


def wide_table(cos_table, sin_table):
    top_half = jnp.concatenate([cos_table, -sin_table], axis=1)
    low_half = jnp.concatenate([sin_table, cos_table], axis=1)
    return jnp.concatenate([top_half, low_half], axis=0)


def plane_transform(density, wide, cos_table, sin_table):
    length = cos_table.shape[0]
    along_z = jnp.einsum("xyk,kq->xyq", density.astype(jnp.float32), wide.astype(jnp.float32)).astype(jnp.bfloat16)
    cos_part = jnp.einsum("xyk,yq->xqk", along_z.astype(jnp.float32), cos_table.astype(jnp.float32))
    sin_part = jnp.einsum("xyk,yq->xqk", along_z.astype(jnp.float32), sin_table.astype(jnp.float32))
    real_part = cos_part[..., :length] + sin_part[..., length:]
    imag_part = cos_part[..., length:] - sin_part[..., :length]
    return jnp.concatenate([real_part, imag_part], axis=-1).astype(jnp.bfloat16)


def pair_matrix(plane, gvectors, cos_table, sin_table):
    length = cos_table.shape[0]
    freq_x, freq_y, freq_z = gvectors[0], gvectors[1], gvectors[2]
    plane_re = plane[:, freq_y, freq_z].astype(jnp.float32)
    plane_im = plane[:, freq_y, freq_z + length].astype(jnp.float32)
    twiddle_cos = cos_table[:, freq_x].astype(jnp.float32)
    twiddle_sin = sin_table[:, freq_x].astype(jnp.float32)
    norm_factor = float(length) ** -1.5
    elem_re = jnp.sum(plane_re * twiddle_cos + plane_im * twiddle_sin, axis=0) * norm_factor
    elem_im = jnp.sum(plane_im * twiddle_cos - plane_re * twiddle_sin, axis=0) * norm_factor
    return jnp.stack([elem_re, elem_im])


def reference(valence, conduction, val_energy, cond_energy, cond_band, owners, gvectors):
    cos_table, sin_table = dft_tables(NFFT)
    wide = wide_table(cos_table, sin_table)
    cond_levels = cond_energy[cond_band]
    elem_list = []
    weight_list = []
    for round_no in range(ROUNDS):
        start = (owners[round_no] * VAL_DEV).astype(jnp.int32)
        round_bands = lax.dynamic_slice_in_dim(valence, start, VAL_DEV, 0)
        val_levels = lax.dynamic_slice_in_dim(val_energy, start, VAL_DEV, 0)
        for band_no in range(VAL_DEV):
            val_wave = round_bands[band_no].astype(jnp.float32)

            def pair_elements(cond_wave):
                cond_f = cond_wave.astype(jnp.float32)
                dens_re = val_wave[0] * cond_f[0] + val_wave[1] * cond_f[1]
                dens_im = val_wave[0] * cond_f[1] - val_wave[1] * cond_f[0]
                density = jnp.concatenate([dens_re, dens_im], axis=-1).astype(jnp.bfloat16)
                plane = plane_transform(density, wide, cos_table, sin_table)
                return pair_matrix(plane, gvectors, cos_table, sin_table)

            elem_list.append(lax.map(pair_elements, conduction))
            weight_list.append(2.0 / (PAIRS * (val_levels[band_no] - cond_levels)))
    elements = jnp.concatenate(elem_list, axis=0)
    weight = jnp.concatenate(weight_list, axis=0)
    weighted = elements * weight[:, None, None]
    high = lax.Precision.HIGHEST
    chi_re = jnp.dot(weighted[:, 0].T, elements[:, 0], precision=high) + jnp.dot(weighted[:, 1].T, elements[:, 1], precision=high)
    chi_im = jnp.dot(weighted[:, 1].T, elements[:, 0], precision=high) - jnp.dot(weighted[:, 0].T, elements[:, 1], precision=high)
    return jnp.stack([chi_re, chi_im])
```

```python
import functools
import math

import jax
import jax.numpy as jnp
import numpy as np
from jax import lax
from jax.experimental import pallas as pl
from jax.experimental.pallas import tpu as pltpu
from jax.sharding import PartitionSpec as P

LENGTH = 160
GMAX = 10
SIDE = 2 * GMAX + 1
PARTS = 16
ROWS = 200
TAIL = 104
WIRE = 2 * ROWS + TAIL
PAIRS = 64
KROWS = 24
GCHUNK = 256
BF = jnp.bfloat16
F32 = jnp.float32


def host_tables():
    freq = (np.arange(SIDE) - GMAX) % LENGTH
    pos = np.arange(LENGTH)
    angle = ((freq[:, None] * pos[None, :]) % LENGTH).astype(np.float32) * np.float32(2.0 * math.pi / LENGTH)
    rnd = lambda a: a.astype(np.float32).astype(jnp.bfloat16).astype(np.float32)
    return rnd(np.cos(angle)), rnd(np.sin(angle))


def z_table():
    cos, sin = host_tables()
    out = np.zeros((2 * KROWS, 384), np.float32)
    cm, sm, ct, st = cos[:, :128], sin[:, :128], cos[:, 128:], sin[:, 128:]
    out[:SIDE] = np.concatenate([cm, sm, ct, ct, st, -st], axis=1)
    out[KROWS : KROWS + SIDE] = np.concatenate([-sm, cm, -st, -st, ct, -ct], axis=1)
    return out.astype(jnp.bfloat16)


def y_tables():
    cos, sin = host_tables()
    out = np.zeros((4, 256, 4, 32), np.float32)
    for shift in range(4):
        for row in range(ROWS):
            flat = 40 * shift + row
            x, y = divmod(flat, LENGTH)
            out[shift, row, 2 * x, :SIDE] = cos[:, y]
            out[shift, row, 2 * x + 1, :SIDE] = sin[:, y]
    return out.reshape(4, 256, 128).astype(jnp.bfloat16)


def pack_kernel(number_ref, cond_ref, val_ref, out_ref):
    number = number_ref[0].astype(F32)
    for band in range(3):
        src = cond_ref if band == 0 else val_ref.at[band - 1]
        real, imag = src[0], src[1]
        out_ref[0, band, 0:ROWS] = real[:, :128]
        out_ref[0, band, ROWS : 2 * ROWS] = imag[:, :128]
        tail = jnp.concatenate([real[:, 128:].astype(F32), imag[:, 128:].astype(F32)], axis=1)
        low = tail[:TAIL]
        fill = jnp.full((2 * TAIL - ROWS, 64), 1.0, F32) * number
        high = jnp.concatenate([tail[TAIL:], fill], axis=0)
        out_ref[0, band, 2 * ROWS :] = jnp.concatenate([low, high], axis=1).astype(BF)


def pack(conduction, valence, number):
    return pl.pallas_call(
        pack_kernel,
        out_shape=jax.ShapeDtypeStruct((PARTS, 3, WIRE, 128), BF),
        grid_spec=pltpu.PrefetchScalarGridSpec(
            num_scalar_prefetch=1,
            grid=(PARTS,),
            in_specs=[
                pl.BlockSpec((2, ROWS, LENGTH), lambda t, n: (0, t, 0)),
                pl.BlockSpec((2, 2, ROWS, LENGTH), lambda t, n: (0, 0, t, 0)),
            ],
            out_specs=pl.BlockSpec((1, 3, WIRE, 128), lambda t, n: (t, 0, 0, 0)),
        ),
        name="pack",
    )(number, conduction, valence)


def unpack_tail(tail):
    return jnp.concatenate([tail[:, :64], tail[: ROWS - TAIL, 64:]], axis=0)


def z_kernel(own_ref, v0_ref, v1_ref, cond_ref, table_ref, out_ref, val_main, val_tail, low_ref, high_ref):
    step = pl.program_id(0)

    @pl.when(step == 0)
    def _():
        for i in range(4):
            src = (v0_ref if i < 2 else v1_ref).at[0, 1 + i % 2]
            val_main[i, 0] = src[0:ROWS].astype(F32)
            val_main[i, 1] = src[ROWS : 2 * ROWS].astype(F32)
            both = unpack_tail(src[2 * ROWS :].astype(F32))
            val_tail[i] = jnp.concatenate([both, both], axis=1)
        high_ref[...] = jnp.zeros_like(high_ref)

    cre = cond_ref[0, 0, 0:ROWS].astype(F32)
    cim = cond_ref[0, 0, ROWS : 2 * ROWS].astype(F32)
    both = unpack_tail(cond_ref[0, 0, 2 * ROWS :].astype(F32))
    ctail = jnp.concatenate([both, both[:, 32:], both[:, :32]], axis=1)
    for i in range(4):
        vre, vim = val_main[i, 0], val_main[i, 1]
        dre = vre * cre + vim * cim
        dim = vre * cim - vim * cre
        tail = val_tail[i] * ctail
        density = jnp.concatenate([dre, dim, tail], axis=1).astype(BF)
        along = lax.dot_general(
            table_ref[...], density, (((1,), (1,)), ((), ())), preferred_element_type=F32
        )
        for part in range(2):
            start = part * PAIRS + step * 4 + i
            piece = along[part * KROWS : (part + 1) * KROWS]
            low_ref[pl.ds(start, KROWS, stride=128), :] = piece[:, :128]
            high_ref[pl.ds(start, KROWS, stride=128), 0 : ROWS - 128] = piece[:, 128:]

    @pl.when(step == pl.num_programs(0) - 1)
    def _():
        out_ref[:, :128] = low_ref[...].astype(BF)
        out_ref[:, 128:] = high_ref[...].astype(BF)


def z_transform(wire, owners):
    return pl.pallas_call(
        z_kernel,
        out_shape=jax.ShapeDtypeStruct((KROWS * 128, 256), BF),
        grid_spec=pltpu.PrefetchScalarGridSpec(
            num_scalar_prefetch=1,
            grid=(PARTS,),
            in_specs=[
                pl.BlockSpec((1, 3, WIRE, 128), lambda c, o: (o[0], 0, 0, 0)),
                pl.BlockSpec((1, 3, WIRE, 128), lambda c, o: (o[1], 0, 0, 0)),
                pl.BlockSpec((1, 1, WIRE, 128), lambda c, o: (c, 0, 0, 0)),
                pl.BlockSpec((2 * KROWS, 384), lambda c, o: (0, 0)),
            ],
            out_specs=pl.BlockSpec((KROWS * 128, 256), lambda c, o: (0, 0)),
            scratch_shapes=[
                pltpu.VMEM((4, 2, ROWS, 128), F32),
                pltpu.VMEM((4, ROWS, 128), F32),
                pltpu.VMEM((KROWS * 128, 128), F32),
                pltpu.VMEM((KROWS * 128, 128), F32),
            ],
        ),
        compiler_params=pltpu.CompilerParams(vmem_limit_bytes=40 * 2**20),
        name="ztransform",
    )(owners, wire, wire, wire, jnp.asarray(z_table()))


def g_kernel(along_ref, ytab_ref, index_ref, phase_ref, out_ref, plane_ref):
    @pl.when(pl.program_id(0) == 0)
    def _():
        lane = lax.broadcasted_iota(jnp.int32, (256, 256), 1) // 32
        for tile in range(3):
            parts = [None] * 4
            for s in range(8):
                k = tile * 8 + s
                if k >= SIDE:
                    continue
                left = along_ref[k * 128 : (k + 1) * 128]
                for t in range(4):
                    right = jnp.where(lane == s, ytab_ref[t], jnp.zeros((256, 256), BF))
                    term = jnp.dot(left, right, preferred_element_type=F32)
                    parts[t] = term if parts[t] is None else parts[t] + term
            for x in range(2):
                c, s = parts[2 * x], parts[2 * x + 1]
                real = c[:PAIRS] + s[PAIRS:]
                imag = c[PAIRS:] - s[:PAIRS]
                block = jnp.concatenate([real, imag], axis=0)
                plane_ref[x, :, tile * 256 : (tile + 1) * 256] = block.astype(BF)

    row = lax.broadcasted_iota(jnp.int32, (768, GCHUNK), 0)
    pick = jnp.where(row == index_ref[0], 1.0, 0.0).astype(BF)
    real = jnp.zeros((PAIRS, GCHUNK), F32)
    imag = jnp.zeros((PAIRS, GCHUNK), F32)
    for x in range(2):
        at = jnp.dot(plane_ref[x], pick, preferred_element_type=F32)
        c = phase_ref[0, 2 * x : 2 * x + 1]
        s = phase_ref[0, 2 * x + 1 : 2 * x + 2]
        real = real + at[:PAIRS] * c + at[PAIRS:] * s
        imag = imag + at[PAIRS:] * c - at[:PAIRS] * s
    out_ref[0, :PAIRS] = real.astype(BF)
    out_ref[0, PAIRS:] = imag.astype(BF)


def g_elements(along, ytab, index, phase):
    chunks = index.shape[0]
    return pl.pallas_call(
        g_kernel,
        out_shape=jax.ShapeDtypeStruct((chunks, 128, GCHUNK), BF),
        grid=(chunks,),
        in_specs=[
            pl.BlockSpec((KROWS * 128, 256), lambda i: (0, 0)),
            pl.BlockSpec((4, 256, 256), lambda i: (0, 0, 0)),
            pl.BlockSpec((1, 1, GCHUNK), lambda i: (i, 0, 0)),
            pl.BlockSpec((1, 4, GCHUNK), lambda i: (i, 0, 0)),
        ],
        out_specs=pl.BlockSpec((1, 128, GCHUNK), lambda i: (i, 0, 0)),
        scratch_shapes=[pltpu.VMEM((2, 128, 768), BF)],
        compiler_params=pltpu.CompilerParams(vmem_limit_bytes=40 * 2**20),
        name="gelements",
    )(along, ytab, index, phase)


def shards(valence, conduction, val_energy, cond_energy, cond_band, owners, gvectors):
    grid_pos = lax.axis_index("grid")
    band_pos = lax.axis_index("band")
    x_local = valence.shape[2]
    n_grid = lax.axis_size("grid")

    wire = pack(
        conduction.reshape(2, x_local * LENGTH, LENGTH),
        valence.reshape(2, 2, x_local * LENGTH, LENGTH),
        cond_band,
    )
    wire = lax.all_to_all(wire, "band", 0, 0, tiled=True)

    numbers = wire[:, 0, WIRE - 1, 127].astype(jnp.int32)
    order = jnp.arange(cond_energy.shape[0], dtype=jnp.int32)
    levels = jnp.sum(jnp.where(numbers[:, None] == order[None, :], cond_energy[None, :], 0.0), axis=1)
    val_index = (owners[:, None] * 2 + jnp.arange(2, dtype=jnp.int32)[None, :]).reshape(4)
    val_levels = val_energy[val_index]
    weight = (2.0 / (PAIRS * (val_levels[None, :] - levels[:, None]))).reshape(PAIRS)

    along = z_transform(wire, owners)

    ytab = lax.dynamic_index_in_dim(jnp.asarray(y_tables()), band_pos % 4, 0, keepdims=False)
    ytab = jnp.tile(ytab.reshape(256, 4, 32).transpose(1, 0, 2), (1, 1, 8))
    signed = (gvectors + GMAX) % LENGTH
    index = (signed[2] * 32 + signed[1]).reshape(PARTS, 1, GCHUNK)
    x_first = grid_pos * x_local + 5 * (band_pos // 4) + band_pos % 4
    norm = float(LENGTH) ** (-1.5)
    waves = []
    for x in range(2):
        angle = (gvectors[0] * (x_first + x) % LENGTH).astype(F32) * (2.0 * math.pi / LENGTH)
        waves += [jnp.cos(angle), jnp.sin(angle)]
    phase = jnp.stack(waves).astype(BF).astype(F32) * norm
    phase = phase.reshape(4, PARTS, GCHUNK).transpose(1, 0, 2)
    parts = g_elements(along, ytab, index, phase)

    parts = lax.all_to_all(parts, "band", 0, 0, tiled=True)
    block = jnp.sum(parts.astype(F32), axis=0)
    zh_flip = [(g, g ^ 1) for g in range(n_grid)]
    y_flip = [(g, g ^ 2) for g in range(n_grid)]
    y_rest = [(g, 6 - (g & 6) + (g & 1)) for g in range(n_grid)]
    for perm in (zh_flip, y_flip, y_rest):
        block = block + lax.ppermute(block, "grid", perm)

    straight, crossed = [], []
    for b in range(PARTS):
        for g in range(n_grid):
            straight.append((b * n_grid + g, (2 * g + b % 2) * n_grid + b // 2))
            crossed.append((b * n_grid + g, (2 * g + 1 - b % 2) * n_grid + b // 2))
    same = lax.ppermute(block, ("band", "grid"), straight)
    other = lax.ppermute(block, ("band", "grid"), crossed)
    odd = (band_pos % 2) == 1
    first = jnp.where(odd, other, same)
    second = jnp.where(odd, same, other)
    rows = jnp.concatenate([first, second], axis=1)

    w2 = jnp.concatenate([weight, weight])[:, None]
    for_real = block * w2
    for_imag = jnp.concatenate([-for_real[PAIRS:], for_real[:PAIRS]], axis=0)
    high = lax.Precision.HIGHEST
    chi_re = jnp.einsum("pr,pc->rc", rows, for_real, precision=high)
    chi_im = jnp.einsum("pr,pc->rc", rows, for_imag, precision=high)
    return jnp.stack([chi_re, chi_im])


def solution(mesh):
    return jax.shard_map(
        shards,
        mesh=mesh,
        in_specs=(
            P("band", None, "grid", None, None),
            P("band", None, "grid", None, None),
            P(),
            P(),
            P("band"),
            P(),
            P(),
        ),
        out_specs=P(None, "grid", "band"),
        check_vma=False,
    )
```

```python
import functools
import math

import jax
import jax.numpy as jnp
import numpy as np
from jax import lax
from jax.experimental import pallas as pl
from jax.experimental.pallas import tpu as pltpu
from jax.sharding import PartitionSpec as P

LENGTH = 160
GMAX = 10
SIDE = 2 * GMAX + 1
PARTS = 16
ROWS = 200
TAIL = 104
WIRE = 2 * ROWS + TAIL
PAIRS = 64
KROWS = 24
GCHUNK = 256
BF = jnp.bfloat16
F32 = jnp.float32


def host_tables():
    freq = (np.arange(SIDE) - GMAX) % LENGTH
    pos = np.arange(LENGTH)
    angle = ((freq[:, None] * pos[None, :]) % LENGTH).astype(np.float32) * np.float32(2.0 * math.pi / LENGTH)
    rnd = lambda a: a.astype(np.float32).astype(jnp.bfloat16).astype(np.float32)
    return rnd(np.cos(angle)), rnd(np.sin(angle))


def z_table():
    cos, sin = host_tables()
    out = np.zeros((2 * KROWS, 384), np.float32)
    cm, sm, ct, st = cos[:, :128], sin[:, :128], cos[:, 128:], sin[:, 128:]
    out[:SIDE] = np.concatenate([cm, sm, ct, ct, st, -st], axis=1)
    out[KROWS : KROWS + SIDE] = np.concatenate([-sm, cm, -st, -st, ct, -ct], axis=1)
    return out.astype(jnp.bfloat16)


def y_tables():
    cos, sin = host_tables()
    out = np.zeros((4, 256, 4, 32), np.float32)
    for shift in range(4):
        for row in range(ROWS):
            flat = 40 * shift + row
            x, y = divmod(flat, LENGTH)
            out[shift, row, 2 * x, :SIDE] = cos[:, y]
            out[shift, row, 2 * x + 1, :SIDE] = sin[:, y]
    return out.reshape(4, 256, 128).astype(jnp.bfloat16)


def pack_band(src, out, fill):
    real, imag = src[0], src[1]
    out[0:ROWS] = real[:, :128]
    out[ROWS : 2 * ROWS] = imag[:, :128]
    tail = jnp.concatenate([real[:, 128:].astype(F32), imag[:, 128:].astype(F32)], axis=1)
    low = tail[:TAIL]
    high = jnp.concatenate([tail[TAIL:], jnp.full((2 * TAIL - ROWS, 64), 1.0, F32) * fill], axis=0)
    out[2 * ROWS :] = jnp.concatenate([low, high], axis=1).astype(BF)


def pack_cond_kernel(number_ref, cond_ref, out_ref):
    pack_band(cond_ref, out_ref.at[0], number_ref[0].astype(F32))


def pack_cond(conduction, number):
    return pl.pallas_call(
        pack_cond_kernel,
        out_shape=jax.ShapeDtypeStruct((PARTS, WIRE, 128), BF),
        grid_spec=pltpu.PrefetchScalarGridSpec(
            num_scalar_prefetch=1,
            grid=(PARTS,),
            in_specs=[pl.BlockSpec((2, ROWS, LENGTH), lambda t, n: (0, t, 0))],
            out_specs=pl.BlockSpec((1, WIRE, 128), lambda t, n: (t, 0, 0)),
        ),
        name="packcond",
    )(number, conduction)


def pack_val_kernel(core_ref, mine_ref, theirs_ref, mine_out, theirs_out):
    pack_band(mine_ref.at[0], mine_out.at[0], 0.0)
    pack_band(theirs_ref.at[0], theirs_out.at[0], 0.0)


def pack_val(valence, core):
    block = (1, 2, ROWS, LENGTH)
    out = jax.ShapeDtypeStruct((PARTS, WIRE, 128), BF)
    return pl.pallas_call(
        pack_val_kernel,
        out_shape=(out, out),
        grid_spec=pltpu.PrefetchScalarGridSpec(
            num_scalar_prefetch=1,
            grid=(PARTS,),
            in_specs=[
                pl.BlockSpec(block, lambda t, k: (k[0], 0, t, 0)),
                pl.BlockSpec(block, lambda t, k: (1 - k[0], 0, t, 0)),
            ],
            out_specs=[
                pl.BlockSpec((1, WIRE, 128), lambda t, k: (t, 0, 0)),
                pl.BlockSpec((1, WIRE, 128), lambda t, k: (t, 0, 0)),
            ],
        ),
        name="packval",
    )(core, valence, valence)


def unpack_tail(tail):
    return jnp.concatenate([tail[:, :64], tail[: ROWS - TAIL, 64:]], axis=0)


def z_kernel(chip_ref, v0_ref, v1_ref, cond_ref, table_ref, out_ref, val_main, val_tail, low_ref, high_ref):
    step = pl.program_id(0)

    @pl.when(step == 0)
    def _():
        for i in range(4):
            src = (v0_ref if i < 2 else v1_ref).at[i % 2]
            val_main[i, 0] = src[0:ROWS].astype(F32)
            val_main[i, 1] = src[ROWS : 2 * ROWS].astype(F32)
            both = unpack_tail(src[2 * ROWS :].astype(F32))
            val_tail[i] = jnp.concatenate([both, both], axis=1)
        high_ref[...] = jnp.zeros_like(high_ref)

    cre = cond_ref[0, 0:ROWS].astype(F32)
    cim = cond_ref[0, ROWS : 2 * ROWS].astype(F32)
    both = unpack_tail(cond_ref[0, 2 * ROWS :].astype(F32))
    ctail = jnp.concatenate([both, both[:, 32:], both[:, :32]], axis=1)
    for i in range(4):
        vre, vim = val_main[i, 0], val_main[i, 1]
        dre = vre * cre + vim * cim
        dim = vre * cim - vim * cre
        tail = val_tail[i] * ctail
        density = jnp.concatenate([dre, dim, tail], axis=1).astype(BF)
        along = lax.dot_general(
            table_ref[...], density, (((1,), (1,)), ((), ())), preferred_element_type=F32
        )
        for part in range(2):
            start = part * PAIRS + step * 4 + i
            piece = along[part * KROWS : (part + 1) * KROWS]
            low_ref[pl.ds(start, KROWS, stride=128), :] = piece[:, :128]
            high_ref[pl.ds(start, KROWS, stride=128), 0 : ROWS - 128] = piece[:, 128:]

    @pl.when(step == pl.num_programs(0) - 1)
    def _():
        out_ref[:, :128] = low_ref[...].astype(BF)
        out_ref[:, 128:] = high_ref[...].astype(BF)


def z_transform(chip, val_wire, second, cond_wire):
    return pl.pallas_call(
        z_kernel,
        out_shape=jax.ShapeDtypeStruct((KROWS * 128, 256), BF),
        grid_spec=pltpu.PrefetchScalarGridSpec(
            num_scalar_prefetch=1,
            grid=(PARTS,),
            in_specs=[
                pl.BlockSpec((2, WIRE, 128), lambda c, o: (o[0], 0, 0)),
                pl.BlockSpec((2, WIRE, 128), lambda c, o: (0, 0, 0)),
                pl.BlockSpec((1, WIRE, 128), lambda c, o: (c, 0, 0)),
                pl.BlockSpec((2 * KROWS, 384), lambda c, o: (0, 0)),
            ],
            out_specs=pl.BlockSpec((KROWS * 128, 256), lambda c, o: (0, 0)),
            scratch_shapes=[
                pltpu.VMEM((4, 2, ROWS, 128), F32),
                pltpu.VMEM((4, ROWS, 128), F32),
                pltpu.VMEM((KROWS * 128, 128), F32),
                pltpu.VMEM((KROWS * 128, 128), F32),
            ],
        ),
        compiler_params=pltpu.CompilerParams(vmem_limit_bytes=40 * 2**20),
        name="ztransform",
    )(chip, val_wire, second, cond_wire, jnp.asarray(z_table()))


def g_kernel(along_ref, ytab_ref, index_ref, phase_ref, out_ref, plane_ref):
    @pl.when(pl.program_id(0) == 0)
    def _():
        lane = lax.broadcasted_iota(jnp.int32, (256, 256), 1) // 32
        for tile in range(3):
            parts = [None] * 4
            for s in range(8):
                k = tile * 8 + s
                if k >= SIDE:
                    continue
                left = along_ref[k * 128 : (k + 1) * 128]
                for t in range(4):
                    right = jnp.where(lane == s, ytab_ref[t], jnp.zeros((256, 256), BF))
                    term = jnp.dot(left, right, preferred_element_type=F32)
                    parts[t] = term if parts[t] is None else parts[t] + term
            for x in range(2):
                c, s = parts[2 * x], parts[2 * x + 1]
                real = c[:PAIRS] + s[PAIRS:]
                imag = c[PAIRS:] - s[:PAIRS]
                block = jnp.concatenate([real, imag], axis=0)
                plane_ref[x, :, tile * 256 : (tile + 1) * 256] = block.astype(BF)

    row = lax.broadcasted_iota(jnp.int32, (768, GCHUNK), 0)
    pick = jnp.where(row == index_ref[0], 1.0, 0.0).astype(BF)
    real = jnp.zeros((PAIRS, GCHUNK), F32)
    imag = jnp.zeros((PAIRS, GCHUNK), F32)
    for x in range(2):
        at = jnp.dot(plane_ref[x], pick, preferred_element_type=F32)
        c = phase_ref[0, 2 * x : 2 * x + 1]
        s = phase_ref[0, 2 * x + 1 : 2 * x + 2]
        real = real + at[:PAIRS] * c + at[PAIRS:] * s
        imag = imag + at[PAIRS:] * c - at[:PAIRS] * s
    out_ref[0, :PAIRS] = real.astype(BF)
    out_ref[0, PAIRS:] = imag.astype(BF)


def g_elements(along, ytab, index, phase):
    chunks = index.shape[0]
    return pl.pallas_call(
        g_kernel,
        out_shape=jax.ShapeDtypeStruct((chunks, 128, GCHUNK), BF),
        grid=(chunks,),
        in_specs=[
            pl.BlockSpec((KROWS * 128, 256), lambda i: (0, 0)),
            pl.BlockSpec((4, 256, 256), lambda i: (0, 0, 0)),
            pl.BlockSpec((1, 1, GCHUNK), lambda i: (i, 0, 0)),
            pl.BlockSpec((1, 4, GCHUNK), lambda i: (i, 0, 0)),
        ],
        out_specs=pl.BlockSpec((1, 128, GCHUNK), lambda i: (i, 0, 0)),
        scratch_shapes=[pltpu.VMEM((2, 128, 768), BF)],
        compiler_params=pltpu.CompilerParams(vmem_limit_bytes=40 * 2**20),
        name="gelements",
    )(along, ytab, index, phase)


def shards(valence, conduction, val_energy, cond_energy, cond_band, owners, gvectors):
    grid_pos = lax.axis_index("grid")
    band_pos = lax.axis_index("band")
    x_local = valence.shape[2]
    n_grid = lax.axis_size("grid")

    rows_all = x_local * LENGTH
    cond_wire = pack_cond(conduction.reshape(2, rows_all, LENGTH), cond_band)
    cond_wire, core = lax.optimization_barrier((cond_wire, band_pos & 1))
    cond_wire = lax.all_to_all(cond_wire, "band", 0, 0, tiled=True)

    first, second = owners[0], owners[1]
    mine, theirs = pack_val(valence.reshape(2, 2, rows_all, LENGTH), core[None])
    sibling = lax.ppermute(theirs, "band", [(b, b ^ 1) for b in range(PARTS)])
    here = (first >> 1) == (band_pos >> 1)
    own = jnp.where(here, first == band_pos, second == band_pos)
    val_wire = lax.all_to_all(jnp.where(own, mine, sibling), "band", 0, 0, tiled=True)

    cond_wire, val_wire = lax.optimization_barrier((cond_wire, val_wire))

    def exchange_again(operands):
        mine, sibling, _ = operands
        again = lax.all_to_all(jnp.where(second == band_pos, mine, sibling), "band", 0, 0, tiled=True)
        return lax.dynamic_slice_in_dim(again, (second >> 1) * 2, 2, 0)

    def from_first(operands):
        return lax.dynamic_slice_in_dim(operands[2], (second >> 1) * 2, 2, 0)

    both = (first != second) & ((first >> 1) == (second >> 1))
    second_wire = lax.cond(both, exchange_again, from_first, (mine, sibling, val_wire))

    numbers = cond_wire[:, WIRE - 1, 127].astype(jnp.int32)
    order = jnp.arange(cond_energy.shape[0], dtype=jnp.int32)
    levels = jnp.sum(jnp.where(numbers[:, None] == order[None, :], cond_energy[None, :], 0.0), axis=1)
    val_index = (owners[:, None] * 2 + jnp.arange(2, dtype=jnp.int32)[None, :]).reshape(4)
    val_levels = val_energy[val_index]
    weight = (2.0 / (PAIRS * (val_levels[None, :] - levels[:, None]))).reshape(PAIRS)

    along = z_transform((first >> 1)[None], val_wire, second_wire, cond_wire)

    ytab = lax.dynamic_index_in_dim(jnp.asarray(y_tables()), (band_pos & 3), 0, keepdims=False)
    ytab = jnp.tile(ytab.reshape(256, 4, 32).transpose(1, 0, 2), (1, 1, 8))
    signed = (gvectors + GMAX) % LENGTH
    index = (signed[2] * 32 + signed[1]).reshape(PARTS, 1, GCHUNK)
    x_first = grid_pos * x_local + 5 * (band_pos >> 2) + (band_pos & 3)
    norm = float(LENGTH) ** (-1.5)
    waves = []
    for x in range(2):
        angle = (gvectors[0] * (x_first + x) % LENGTH).astype(F32) * (2.0 * math.pi / LENGTH)
        waves += [jnp.cos(angle), jnp.sin(angle)]
    phase = jnp.stack(waves).astype(BF).astype(F32) * norm
    phase = phase.reshape(4, PARTS, GCHUNK).transpose(1, 0, 2)
    parts = g_elements(along, ytab, index, phase)

    parts = lax.all_to_all(parts, "band", 0, 0, tiled=True)
    block = jnp.sum(parts.astype(F32), axis=0)
    zh_flip = [(g, g ^ 1) for g in range(n_grid)]
    y_flip = [(g, g ^ 2) for g in range(n_grid)]
    y_rest = [(g, 6 - (g & 6) + (g & 1)) for g in range(n_grid)]
    for perm in (zh_flip, y_flip, y_rest):
        block = block + lax.ppermute(block, "grid", perm)

    straight, crossed = [], []
    for b in range(PARTS):
        for g in range(n_grid):
            straight.append((b * n_grid + g, (2 * g + b % 2) * n_grid + b // 2))
            crossed.append((b * n_grid + g, (2 * g + 1 - b % 2) * n_grid + b // 2))
    block = block.astype(BF)
    same = lax.ppermute(block, ("band", "grid"), straight)
    other = lax.ppermute(block, ("band", "grid"), crossed)
    odd = (band_pos & 1) == 1
    left = jnp.where(odd, other, same)
    right = jnp.where(odd, same, other)
    rows = jnp.concatenate([left, right], axis=1).astype(F32)
    block = block.astype(F32)

    w2 = jnp.concatenate([weight, weight])[:, None]
    for_real = block * w2
    for_imag = jnp.concatenate([-for_real[PAIRS:], for_real[:PAIRS]], axis=0)
    high = lax.Precision.HIGHEST
    chi_re = jnp.einsum("pr,pc->rc", rows, for_real, precision=high)
    chi_im = jnp.einsum("pr,pc->rc", rows, for_imag, precision=high)
    return jnp.stack([chi_re, chi_im])


def solution(mesh):
    return jax.shard_map(
        shards,
        mesh=mesh,
        in_specs=(
            P("band", None, "grid", None, None),
            P("band", None, "grid", None, None),
            P(),
            P(),
            P("band"),
            P(),
            P(),
        ),
        out_specs=P(None, "grid", "band"),
        check_vma=False,
    )
```

```python
import functools
import math

import jax
import jax.numpy as jnp
import numpy as np
from jax import lax
from jax.experimental import pallas as pl
from jax.experimental.pallas import tpu as pltpu
from jax.sharding import PartitionSpec as P

LENGTH = 160
GMAX = 10
SIDE = 2 * GMAX + 1
PARTS = 16
ROWS = 200
TAIL = 104
WIRE = 2 * ROWS + TAIL
PAIRS = 64
PACK = 8
CONDS = 4
SLOTS = 12
KROWS = 24
GCHUNK = 256
BF = jnp.bfloat16
F32 = jnp.float32


def host_tables():
    freq = (np.arange(SIDE) - GMAX) % LENGTH
    pos = np.arange(LENGTH)
    angle = ((freq[:, None] * pos[None, :]) % LENGTH).astype(np.float32) * np.float32(2.0 * math.pi / LENGTH)
    rnd = lambda a: a.astype(np.float32).astype(jnp.bfloat16).astype(np.float32)
    return rnd(np.cos(angle)), rnd(np.sin(angle))


def z_table():
    cos, sin = host_tables()
    out = np.zeros((2 * KROWS, 384), np.float32)
    cm, sm, ct, st = cos[:, :128], sin[:, :128], cos[:, 128:], sin[:, 128:]
    out[:SIDE] = np.concatenate([cm, sm, ct, ct, st, -st], axis=1)
    out[KROWS : KROWS + SIDE] = np.concatenate([-sm, cm, -st, -st, ct, -ct], axis=1)
    return out.astype(jnp.bfloat16)


def y_tables():
    cos, sin = host_tables()
    out = np.zeros((4, 256, 4, 32), np.float32)
    for shift in range(4):
        for row in range(ROWS):
            flat = 40 * shift + row
            x, y = divmod(flat, LENGTH)
            out[shift, row, 2 * x, :SIDE] = cos[:, y]
            out[shift, row, 2 * x + 1, :SIDE] = sin[:, y]
    return out.reshape(4, 256, 128).astype(jnp.bfloat16)


def pack_band(src, out, fill):
    real, imag = src[0], src[1]
    out[0:ROWS] = real[:, :128]
    out[ROWS : 2 * ROWS] = imag[:, :128]
    tail = jnp.concatenate([real[:, 128:].astype(F32), imag[:, 128:].astype(F32)], axis=1)
    low = tail[:TAIL]
    high = jnp.concatenate([tail[TAIL:], jnp.full((2 * TAIL - ROWS, 64), 1.0, F32) * fill], axis=0)
    out[2 * ROWS :] = jnp.concatenate([low, high], axis=1).astype(BF)


def pack_cond_kernel(number_ref, cond_ref, out_ref):
    for t in range(PACK):
        rows = pl.ds(t * ROWS, ROWS)
        pack_band(cond_ref.at[:, rows], out_ref.at[t], number_ref[0].astype(F32))


def pack_cond(conduction, number):
    return pl.pallas_call(
        pack_cond_kernel,
        out_shape=jax.ShapeDtypeStruct((PARTS, WIRE, 128), BF),
        grid_spec=pltpu.PrefetchScalarGridSpec(
            num_scalar_prefetch=1,
            grid=(PARTS // PACK,),
            in_specs=[pl.BlockSpec((2, PACK * ROWS, LENGTH), lambda t, n: (0, t, 0))],
            out_specs=pl.BlockSpec((PACK, WIRE, 128), lambda t, n: (t, 0, 0)),
        ),
        cost_estimate=pl.CostEstimate(flops=0, transcendentals=0, bytes_accessed=6_000_000),
        name="packcond",
    )(number, conduction)


def pack_val_kernel(band_ref, val_ref, out_ref):
    for t in range(PACK):
        pack_band(val_ref.at[0, :, pl.ds(t * ROWS, ROWS)], out_ref.at[t], 0.0)


def pack_choice_kernel(band_ref, own_ref, val_ref, other_ref, out_ref):
    @pl.when(own_ref[0] == 1)
    def _():
        pack_val_kernel(band_ref, val_ref, out_ref)

    @pl.when(own_ref[0] == 0)
    def _():
        out_ref[...] = other_ref[...]


def pack_val(valence, band, own=None, other=None):
    wire_spec = pl.BlockSpec((PACK, WIRE, 128), lambda t, *_: (t, 0, 0))
    scalars, arrays, specs, kernel = (band,), (valence,), [], pack_val_kernel
    specs.append(pl.BlockSpec((1, 2, PACK * ROWS, LENGTH), lambda t, k, *_: (k[0], 0, t, 0)))
    if other is not None:
        scalars, arrays, kernel = (band, own), (valence, other), pack_choice_kernel
        specs.append(wire_spec)
    return pl.pallas_call(
        kernel,
        out_shape=jax.ShapeDtypeStruct((PARTS, WIRE, 128), BF),
        grid_spec=pltpu.PrefetchScalarGridSpec(
            num_scalar_prefetch=len(scalars),
            grid=(PARTS // PACK,),
            in_specs=specs,
            out_specs=wire_spec,
        ),
        cost_estimate=pl.CostEstimate(flops=0, transcendentals=0, bytes_accessed=8_000_000),
        compiler_params=pltpu.CompilerParams(vmem_limit_bytes=40 * 2**20),
        name="packval",
    )(*scalars, *arrays)


def unpack_tail(tail):
    return jnp.concatenate([tail[:, :64], tail[: ROWS - TAIL, 64:]], axis=0)


def plane_tables(shift):
    tab = lax.dynamic_index_in_dim(jnp.asarray(y_tables()), shift, 0, keepdims=False)
    tab = tab.reshape(256, 4, 32)[:, :, :SIDE].transpose(1, 0, 2)
    return jnp.pad(jnp.tile(tab, (1, 1, SLOTS)), ((0, 0), (0, 0), (0, 256 - SLOTS * SIDE)))


def z_kernel(chip_ref, v0_ref, v1_ref, cond_ref, table_ref, ytab_ref, out_ref, val_main, val_tail, low_ref, high_ref):
    step = pl.program_id(0)

    @pl.when(step == 0)
    def _():
        for i in range(4):
            src = (v0_ref if i < 2 else v1_ref).at[i % 2]
            val_main[i, 0] = src[0:ROWS].astype(F32)
            val_main[i, 1] = src[ROWS : 2 * ROWS].astype(F32)
            both = unpack_tail(src[2 * ROWS :].astype(F32))
            val_tail[i] = jnp.concatenate([both, both], axis=1)
        high_ref[...] = jnp.zeros_like(high_ref)

    @pl.loop(0, CONDS)
    def _(c):
        cre = cond_ref[c, 0:ROWS].astype(F32)
        cim = cond_ref[c, ROWS : 2 * ROWS].astype(F32)
        both = unpack_tail(cond_ref[c, 2 * ROWS :].astype(F32))
        ctail = jnp.concatenate([both, both[:, 32:], both[:, :32]], axis=1)
        for i in range(4):
            vre, vim = val_main[i, 0], val_main[i, 1]
            dre = vre * cre + vim * cim
            dim = vre * cim - vim * cre
            tail = val_tail[i] * ctail
            density = jnp.concatenate([dre, dim, tail], axis=1).astype(BF)
            along = lax.dot_general(
                table_ref[...], density, (((1,), (1,)), ((), ())), preferred_element_type=F32
            )
            for part in range(2):
                start = part * PAIRS + (step * CONDS + c) * 4 + i
                piece = along[part * KROWS : (part + 1) * KROWS]
                low_ref[pl.ds(start, KROWS, stride=128), :] = piece[:, :128]
                high_ref[pl.ds(start, KROWS, stride=128), 0 : ROWS - 128] = piece[:, 128:]

    @pl.when(step == pl.num_programs(0) - 1)
    def _():
        lane = lax.broadcasted_iota(jnp.int32, (256, 256), 1)
        acc = [None] * 4
        for s in range(SLOTS):
            left = []
            for k in (s, s + SLOTS):
                rows = pl.ds(k * 128, 128)
                left.append(jnp.concatenate([low_ref[rows], high_ref[rows]], axis=1).astype(BF))
            left = jnp.concatenate(left, axis=0)
            keep = (lane >= s * SIDE) & (lane < (s + 1) * SIDE)
            for t in range(4):
                right = jnp.where(keep, ytab_ref[t], jnp.zeros((256, 256), BF))
                term = jnp.dot(left, right, preferred_element_type=F32)
                acc[t] = term if acc[t] is None else acc[t] + term
        for x in range(2):
            for tile in range(2):
                c = acc[2 * x][tile * 128 : (tile + 1) * 128]
                s = acc[2 * x + 1][tile * 128 : (tile + 1) * 128]
                lanes = pl.ds(tile * 256, 256)
                out_ref[x * 128 : x * 128 + PAIRS, lanes] = (c[:PAIRS] + s[PAIRS:]).astype(BF)
                out_ref[x * 128 + PAIRS : (x + 1) * 128, lanes] = (c[PAIRS:] - s[:PAIRS]).astype(BF)


def z_transform(chip, val_wire, second, cond_wire, ytab):
    return pl.pallas_call(
        z_kernel,
        out_shape=jax.ShapeDtypeStruct((256, 512), BF),
        grid_spec=pltpu.PrefetchScalarGridSpec(
            num_scalar_prefetch=1,
            grid=(PARTS // CONDS,),
            in_specs=[
                pl.BlockSpec((2, WIRE, 128), lambda c, o: (o[0], 0, 0)),
                pl.BlockSpec((2, WIRE, 128), lambda c, o: (0, 0, 0)),
                pl.BlockSpec((CONDS, WIRE, 128), lambda c, o: (c, 0, 0)),
                pl.BlockSpec((2 * KROWS, 384), lambda c, o: (0, 0)),
                pl.BlockSpec((4, 256, 256), lambda c, o: (0, 0, 0)),
            ],
            out_specs=pl.BlockSpec((256, 512), lambda c, o: (0, 0)),
            scratch_shapes=[
                pltpu.VMEM((4, 2, ROWS, 128), F32),
                pltpu.VMEM((4, ROWS, 128), F32),
                pltpu.VMEM((KROWS * 128, 128), F32),
                pltpu.VMEM((KROWS * 128, 128), F32),
            ],
        ),
        compiler_params=pltpu.CompilerParams(vmem_limit_bytes=40 * 2**20),
        name="ztransform",
    )(chip, val_wire, second, cond_wire, jnp.asarray(z_table()), ytab)


def g_kernel(parity_ref, plane_ref, index_ref, phase_ref, out_ref):
    row = lax.broadcasted_iota(jnp.int32, (512, GCHUNK), 0)
    for chunk in range(out_ref.shape[0]):
        pick = jnp.where(row == index_ref[chunk, 0], 1.0, 0.0).astype(BF)
        at = jnp.dot(plane_ref[...], pick, preferred_element_type=F32)
        real = jnp.zeros((PAIRS, GCHUNK), F32)
        imag = jnp.zeros((PAIRS, GCHUNK), F32)
        for x in range(2):
            c = phase_ref[chunk, 0, 2 * x : 2 * x + 1]
            s = phase_ref[chunk, 0, 2 * x + 1 : 2 * x + 2]
            re = at[x * 128 : x * 128 + PAIRS]
            im = at[x * 128 + PAIRS : (x + 1) * 128]
            real = real + re * c + im * s
            imag = imag + im * c - re * s
        out_ref[chunk, :PAIRS] = real.astype(out_ref.dtype)
        out_ref[chunk, PAIRS:] = imag.astype(out_ref.dtype)


def g_elements(parity, plane, index, phase, dtype):
    chips = index.shape[0]
    return pl.pallas_call(
        g_kernel,
        out_shape=jax.ShapeDtypeStruct((chips, 128, GCHUNK), dtype),
        grid_spec=pltpu.PrefetchScalarGridSpec(
            num_scalar_prefetch=1,
            grid=(1,),
            in_specs=[
                pl.BlockSpec((256, 512), lambda i, k: (0, 0)),
                pl.BlockSpec((chips, 1, 1, GCHUNK), lambda i, k: (0, k[0], 0, 0)),
                pl.BlockSpec((chips, 1, 4, GCHUNK), lambda i, k: (0, k[0], 0, 0)),
            ],
            out_specs=pl.BlockSpec((chips, 128, GCHUNK), lambda i, k: (0, 0, 0)),
        ),
        compiler_params=pltpu.CompilerParams(vmem_limit_bytes=40 * 2**20),
        cost_estimate=pl.CostEstimate(flops=2 * 10**9, transcendentals=0, bytes_accessed=12_000_000),
        name="gelements",
    )(parity, plane, index, phase)


def shards(valence, conduction, val_energy, cond_energy, cond_band, owners, gvectors):
    grid_pos = lax.axis_index("grid")
    band_pos = lax.axis_index("band")
    x_local = valence.shape[2]
    n_grid = lax.axis_size("grid")

    rows_all = x_local * LENGTH
    cond_wire = pack_cond(conduction.reshape(2, rows_all, LENGTH), cond_band)
    cond_wire, core = lax.optimization_barrier((cond_wire, band_pos & 1))
    cond_wire = lax.all_to_all(cond_wire, "band", 0, 0, tiled=True)

    first, second = owners[0], owners[1]
    bands = valence.reshape(2, 2, rows_all, LENGTH)
    sibling = pack_val(bands, (1 - core)[None])
    sibling = lax.ppermute(sibling, "band", [(b, b ^ 1) for b in range(PARTS)])
    here = (first >> 1) == (band_pos >> 1)
    own = jnp.where(here, first == band_pos, second == band_pos)
    val_wire = pack_val(bands, core[None], own.astype(jnp.int32)[None], sibling)
    val_wire = lax.all_to_all(val_wire, "band", 0, 0, tiled=True)
    cond_wire, val_wire = lax.optimization_barrier((cond_wire, val_wire))

    ytab = plane_tables(band_pos & 3)
    chip = (first >> 1)[None]

    def exchange_again(operands):
        bands, sibling, val_wire, cond_wire, ytab = operands
        again = pack_val(bands, core[None], (second == band_pos).astype(jnp.int32)[None], sibling)
        again = lax.all_to_all(again, "band", 0, 0, tiled=True)
        again = lax.dynamic_slice_in_dim(again, (second >> 1) * 2, 2, 0)
        return z_transform(chip, val_wire, again, cond_wire, ytab)

    def from_first(operands):
        _, _, val_wire, cond_wire, ytab = operands
        again = lax.dynamic_slice_in_dim(val_wire, (second >> 1) * 2, 2, 0)
        return z_transform(chip, val_wire, again, cond_wire, ytab)

    both = (first != second) & ((first >> 1) == (second >> 1))
    plane = lax.cond(both, exchange_again, from_first, (bands, sibling, val_wire, cond_wire, ytab))

    numbers = cond_wire[:, WIRE - 1, 127].astype(jnp.int32)
    order = jnp.arange(cond_energy.shape[0], dtype=jnp.int32)
    levels = jnp.sum(jnp.where(numbers[:, None] == order[None, :], cond_energy[None, :], 0.0), axis=1)
    val_index = (owners[:, None] * 2 + jnp.arange(2, dtype=jnp.int32)[None, :]).reshape(4)
    val_levels = val_energy[val_index]
    weight = (2.0 / (PAIRS * (val_levels[None, :] - levels[:, None]))).reshape(PAIRS)

    signed = (gvectors + GMAX) % LENGTH
    slot = jnp.where(signed[2] < SLOTS, signed[2] * SIDE, 256 + (signed[2] - SLOTS) * SIDE)
    index = (slot + signed[1]).reshape(PARTS // 2, 2, 1, GCHUNK)
    x_first = grid_pos * x_local + 5 * (band_pos >> 2) + (band_pos & 3)
    norm = float(LENGTH) ** (-1.5)
    waves = []
    for x in range(2):
        angle = (gvectors[0] * (x_first + x) % LENGTH).astype(F32) * (2.0 * math.pi / LENGTH)
        waves += [jnp.cos(angle), jnp.sin(angle)]
    phase = jnp.stack(waves).astype(BF).astype(F32) * norm
    phase = phase.reshape(4, PARTS, GCHUNK).transpose(1, 0, 2).reshape(PARTS // 2, 2, 4, GCHUNK)

    core = band_pos & 1
    away = g_elements((1 - core)[None], plane, index, phase, BF)
    come = lax.ppermute(away, "band", [(b, b ^ 1) for b in range(PARTS)])
    keep = g_elements(core[None], plane, index, phase, F32)
    parts = (keep + come.astype(F32)).astype(BF)
    same_core = [[b for b in range(PARTS) if b % 2 == k] for k in range(2)]
    parts = lax.all_to_all(parts, "band", 0, 0, axis_index_groups=same_core, tiled=True)
    block = jnp.sum(parts.astype(F32), axis=0)
    zh_flip = [(g, g ^ 1) for g in range(n_grid)]
    y_flip = [(g, g ^ 2) for g in range(n_grid)]
    y_rest = [(g, 6 - (g & 6) + (g & 1)) for g in range(n_grid)]
    for perm in (zh_flip, y_flip, y_rest):
        block = block + lax.ppermute(block.astype(BF), "grid", perm).astype(F32)

    straight, crossed = [], []
    for b in range(PARTS):
        for g in range(n_grid):
            straight.append((b * n_grid + g, (2 * g + b % 2) * n_grid + b // 2))
            crossed.append((b * n_grid + g, (2 * g + 1 - b % 2) * n_grid + b // 2))
    block = block.astype(BF)
    same = lax.ppermute(block, ("band", "grid"), straight)
    other = lax.ppermute(block, ("band", "grid"), crossed)
    odd = (band_pos & 1) == 1
    left = jnp.where(odd, other, same)
    right = jnp.where(odd, same, other)
    rows = jnp.concatenate([left, right], axis=1).astype(F32)
    block = block.astype(F32)

    w2 = jnp.concatenate([weight, weight])[:, None]
    for_real = block * w2
    for_imag = jnp.concatenate([-for_real[PAIRS:], for_real[:PAIRS]], axis=0)
    high = lax.Precision.HIGHEST
    chi_re = jnp.einsum("pr,pc->rc", rows, for_real, precision=high)
    chi_im = jnp.einsum("pr,pc->rc", rows, for_imag, precision=high)
    return jnp.stack([chi_re, chi_im])


def solution(mesh):
    return jax.shard_map(
        shards,
        mesh=mesh,
        in_specs=(
            P("band", None, "grid", None, None),
            P("band", None, "grid", None, None),
            P(),
            P(),
            P("band"),
            P(),
            P(),
        ),
        out_specs=P(None, "grid", "band"),
        check_vma=False,
    )
```

```python
import functools
import math

import jax
import jax.numpy as jnp
import numpy as np
from jax import lax
from jax.experimental import pallas as pl
from jax.experimental.pallas import tpu as pltpu
from jax.sharding import PartitionSpec as P

LENGTH = 160
GMAX = 10
SIDE = 2 * GMAX + 1
PARTS = 16
ROWS = 200
TAIL = 104
WIRE = 2 * ROWS + TAIL
PAIRS = 64
CHIPS = 8
STEP = 4
SLOTS = 12
KROWS = 24
GCHUNK = 256
BF = jnp.bfloat16
F32 = jnp.float32


def host_tables():
    freq = (np.arange(SIDE) - GMAX) % LENGTH
    pos = np.arange(LENGTH)
    angle = ((freq[:, None] * pos[None, :]) % LENGTH).astype(np.float32) * np.float32(2.0 * math.pi / LENGTH)
    rnd = lambda a: a.astype(np.float32).astype(jnp.bfloat16).astype(np.float32)
    return rnd(np.cos(angle)), rnd(np.sin(angle))


def z_table():
    cos, sin = host_tables()
    out = np.zeros((2 * KROWS, 384), np.float32)
    cm, sm, ct, st = cos[:, :128], sin[:, :128], cos[:, 128:], sin[:, 128:]
    out[:SIDE] = np.concatenate([cm, sm, ct, ct, st, -st], axis=1)
    out[KROWS : KROWS + SIDE] = np.concatenate([-sm, cm, -st, -st, ct, -ct], axis=1)
    return out.astype(jnp.bfloat16)


def y_tables():
    cos, sin = host_tables()
    out = np.zeros((4, 256, 4, 32), np.float32)
    for shift in range(4):
        for row in range(ROWS):
            flat = 40 * shift + row
            x, y = divmod(flat, LENGTH)
            out[shift, row, 2 * x, :SIDE] = cos[:, y]
            out[shift, row, 2 * x + 1, :SIDE] = sin[:, y]
    return out.reshape(4, 256, 128).astype(jnp.bfloat16)


def pack_band(src, out, fill):
    real, imag = src[0], src[1]
    out[0:ROWS] = real[:, :128]
    out[ROWS : 2 * ROWS] = imag[:, :128]
    tail = jnp.concatenate([real[:, 128:].astype(F32), imag[:, 128:].astype(F32)], axis=1)
    low = tail[:TAIL]
    high = jnp.concatenate([tail[TAIL:], jnp.full((2 * TAIL - ROWS, 64), 1.0, F32) * fill], axis=0)
    out[2 * ROWS :] = jnp.concatenate([low, high], axis=1).astype(BF)


def pack_cond_kernel(core_ref, number_ref, keep_ref, give_ref, keep_out, give_out):
    number = number_ref[0].astype(F32)
    for c in range(STEP):
        pack_band(keep_ref.at[:, c, 0], keep_out.at[c], number)
        pack_band(give_ref.at[:, c, 0], give_out.at[c], number)


def pack_cond(conduction, core, number):
    block = (2, STEP, 1, ROWS, LENGTH)
    out = pltpu.HBM((CHIPS, WIRE, 128), BF)
    return pl.pallas_call(
        pack_cond_kernel,
        out_shape=(out, out),
        grid_spec=pltpu.PrefetchScalarGridSpec(
            num_scalar_prefetch=2,
            grid=(CHIPS // STEP,),
            in_specs=[
                pl.BlockSpec(block, lambda t, k, n: (0, t, k[0], 0, 0)),
                pl.BlockSpec(block, lambda t, k, n: (0, t, 1 - k[0], 0, 0)),
            ],
            out_specs=[
                pl.BlockSpec((STEP, WIRE, 128), lambda t, k, n: (t, 0, 0)),
                pl.BlockSpec((STEP, WIRE, 128), lambda t, k, n: (t, 0, 0)),
            ],
        ),
        cost_estimate=pl.CostEstimate(flops=0, transcendentals=0, bytes_accessed=6_000_000),
        compiler_params=pltpu.CompilerParams(vmem_limit_bytes=40 * 2**20),
        name="packcond",
    )(core, number, conduction, conduction)


def pack_bands(val_ref, out_ref):
    for c in range(STEP):
        for band in range(2):
            pack_band(val_ref.at[band, :, c, 0], out_ref.at[c, band], 0.0)


def pack_give_kernel(core_ref, val_ref, out_ref):
    pack_bands(val_ref, out_ref)


VAL_BLOCK = (2, 2, STEP, 1, ROWS, LENGTH)


def pack_give(valence, core):
    return pl.pallas_call(
        pack_give_kernel,
        out_shape=pltpu.HBM((CHIPS, 2, WIRE, 128), BF),
        grid_spec=pltpu.PrefetchScalarGridSpec(
            num_scalar_prefetch=1,
            grid=(CHIPS // STEP,),
            in_specs=[pl.BlockSpec(VAL_BLOCK, lambda t, k: (0, 0, t, 1 - k[0], 0, 0))],
            out_specs=pl.BlockSpec((STEP, 2, WIRE, 128), lambda t, k: (t, 0, 0, 0)),
        ),
        cost_estimate=pl.CostEstimate(flops=0, transcendentals=0, bytes_accessed=6_000_000),
        compiler_params=pltpu.CompilerParams(vmem_limit_bytes=40 * 2**20),
        name="packgive",
    )(core, valence)


def pack_choice_kernel(core_ref, own_ref, val_ref, other_ref, *refs):
    out_ref = refs[-1]

    @pl.when(own_ref[0] == 1)
    def _():
        pack_bands(val_ref, out_ref)

    @pl.when(own_ref[0] == 0)
    def _():
        out_ref[:, 0:2] = other_ref[...]

    if len(refs) == 2:
        out_ref[:, 2] = refs[0][...]


def pack_choice(valence, core, own, other, cond=None):
    slots = 2 if cond is None else 3
    arrays = (valence, other) if cond is None else (valence, other, cond)
    specs = [
        pl.BlockSpec(VAL_BLOCK, lambda t, k, o: (0, 0, t, k[0], 0, 0)),
        pl.BlockSpec((STEP, 2, WIRE, 128), lambda t, k, o: (t, 0, 0, 0)),
        pl.BlockSpec((STEP, WIRE, 128), lambda t, k, o: (t, 0, 0)),
    ]
    return pl.pallas_call(
        pack_choice_kernel,
        out_shape=pltpu.HBM((CHIPS, slots, WIRE, 128), BF),
        grid_spec=pltpu.PrefetchScalarGridSpec(
            num_scalar_prefetch=2,
            grid=(CHIPS // STEP,),
            in_specs=specs[: len(arrays)],
            out_specs=pl.BlockSpec((STEP, slots, WIRE, 128), lambda t, k, o: (t, 0, 0, 0)),
        ),
        cost_estimate=pl.CostEstimate(flops=0, transcendentals=0, bytes_accessed=10_000_000),
        compiler_params=pltpu.CompilerParams(vmem_limit_bytes=40 * 2**20),
        name="packchoice",
    )(core, own, *arrays)


def unpack_tail(tail):
    return jnp.concatenate([tail[:, :64], tail[: ROWS - TAIL, 64:]], axis=0)


def plane_tables(shift):
    tab = lax.dynamic_index_in_dim(jnp.asarray(y_tables()), shift, 0, keepdims=False)
    tab = tab.reshape(256, 4, 32)[:, :, :SIDE].transpose(1, 0, 2)
    return jnp.pad(jnp.tile(tab, (1, 1, SLOTS)), ((0, 0), (0, 0), (0, 256 - SLOTS * SIDE)))


def z_kernel(
    where_ref, v0_ref, v1_ref, own_ref, sib_ref, table_ref, ytab_ref, out_ref, val_main, val_tail, low_ref, high_ref
):
    step = pl.program_id(0)

    @pl.when(step == 0)
    def _():
        for i in range(4):
            src = (v0_ref if i < 2 else v1_ref).at[0, i % 2]
            val_main[i, 0] = src[0:ROWS].astype(F32)
            val_main[i, 1] = src[ROWS : 2 * ROWS].astype(F32)
            both = unpack_tail(src[2 * ROWS :].astype(F32))
            val_tail[i] = jnp.concatenate([both, both], axis=1)
        high_ref[...] = jnp.zeros_like(high_ref)

    @pl.loop(0, STEP)
    def _(c):
        for which in range(2):
            src = own_ref.at[c] if which == 0 else sib_ref.at[c, 0]
            core = where_ref[2] if which == 0 else 1 - where_ref[2]
            first = ((step * STEP + c) * 2 + core) * 4
            cre = src[0:ROWS].astype(F32)
            cim = src[ROWS : 2 * ROWS].astype(F32)
            both = unpack_tail(src[2 * ROWS :].astype(F32))
            ctail = jnp.concatenate([both, both[:, 32:], both[:, :32]], axis=1)
            for i in range(0, 4, 2):
                density = []
                for j in (i, i + 1):
                    vre, vim = val_main[j, 0], val_main[j, 1]
                    density += [vre * cre + vim * cim, vre * cim - vim * cre, val_tail[j] * ctail]
                density = jnp.concatenate(density, axis=1).astype(BF)
                along = lax.dot_general(
                    table_ref[...], density, (((1,), (1,)), ((), ())), preferred_element_type=F32
                )
                for j in range(2):
                    for part in range(2):
                        start = part * PAIRS + first + i + j
                        at = (2 * j + part) * KROWS
                        piece = along[at : at + KROWS]
                        low_ref[pl.ds(start, KROWS, stride=128), :] = piece[:, :128]
                        high_ref[pl.ds(start, KROWS, stride=128), 0 : ROWS - 128] = piece[:, 128:]

    @pl.when(step == pl.num_programs(0) - 1)
    def _():
        lane = lax.broadcasted_iota(jnp.int32, (256, 256), 1)
        acc = [None] * 4
        for s in range(SLOTS):
            left = []
            for k in (s, s + SLOTS):
                rows = pl.ds(k * 128, 128)
                left.append(jnp.concatenate([low_ref[rows], high_ref[rows]], axis=1).astype(BF))
            left = jnp.concatenate(left, axis=0)
            keep = (lane >= s * SIDE) & (lane < (s + 1) * SIDE)
            for t in range(4):
                right = jnp.where(keep, ytab_ref[t], jnp.zeros((256, 256), BF))
                term = jnp.dot(left, right, preferred_element_type=F32)
                acc[t] = term if acc[t] is None else acc[t] + term
        for x in range(2):
            for tile in range(2):
                c = acc[2 * x][tile * 128 : (tile + 1) * 128]
                s = acc[2 * x + 1][tile * 128 : (tile + 1) * 128]
                lanes = pl.ds(tile * 256, 256)
                out_ref[x * 128 : x * 128 + PAIRS, lanes] = (c[:PAIRS] + s[PAIRS:]).astype(BF)
                out_ref[x * 128 + PAIRS : (x + 1) * 128, lanes] = (c[PAIRS:] - s[:PAIRS]).astype(BF)


def z_transform(where, val_wire, second, own, ytab):
    single = z_table()
    table = np.zeros((4 * KROWS, 768), single.dtype)
    table[: 2 * KROWS, :384] = single
    table[2 * KROWS :, 384:] = single
    return pl.pallas_call(
        z_kernel,
        out_shape=jax.ShapeDtypeStruct((256, 512), BF),
        grid_spec=pltpu.PrefetchScalarGridSpec(
            num_scalar_prefetch=1,
            grid=(CHIPS // STEP,),
            in_specs=[
                pl.BlockSpec((1, 2, WIRE, 128), lambda c, o: (o[0], 0, 0, 0)),
                pl.BlockSpec((1, 2, WIRE, 128), lambda c, o: (o[1], 0, 0, 0)),
                pl.BlockSpec((STEP, WIRE, 128), lambda c, o: (c, 0, 0)),
                pl.BlockSpec((STEP, 1, WIRE, 128), lambda c, o: (c, 2, 0, 0)),
                pl.BlockSpec((4 * KROWS, 768), lambda c, o: (0, 0)),
                pl.BlockSpec((4, 256, 256), lambda c, o: (0, 0, 0)),
            ],
            out_specs=pl.BlockSpec((256, 512), lambda c, o: (0, 0)),
            scratch_shapes=[
                pltpu.VMEM((4, 2, ROWS, 128), F32),
                pltpu.VMEM((4, ROWS, 128), F32),
                pltpu.VMEM((KROWS * 128, 128), F32),
                pltpu.VMEM((KROWS * 128, 128), F32),
            ],
        ),
        compiler_params=pltpu.CompilerParams(vmem_limit_bytes=40 * 2**20),
        name="ztransform",
    )(where, val_wire, second, own, val_wire, jnp.asarray(table), ytab)


def g_kernel(parity_ref, plane_ref, index_ref, phase_ref, out_ref):
    row = lax.broadcasted_iota(jnp.int32, (512, GCHUNK), 0)
    for chunk in range(out_ref.shape[0]):
        pick = jnp.where(row == index_ref[chunk, 0], 1.0, 0.0).astype(BF)
        at = jnp.dot(plane_ref[...], pick, preferred_element_type=F32)
        real = jnp.zeros((PAIRS, GCHUNK), F32)
        imag = jnp.zeros((PAIRS, GCHUNK), F32)
        for x in range(2):
            c = phase_ref[chunk, 0, 2 * x : 2 * x + 1]
            s = phase_ref[chunk, 0, 2 * x + 1 : 2 * x + 2]
            re = at[x * 128 : x * 128 + PAIRS]
            im = at[x * 128 + PAIRS : (x + 1) * 128]
            real = real + re * c + im * s
            imag = imag + im * c - re * s
        out_ref[chunk, :PAIRS] = real.astype(out_ref.dtype)
        out_ref[chunk, PAIRS:] = imag.astype(out_ref.dtype)


def g_elements(parity, plane, index, phase, dtype):
    chips = index.shape[0]
    return pl.pallas_call(
        g_kernel,
        out_shape=jax.ShapeDtypeStruct((chips, 128, GCHUNK), dtype),
        grid_spec=pltpu.PrefetchScalarGridSpec(
            num_scalar_prefetch=1,
            grid=(1,),
            in_specs=[
                pl.BlockSpec((256, 512), lambda i, k: (0, 0)),
                pl.BlockSpec((chips, 1, 1, GCHUNK), lambda i, k: (0, k[0], 0, 0)),
                pl.BlockSpec((chips, 1, 4, GCHUNK), lambda i, k: (0, k[0], 0, 0)),
            ],
            out_specs=pl.BlockSpec((chips, 128, GCHUNK), lambda i, k: (0, 0, 0)),
        ),
        compiler_params=pltpu.CompilerParams(vmem_limit_bytes=40 * 2**20),
        cost_estimate=pl.CostEstimate(flops=2 * 10**9, transcendentals=0, bytes_accessed=12_000_000),
        name="gelements",
    )(parity, plane, index, phase)


def shards(valence, conduction, val_energy, cond_energy, cond_band, owners, gvectors):
    grid_pos = lax.axis_index("grid")
    band_pos = lax.axis_index("band")
    x_local = valence.shape[2]
    n_grid = lax.axis_size("grid")

    core = band_pos & 1
    siblings = [(b, b ^ 1) for b in range(PARTS)]
    same_core = [[b for b in range(PARTS) if b % 2 == k] for k in range(2)]

    conduction = pltpu.with_memory_space_constraint(conduction.reshape(2, CHIPS, 2, ROWS, LENGTH), pltpu.HBM)
    keep, give = pack_cond(conduction, core[None], cond_band)
    cond_sib = lax.ppermute(give, "band", siblings)
    keep, core_late = lax.optimization_barrier((keep, core))
    cond_own = lax.all_to_all(keep, "band", 0, 0, axis_index_groups=same_core, tiled=True)

    first, second = owners[0], owners[1]
    bands = pltpu.with_memory_space_constraint(valence.reshape(2, 2, CHIPS, 2, ROWS, LENGTH), pltpu.HBM)
    val_sib = lax.ppermute(pack_give(bands, core_late[None]), "band", siblings)
    here = (first >> 1) == (band_pos >> 1)
    own = jnp.where(here, first == band_pos, second == band_pos)
    wire = pack_choice(bands, core[None], own.astype(jnp.int32)[None], val_sib, cond_sib)
    cond_own, wire = lax.optimization_barrier((cond_own, wire))
    wire = lax.all_to_all(wire, "band", 0, 0, axis_index_groups=same_core, tiled=True)

    ytab = plane_tables(band_pos & 3)
    where = jnp.stack([first >> 1, second >> 1, core])

    def exchange_again(operands):
        bands, val_sib, wire, cond_own, ytab = operands
        again = pack_choice(bands, core[None], (second == band_pos).astype(jnp.int32)[None], val_sib)
        again = lax.all_to_all(again, "band", 0, 0, axis_index_groups=same_core, tiled=True)
        return z_transform(where, wire, again, cond_own, ytab)

    def from_first(operands):
        _, _, wire, cond_own, ytab = operands
        return z_transform(where, wire, wire, cond_own, ytab)

    both = (first != second) & ((first >> 1) == (second >> 1))
    plane = lax.cond(both, exchange_again, from_first, (bands, val_sib, wire, cond_own, ytab))

    last = jnp.stack([cond_own[:, WIRE - 1, 127], wire[:, 2, WIRE - 1, 127]], axis=1)
    numbers = jnp.where(core == 0, last, last[:, ::-1]).reshape(PARTS).astype(jnp.int32)
    order = jnp.arange(cond_energy.shape[0], dtype=jnp.int32)
    levels = jnp.sum(jnp.where(numbers[:, None] == order[None, :], cond_energy[None, :], 0.0), axis=1)
    val_index = (owners[:, None] * 2 + jnp.arange(2, dtype=jnp.int32)[None, :]).reshape(4)
    val_levels = val_energy[val_index]
    weight = (2.0 / (PAIRS * (val_levels[None, :] - levels[:, None]))).reshape(PAIRS)

    signed = (gvectors + GMAX) % LENGTH
    slot = jnp.where(signed[2] < SLOTS, signed[2] * SIDE, 256 + (signed[2] - SLOTS) * SIDE)
    index = (slot + signed[1]).reshape(PARTS // 2, 2, 1, GCHUNK)
    x_first = grid_pos * x_local + 5 * (band_pos >> 2) + (band_pos & 3)
    norm = float(LENGTH) ** (-1.5)
    waves = []
    for x in range(2):
        angle = (gvectors[0] * (x_first + x) % LENGTH).astype(F32) * (2.0 * math.pi / LENGTH)
        waves += [jnp.cos(angle), jnp.sin(angle)]
    phase = jnp.stack(waves).astype(BF).astype(F32) * norm
    phase = phase.reshape(4, PARTS, GCHUNK).transpose(1, 0, 2).reshape(PARTS // 2, 2, 4, GCHUNK)

    away = g_elements((1 - core)[None], plane, index, phase, BF)
    come = lax.ppermute(away, "band", siblings)
    keep = g_elements(core[None], plane, index, phase, F32)
    parts = (keep + come.astype(F32)).astype(BF)
    parts = lax.all_to_all(parts, "band", 0, 0, axis_index_groups=same_core, tiled=True)
    block = jnp.sum(parts.astype(F32), axis=0)
    block = block + lax.ppermute(block.astype(BF), "grid", [(g, g ^ 1) for g in range(n_grid)]).astype(F32)
    narrow = block.astype(BF)
    for turn in (2, 4, 6):
        step = [(g, (g + turn) % n_grid) for g in range(n_grid)]
        block = block + lax.ppermute(narrow, "grid", step).astype(F32)

    straight, crossed = [], []
    for b in range(PARTS):
        for g in range(n_grid):
            straight.append((b * n_grid + g, (2 * g + b % 2) * n_grid + b // 2))
            crossed.append((b * n_grid + g, (2 * g + 1 - b % 2) * n_grid + b // 2))
    block = block.astype(BF)
    same = lax.ppermute(block, ("band", "grid"), straight)
    other = lax.ppermute(block, ("band", "grid"), crossed)
    odd = (band_pos & 1) == 1
    left = jnp.where(odd, other, same)
    right = jnp.where(odd, same, other)
    rows = jnp.concatenate([left, right], axis=1).astype(F32)
    block = block.astype(F32)

    w2 = jnp.concatenate([weight, weight])[:, None]
    for_real = block * w2
    for_imag = jnp.concatenate([-for_real[PAIRS:], for_real[:PAIRS]], axis=0)
    high = lax.Precision.HIGHEST
    chi_re = jnp.einsum("pr,pc->rc", rows, for_real, precision=high)
    chi_im = jnp.einsum("pr,pc->rc", rows, for_imag, precision=high)
    return jnp.stack([chi_re, chi_im])


def solution(mesh):
    return jax.shard_map(
        shards,
        mesh=mesh,
        in_specs=(
            P("band", None, "grid", None, None),
            P("band", None, "grid", None, None),
            P(),
            P(),
            P("band"),
            P(),
            P(),
        ),
        out_specs=P(None, "grid", "band"),
        check_vma=False,
    )
```

```python
import functools
import math

import jax
import jax.numpy as jnp
import numpy as np
from jax import lax
from jax.experimental import pallas as pl
from jax.experimental.pallas import tpu as pltpu
from jax.sharding import PartitionSpec as P

LENGTH = 160
GMAX = 10
SIDE = 2 * GMAX + 1
PARTS = 16
ROWS = 200
TAIL = 104
WIRE = 2 * ROWS + TAIL
PAIRS = 64
PACK = 8
CONDS = 4
SLOTS = 12
KROWS = 24
GCHUNK = 256
BF = jnp.bfloat16
F32 = jnp.float32


def host_tables():
    freq = (np.arange(SIDE) - GMAX) % LENGTH
    pos = np.arange(LENGTH)
    angle = ((freq[:, None] * pos[None, :]) % LENGTH).astype(np.float32) * np.float32(2.0 * math.pi / LENGTH)
    rnd = lambda a: a.astype(np.float32).astype(jnp.bfloat16).astype(np.float32)
    return rnd(np.cos(angle)), rnd(np.sin(angle))


def z_table():
    cos, sin = host_tables()
    out = np.zeros((2 * KROWS, 384), np.float32)
    cm, sm, ct, st = cos[:, :128], sin[:, :128], cos[:, 128:], sin[:, 128:]
    out[:SIDE] = np.concatenate([cm, sm, ct, ct, st, -st], axis=1)
    out[KROWS : KROWS + SIDE] = np.concatenate([-sm, cm, -st, -st, ct, -ct], axis=1)
    return out.astype(jnp.bfloat16)


def y_tables():
    cos, sin = host_tables()
    out = np.zeros((4, 256, 4, 32), np.float32)
    for shift in range(4):
        for row in range(ROWS):
            flat = 40 * shift + row
            x, y = divmod(flat, LENGTH)
            out[shift, row, 2 * x, :SIDE] = cos[:, y]
            out[shift, row, 2 * x + 1, :SIDE] = sin[:, y]
    return out.reshape(4, 256, 128).astype(jnp.bfloat16)


def pack_band(src, out, fill):
    real, imag = src[0], src[1]
    out[0:ROWS] = real[:, :128]
    out[ROWS : 2 * ROWS] = imag[:, :128]
    tail = jnp.concatenate([real[:, 128:].astype(F32), imag[:, 128:].astype(F32)], axis=1)
    low = tail[:TAIL]
    high = jnp.concatenate([tail[TAIL:], jnp.full((2 * TAIL - ROWS, 64), 1.0, F32) * fill], axis=0)
    out[2 * ROWS :] = jnp.concatenate([low, high], axis=1).astype(BF)


def pack_cond_kernel(number_ref, cond_ref, out_ref):
    for t in range(PACK):
        rows = pl.ds(t * ROWS, ROWS)
        pack_band(cond_ref.at[:, rows], out_ref.at[t], number_ref[0].astype(F32))


def pack_cond(conduction, number):
    return pl.pallas_call(
        pack_cond_kernel,
        out_shape=jax.ShapeDtypeStruct((PARTS, WIRE, 128), BF),
        grid_spec=pltpu.PrefetchScalarGridSpec(
            num_scalar_prefetch=1,
            grid=(PARTS // PACK,),
            in_specs=[pl.BlockSpec((2, PACK * ROWS, LENGTH), lambda t, n: (0, t, 0))],
            out_specs=pl.BlockSpec((PACK, WIRE, 128), lambda t, n: (t, 0, 0)),
        ),
        cost_estimate=pl.CostEstimate(flops=0, transcendentals=0, bytes_accessed=6_000_000),
        name="packcond",
    )(number, conduction)


def pack_val_kernel(band_ref, val_ref, out_ref):
    for t in range(PACK):
        pack_band(val_ref.at[0, :, pl.ds(t * ROWS, ROWS)], out_ref.at[t], 0.0)


def pack_choice_kernel(band_ref, own_ref, val_ref, other_ref, out_ref):
    @pl.when(own_ref[0] == 1)
    def _():
        pack_val_kernel(band_ref, val_ref, out_ref)

    @pl.when(own_ref[0] == 0)
    def _():
        out_ref[...] = other_ref[...]


def pack_val(valence, band, own=None, other=None):
    wire_spec = pl.BlockSpec((PACK, WIRE, 128), lambda t, *_: (t, 0, 0))
    scalars, arrays, specs, kernel = (band,), (valence,), [], pack_val_kernel
    specs.append(pl.BlockSpec((1, 2, PACK * ROWS, LENGTH), lambda t, k, *_: (k[0], 0, t, 0)))
    if other is not None:
        scalars, arrays, kernel = (band, own), (valence, other), pack_choice_kernel
        specs.append(wire_spec)
    return pl.pallas_call(
        kernel,
        out_shape=jax.ShapeDtypeStruct((PARTS, WIRE, 128), BF),
        grid_spec=pltpu.PrefetchScalarGridSpec(
            num_scalar_prefetch=len(scalars),
            grid=(PARTS // PACK,),
            in_specs=specs,
            out_specs=wire_spec,
        ),
        cost_estimate=pl.CostEstimate(flops=0, transcendentals=0, bytes_accessed=8_000_000),
        compiler_params=pltpu.CompilerParams(vmem_limit_bytes=40 * 2**20),
        name="packval",
    )(*scalars, *arrays)


def unpack_tail(tail):
    return jnp.concatenate([tail[:, :64], tail[: ROWS - TAIL, 64:]], axis=0)


def plane_tables(shift):
    tab = lax.dynamic_index_in_dim(jnp.asarray(y_tables()), shift, 0, keepdims=False)
    tab = tab.reshape(256, 4, 32)[:, :, :SIDE].transpose(1, 0, 2)
    return jnp.pad(jnp.tile(tab, (1, 1, SLOTS)), ((0, 0), (0, 0), (0, 256 - SLOTS * SIDE)))


def z_kernel(chip_ref, v0_ref, v1_ref, cond_ref, table_ref, ytab_ref, out_ref, val_main, val_tail, low_ref, high_ref):
    step = pl.program_id(0)

    @pl.when(step == 0)
    def _():
        for i in range(4):
            src = (v0_ref if i < 2 else v1_ref).at[i % 2]
            val_main[i, 0] = src[0:ROWS].astype(F32)
            val_main[i, 1] = src[ROWS : 2 * ROWS].astype(F32)
            both = unpack_tail(src[2 * ROWS :].astype(F32))
            val_tail[i] = jnp.concatenate([both, both], axis=1)
        high_ref[...] = jnp.zeros_like(high_ref)

    @pl.loop(0, CONDS)
    def _(c):
        cre = cond_ref[c, 0:ROWS].astype(F32)
        cim = cond_ref[c, ROWS : 2 * ROWS].astype(F32)
        both = unpack_tail(cond_ref[c, 2 * ROWS :].astype(F32))
        ctail = jnp.concatenate([both, both[:, 32:], both[:, :32]], axis=1)
        first = (step * CONDS + c) * 4
        for i in range(0, 4, 2):
            density = []
            for j in (i, i + 1):
                vre, vim = val_main[j, 0], val_main[j, 1]
                density += [vre * cre + vim * cim, vre * cim - vim * cre, val_tail[j] * ctail]
            density = jnp.concatenate(density, axis=1).astype(BF)
            along = lax.dot_general(
                table_ref[...], density, (((1,), (1,)), ((), ())), preferred_element_type=F32
            )
            for j in range(2):
                for part in range(2):
                    start = part * PAIRS + first + i + j
                    at = (2 * j + part) * KROWS
                    piece = along[at : at + KROWS]
                    low_ref[pl.ds(start, KROWS, stride=128), :] = piece[:, :128]
                    high_ref[pl.ds(start, KROWS, stride=128), 0 : ROWS - 128] = piece[:, 128:]

    @pl.when(step == pl.num_programs(0) - 1)
    def _():
        lane = lax.broadcasted_iota(jnp.int32, (256, 256), 1)
        acc = [None] * 4
        for s in range(SLOTS):
            left = []
            for k in (s, s + SLOTS):
                rows = pl.ds(k * 128, 128)
                left.append(jnp.concatenate([low_ref[rows], high_ref[rows]], axis=1).astype(BF))
            left = jnp.concatenate(left, axis=0)
            keep = (lane >= s * SIDE) & (lane < (s + 1) * SIDE)
            for t in range(4):
                right = jnp.where(keep, ytab_ref[t], jnp.zeros((256, 256), BF))
                term = jnp.dot(left, right, preferred_element_type=F32)
                acc[t] = term if acc[t] is None else acc[t] + term
        for x in range(2):
            for tile in range(2):
                c = acc[2 * x][tile * 128 : (tile + 1) * 128]
                s = acc[2 * x + 1][tile * 128 : (tile + 1) * 128]
                lanes = pl.ds(tile * 256, 256)
                out_ref[x * 128 : x * 128 + PAIRS, lanes] = (c[:PAIRS] + s[PAIRS:]).astype(BF)
                out_ref[x * 128 + PAIRS : (x + 1) * 128, lanes] = (c[PAIRS:] - s[:PAIRS]).astype(BF)


def z_transform(chip, val_wire, second, cond_wire, ytab):
    single = z_table()
    table = np.zeros((4 * KROWS, 768), single.dtype)
    table[: 2 * KROWS, :384] = single
    table[2 * KROWS :, 384:] = single
    return pl.pallas_call(
        z_kernel,
        out_shape=jax.ShapeDtypeStruct((256, 512), BF),
        grid_spec=pltpu.PrefetchScalarGridSpec(
            num_scalar_prefetch=1,
            grid=(PARTS // CONDS,),
            in_specs=[
                pl.BlockSpec((2, WIRE, 128), lambda c, o: (o[0], 0, 0)),
                pl.BlockSpec((2, WIRE, 128), lambda c, o: (0, 0, 0)),
                pl.BlockSpec((CONDS, WIRE, 128), lambda c, o: (c, 0, 0)),
                pl.BlockSpec((4 * KROWS, 768), lambda c, o: (0, 0)),
                pl.BlockSpec((4, 256, 256), lambda c, o: (0, 0, 0)),
            ],
            out_specs=pl.BlockSpec((256, 512), lambda c, o: (0, 0)),
            scratch_shapes=[
                pltpu.VMEM((4, 2, ROWS, 128), F32),
                pltpu.VMEM((4, ROWS, 128), F32),
                pltpu.VMEM((KROWS * 128, 128), F32),
                pltpu.VMEM((KROWS * 128, 128), F32),
            ],
        ),
        compiler_params=pltpu.CompilerParams(vmem_limit_bytes=40 * 2**20),
        name="ztransform",
    )(chip, val_wire, second, cond_wire, jnp.asarray(table), ytab)


def g_kernel(parity_ref, plane_ref, index_ref, phase_ref, out_ref):
    row = lax.broadcasted_iota(jnp.int32, (512, GCHUNK), 0)
    for chunk in range(out_ref.shape[0]):
        pick = jnp.where(row == index_ref[chunk, 0], 1.0, 0.0).astype(BF)
        at = jnp.dot(plane_ref[...], pick, preferred_element_type=F32)
        real = jnp.zeros((PAIRS, GCHUNK), F32)
        imag = jnp.zeros((PAIRS, GCHUNK), F32)
        for x in range(2):
            c = phase_ref[chunk, 0, 2 * x : 2 * x + 1]
            s = phase_ref[chunk, 0, 2 * x + 1 : 2 * x + 2]
            re = at[x * 128 : x * 128 + PAIRS]
            im = at[x * 128 + PAIRS : (x + 1) * 128]
            real = real + re * c + im * s
            imag = imag + im * c - re * s
        out_ref[chunk, :PAIRS] = real.astype(out_ref.dtype)
        out_ref[chunk, PAIRS:] = imag.astype(out_ref.dtype)


def g_elements(parity, plane, index, phase, dtype):
    chips = index.shape[0]
    return pl.pallas_call(
        g_kernel,
        out_shape=jax.ShapeDtypeStruct((chips, 128, GCHUNK), dtype),
        grid_spec=pltpu.PrefetchScalarGridSpec(
            num_scalar_prefetch=1,
            grid=(1,),
            in_specs=[
                pl.BlockSpec((256, 512), lambda i, k: (0, 0)),
                pl.BlockSpec((chips, 1, 1, GCHUNK), lambda i, k: (0, k[0], 0, 0)),
                pl.BlockSpec((chips, 1, 4, GCHUNK), lambda i, k: (0, k[0], 0, 0)),
            ],
            out_specs=pl.BlockSpec((chips, 128, GCHUNK), lambda i, k: (0, 0, 0)),
        ),
        compiler_params=pltpu.CompilerParams(vmem_limit_bytes=40 * 2**20),
        cost_estimate=pl.CostEstimate(flops=2 * 10**9, transcendentals=0, bytes_accessed=12_000_000),
        name="gelements",
    )(parity, plane, index, phase)


def shards(valence, conduction, val_energy, cond_energy, cond_band, owners, gvectors):
    grid_pos = lax.axis_index("grid")
    band_pos = lax.axis_index("band")
    x_local = valence.shape[2]
    n_grid = lax.axis_size("grid")

    rows_all = x_local * LENGTH
    cond_wire = pack_cond(conduction.reshape(2, rows_all, LENGTH), cond_band)
    cond_wire, core = lax.optimization_barrier((cond_wire, band_pos & 1))
    cond_wire = lax.all_to_all(cond_wire, "band", 0, 0, tiled=True)

    first, second = owners[0], owners[1]
    bands = valence.reshape(2, 2, rows_all, LENGTH)
    sibling = pack_val(bands, (1 - core)[None])
    sibling = lax.ppermute(sibling, "band", [(b, b ^ 1) for b in range(PARTS)])
    here = (first >> 1) == (band_pos >> 1)
    own = jnp.where(here, first == band_pos, second == band_pos)
    val_wire = pack_val(bands, core[None], own.astype(jnp.int32)[None], sibling)
    val_wire = lax.all_to_all(val_wire, "band", 0, 0, tiled=True)
    cond_wire, val_wire = lax.optimization_barrier((cond_wire, val_wire))

    ytab = plane_tables(band_pos & 3)
    chip = (first >> 1)[None]

    def exchange_again(operands):
        bands, sibling, val_wire, cond_wire, ytab = operands
        again = pack_val(bands, core[None], (second == band_pos).astype(jnp.int32)[None], sibling)
        again = lax.all_to_all(again, "band", 0, 0, tiled=True)
        again = lax.dynamic_slice_in_dim(again, (second >> 1) * 2, 2, 0)
        return z_transform(chip, val_wire, again, cond_wire, ytab)

    def from_first(operands):
        _, _, val_wire, cond_wire, ytab = operands
        again = lax.dynamic_slice_in_dim(val_wire, (second >> 1) * 2, 2, 0)
        return z_transform(chip, val_wire, again, cond_wire, ytab)

    both = (first != second) & ((first >> 1) == (second >> 1))
    plane = lax.cond(both, exchange_again, from_first, (bands, sibling, val_wire, cond_wire, ytab))

    numbers = cond_wire[:, WIRE - 1, 127].astype(jnp.int32)
    order = jnp.arange(cond_energy.shape[0], dtype=jnp.int32)
    levels = jnp.sum(jnp.where(numbers[:, None] == order[None, :], cond_energy[None, :], 0.0), axis=1)
    val_index = (owners[:, None] * 2 + jnp.arange(2, dtype=jnp.int32)[None, :]).reshape(4)
    val_levels = val_energy[val_index]
    weight = (2.0 / (PAIRS * (val_levels[None, :] - levels[:, None]))).reshape(PAIRS)

    signed = (gvectors + GMAX) % LENGTH
    slot = jnp.where(signed[2] < SLOTS, signed[2] * SIDE, 256 + (signed[2] - SLOTS) * SIDE)
    index = (slot + signed[1]).reshape(PARTS // 2, 2, 1, GCHUNK)
    x_first = grid_pos * x_local + 5 * (band_pos >> 2) + (band_pos & 3)
    norm = float(LENGTH) ** (-1.5)
    waves = []
    for x in range(2):
        angle = (gvectors[0] * (x_first + x) % LENGTH).astype(F32) * (2.0 * math.pi / LENGTH)
        waves += [jnp.cos(angle), jnp.sin(angle)]
    phase = jnp.stack(waves).astype(BF).astype(F32) * norm
    phase = phase.reshape(4, PARTS, GCHUNK).transpose(1, 0, 2).reshape(PARTS // 2, 2, 4, GCHUNK)

    core = band_pos & 1
    siblings = [(b, b ^ 1) for b in range(PARTS)]
    away = g_elements((1 - core)[None], plane, index, phase, BF)
    come = lax.ppermute(away, "band", siblings)
    keep = g_elements(core[None], plane, index, phase, F32)
    parts = (keep + come.astype(F32)).astype(BF)
    parts = lax.all_to_all(parts, "grid", 0, 0, tiled=True)
    block = jnp.sum(parts.astype(F32), axis=0)
    block = block + lax.ppermute(block.astype(BF), "band", [(b, b ^ 2) for b in range(PARTS)]).astype(F32)
    narrow = block.astype(BF)
    for turn in (4, 8, 12):
        step = [(b, (b + turn) % PARTS) for b in range(PARTS)]
        block = block + lax.ppermute(narrow, "band", step).astype(F32)

    narrow = block.astype(BF)
    far = []
    for b in range(PARTS):
        for g in range(n_grid):
            far.append((b * n_grid + g, (2 * g + b % 2) * n_grid + b // 2))
    column = lax.ppermute(narrow, ("band", "grid"), far).astype(F32)
    other = lax.ppermute(narrow, "band", siblings)
    left = jnp.where(core == 1, other, narrow)
    right = jnp.where(core == 1, narrow, other)
    rows = jnp.concatenate([left, right], axis=1).astype(F32)

    w2 = jnp.concatenate([weight, weight])[:, None]
    for_real = column * w2
    for_imag = jnp.concatenate([-for_real[PAIRS:], for_real[:PAIRS]], axis=0)
    high = lax.Precision.HIGHEST
    chi_re = jnp.einsum("pr,pc->rc", rows, for_real, precision=high)
    chi_im = jnp.einsum("pr,pc->rc", rows, for_imag, precision=high)
    return jnp.stack([chi_re, chi_im])


def solution(mesh):
    return jax.shard_map(
        shards,
        mesh=mesh,
        in_specs=(
            P("band", None, "grid", None, None),
            P("band", None, "grid", None, None),
            P(),
            P(),
            P("band"),
            P(),
            P(),
        ),
        out_specs=P(None, "grid", "band"),
        check_vma=False,
    )
```

```python
import functools
import math

import jax
import jax.numpy as jnp
import numpy as np
from jax import lax
from jax.experimental import pallas as pl
from jax.experimental.pallas import tpu as pltpu
from jax.sharding import PartitionSpec as P

LENGTH = 160
GMAX = 10
SIDE = 2 * GMAX + 1
PARTS = 16
ROWS = 200
TAIL = 104
WIRE = 2 * ROWS + TAIL
PAIRS = 64
PACK = 8
CONDS = 4
SLOTS = 12
KROWS = 24
GCHUNK = 256
BF = jnp.bfloat16
F32 = jnp.float32


def host_tables():
    freq = (np.arange(SIDE) - GMAX) % LENGTH
    pos = np.arange(LENGTH)
    angle = ((freq[:, None] * pos[None, :]) % LENGTH).astype(np.float32) * np.float32(2.0 * math.pi / LENGTH)
    rnd = lambda a: a.astype(np.float32).astype(jnp.bfloat16).astype(np.float32)
    return rnd(np.cos(angle)), rnd(np.sin(angle))


def z_table():
    cos, sin = host_tables()
    out = np.zeros((2 * KROWS, 384), np.float32)
    cm, sm, ct, st = cos[:, :128], sin[:, :128], cos[:, 128:], sin[:, 128:]
    out[:SIDE] = np.concatenate([cm, sm, ct, ct, st, -st], axis=1)
    out[KROWS : KROWS + SIDE] = np.concatenate([-sm, cm, -st, -st, ct, -ct], axis=1)
    return out.astype(jnp.bfloat16)


def y_tables():
    cos, sin = host_tables()
    out = np.zeros((4, 256, 4, 32), np.float32)
    for shift in range(4):
        for row in range(ROWS):
            flat = 40 * shift + row
            x, y = divmod(flat, LENGTH)
            out[shift, row, 2 * x, :SIDE] = cos[:, y]
            out[shift, row, 2 * x + 1, :SIDE] = sin[:, y]
    return out.reshape(4, 256, 128).astype(jnp.bfloat16)


def in_hbm(array):
    return pltpu.with_memory_space_constraint(array, pltpu.HBM)


def pack_band(src, out, fill):
    real, imag = src[0], src[1]
    out[0:ROWS] = real[:, :128]
    out[ROWS : 2 * ROWS] = imag[:, :128]
    tail = jnp.concatenate([real[:, 128:].astype(F32), imag[:, 128:].astype(F32)], axis=1)
    low = tail[:TAIL]
    high = jnp.concatenate([tail[TAIL:], jnp.full((2 * TAIL - ROWS, 64), 1.0, F32) * fill], axis=0)
    out[2 * ROWS :] = jnp.concatenate([low, high], axis=1).astype(BF)


def pack_cond_kernel(number_ref, cond_ref, out_ref):
    for t in range(PACK):
        rows = pl.ds(t * ROWS, ROWS)
        pack_band(cond_ref.at[:, rows], out_ref.at[t], number_ref[0].astype(F32))


def pack_cond(conduction, number):
    return pl.pallas_call(
        pack_cond_kernel,
        out_shape=pltpu.HBM((PARTS, WIRE, 128), BF),
        grid_spec=pltpu.PrefetchScalarGridSpec(
            num_scalar_prefetch=1,
            grid=(PARTS // PACK,),
            in_specs=[pl.BlockSpec((2, PACK * ROWS, LENGTH), lambda t, n: (0, t, 0))],
            out_specs=pl.BlockSpec((PACK, WIRE, 128), lambda t, n: (t, 0, 0)),
        ),
        cost_estimate=pl.CostEstimate(flops=0, transcendentals=0, bytes_accessed=6_000_000),
        compiler_params=pltpu.CompilerParams(vmem_limit_bytes=14 * 2**20),
        name="packcond",
    )(number, conduction)


def pack_val_kernel(band_ref, val_ref, out_ref):
    for t in range(PACK):
        pack_band(val_ref.at[0, :, pl.ds(t * ROWS, ROWS)], out_ref.at[t], 0.0)


def pack_choice_kernel(band_ref, own_ref, val_ref, *refs):
    out_ref = refs[-1]

    @pl.when(own_ref[0] == 1)
    def _():
        pack_val_kernel(band_ref, val_ref, out_ref)

    for t in range(PARTS // PACK):

        @pl.when((own_ref[0] == 0) & (pl.program_id(0) == t))
        def _():
            out_ref[...] = refs[t][...]


WIRE_BLOCK = (PACK, WIRE, 128)
VAL_BLOCK = (1, 2, PACK * ROWS, LENGTH)


def pack_give(valence, band, t):
    return pl.pallas_call(
        pack_val_kernel,
        out_shape=jax.ShapeDtypeStruct(WIRE_BLOCK, BF),
        grid_spec=pltpu.PrefetchScalarGridSpec(
            num_scalar_prefetch=1,
            grid=(1,),
            in_specs=[pl.BlockSpec(VAL_BLOCK, lambda i, k: (k[0], 0, t, 0))],
            out_specs=pl.BlockSpec(WIRE_BLOCK, lambda i, k: (0, 0, 0)),
        ),
        cost_estimate=pl.CostEstimate(flops=0, transcendentals=0, bytes_accessed=3_000_000),
        compiler_params=pltpu.CompilerParams(vmem_limit_bytes=14 * 2**20),
        name="packgive",
    )(band, valence)


def pack_choice(valence, band, own, others):
    return pl.pallas_call(
        pack_choice_kernel,
        out_shape=pltpu.HBM((PARTS, WIRE, 128), BF),
        grid_spec=pltpu.PrefetchScalarGridSpec(
            num_scalar_prefetch=2,
            grid=(PARTS // PACK,),
            in_specs=[pl.BlockSpec(VAL_BLOCK, lambda t, k, o: (k[0], 0, t, 0))]
            + [pl.BlockSpec(WIRE_BLOCK, lambda t, k, o: (0, 0, 0)) for _ in others],
            out_specs=pl.BlockSpec(WIRE_BLOCK, lambda t, k, o: (t, 0, 0)),
        ),
        cost_estimate=pl.CostEstimate(flops=0, transcendentals=0, bytes_accessed=8_000_000),
        compiler_params=pltpu.CompilerParams(vmem_limit_bytes=16 * 2**20),
        name="packchoice",
    )(band, own, valence, *others)


def unpack_tail(tail):
    return jnp.concatenate([tail[:, :64], tail[: ROWS - TAIL, 64:]], axis=0)


def plane_tables(shift):
    tab = lax.dynamic_index_in_dim(jnp.asarray(y_tables()), shift, 0, keepdims=False)
    tab = tab.reshape(256, 4, 32)[:, :, :SIDE].transpose(1, 0, 2)
    return jnp.pad(jnp.tile(tab, (1, 1, SLOTS)), ((0, 0), (0, 0), (0, 256 - SLOTS * SIDE)))


def z_kernel(where_ref, v0_ref, v1_ref, again_ref, cond_ref, table_ref, ytab_ref, out_ref, val_main, val_tail, low_ref, high_ref):
    step = pl.program_id(0)

    def take(i, src):
        val_main[i, 0] = src[0:ROWS].astype(F32)
        val_main[i, 1] = src[ROWS : 2 * ROWS].astype(F32)
        both = unpack_tail(src[2 * ROWS :].astype(F32))
        val_tail[i] = jnp.concatenate([both, both], axis=1)

    @pl.when(step == 0)
    def _():
        for j in range(2):
            take(j, v0_ref.at[j])
            take(2 + j, v1_ref.at[j])
        high_ref[...] = jnp.zeros_like(high_ref)

    @pl.when((step == 0) & (where_ref[2] == 1))
    def _():
        for j in range(2):
            take(2 + j, again_ref.at[j])

    @pl.loop(0, CONDS)
    def _(c):
        cre = cond_ref[c, 0:ROWS].astype(F32)
        cim = cond_ref[c, ROWS : 2 * ROWS].astype(F32)
        both = unpack_tail(cond_ref[c, 2 * ROWS :].astype(F32))
        ctail = jnp.concatenate([both, both[:, 32:], both[:, :32]], axis=1)
        first = (step * CONDS + c) * 4
        for i in range(0, 4, 2):
            density = []
            for j in (i, i + 1):
                vre, vim = val_main[j, 0], val_main[j, 1]
                density += [vre * cre + vim * cim, vre * cim - vim * cre, val_tail[j] * ctail]
            density = jnp.concatenate(density, axis=1).astype(BF)
            along = lax.dot_general(
                table_ref[...], density, (((1,), (1,)), ((), ())), preferred_element_type=F32
            )
            for j in range(2):
                for part in range(2):
                    start = part * PAIRS + first + i + j
                    at = (2 * j + part) * KROWS
                    piece = along[at : at + KROWS]
                    low_ref[pl.ds(start, KROWS, stride=128), :] = piece[:, :128]
                    high_ref[pl.ds(start, KROWS, stride=128), 0 : ROWS - 128] = piece[:, 128:]

    @pl.when(step == pl.num_programs(0) - 1)
    def _():
        lane = lax.broadcasted_iota(jnp.int32, (256, 256), 1)
        acc = [None] * 4
        for s in range(SLOTS):
            left = []
            for k in (s, s + SLOTS):
                rows = pl.ds(k * 128, 128)
                left.append(jnp.concatenate([low_ref[rows], high_ref[rows]], axis=1).astype(BF))
            left = jnp.concatenate(left, axis=0)
            keep = (lane >= s * SIDE) & (lane < (s + 1) * SIDE)
            for t in range(4):
                right = jnp.where(keep, ytab_ref[t], jnp.zeros((256, 256), BF))
                term = jnp.dot(left, right, preferred_element_type=F32)
                acc[t] = term if acc[t] is None else acc[t] + term
        for x in range(2):
            for tile in range(2):
                c = acc[2 * x][tile * 128 : (tile + 1) * 128]
                s = acc[2 * x + 1][tile * 128 : (tile + 1) * 128]
                lanes = pl.ds(tile * 256, 256)
                out_ref[x * 128 : x * 128 + PAIRS, lanes] = (c[:PAIRS] + s[PAIRS:]).astype(BF)
                out_ref[x * 128 + PAIRS : (x + 1) * 128, lanes] = (c[PAIRS:] - s[:PAIRS]).astype(BF)


def z_transform(where, val_wire, again, cond_wire, ytab):
    single = z_table()
    table = np.zeros((4 * KROWS, 768), single.dtype)
    table[: 2 * KROWS, :384] = single
    table[2 * KROWS :, 384:] = single
    return pl.pallas_call(
        z_kernel,
        out_shape=jax.ShapeDtypeStruct((256, 512), BF),
        grid_spec=pltpu.PrefetchScalarGridSpec(
            num_scalar_prefetch=1,
            grid=(PARTS // CONDS,),
            in_specs=[
                pl.BlockSpec((2, WIRE, 128), lambda c, o: (o[0], 0, 0)),
                pl.BlockSpec((2, WIRE, 128), lambda c, o: (o[1], 0, 0)),
                pl.BlockSpec((2, WIRE, 128), lambda c, o: (0, 0, 0)),
                pl.BlockSpec((CONDS, WIRE, 128), lambda c, o: (c, 0, 0)),
                pl.BlockSpec((4 * KROWS, 768), lambda c, o: (0, 0)),
                pl.BlockSpec((4, 256, 256), lambda c, o: (0, 0, 0)),
            ],
            out_specs=pl.BlockSpec((256, 512), lambda c, o: (0, 0)),
            scratch_shapes=[
                pltpu.VMEM((4, 2, ROWS, 128), F32),
                pltpu.VMEM((4, ROWS, 128), F32),
                pltpu.VMEM((KROWS * 128, 128), F32),
                pltpu.VMEM((KROWS * 128, 128), F32),
            ],
        ),
        compiler_params=pltpu.CompilerParams(vmem_limit_bytes=20 * 2**20),
        name="ztransform",
    )(where, val_wire, val_wire, again, cond_wire, jnp.asarray(table), ytab)


def g_kernel(parity_ref, plane_ref, index_ref, phase_ref, out_ref):
    row = lax.broadcasted_iota(jnp.int32, (512, GCHUNK), 0)
    for chunk in range(out_ref.shape[0]):
        pick = jnp.where(row == index_ref[chunk, 0], 1.0, 0.0).astype(BF)
        at = jnp.dot(plane_ref[...], pick, preferred_element_type=F32)
        real = jnp.zeros((PAIRS, GCHUNK), F32)
        imag = jnp.zeros((PAIRS, GCHUNK), F32)
        for x in range(2):
            c = phase_ref[chunk, 0, 2 * x : 2 * x + 1]
            s = phase_ref[chunk, 0, 2 * x + 1 : 2 * x + 2]
            re = at[x * 128 : x * 128 + PAIRS]
            im = at[x * 128 + PAIRS : (x + 1) * 128]
            real = real + re * c + im * s
            imag = imag + im * c - re * s
        out_ref[chunk, :PAIRS] = real.astype(out_ref.dtype)
        out_ref[chunk, PAIRS:] = imag.astype(out_ref.dtype)


def g_elements(parity, plane, index, phase, dtype):
    chips = index.shape[0]
    return pl.pallas_call(
        g_kernel,
        out_shape=jax.ShapeDtypeStruct((chips, 128, GCHUNK), dtype),
        grid_spec=pltpu.PrefetchScalarGridSpec(
            num_scalar_prefetch=1,
            grid=(1,),
            in_specs=[
                pl.BlockSpec((256, 512), lambda i, k: (0, 0)),
                pl.BlockSpec((chips, 1, 1, GCHUNK), lambda i, k: (0, k[0], 0, 0)),
                pl.BlockSpec((chips, 1, 4, GCHUNK), lambda i, k: (0, k[0], 0, 0)),
            ],
            out_specs=pl.BlockSpec((chips, 128, GCHUNK), lambda i, k: (0, 0, 0)),
        ),
        compiler_params=pltpu.CompilerParams(vmem_limit_bytes=10 * 2**20),
        cost_estimate=pl.CostEstimate(flops=2 * 10**9, transcendentals=0, bytes_accessed=12_000_000),
        name="gelements",
    )(parity, plane, index, phase)


def chi_kernel(core_ref, mine_ref, other_ref, column_ref, weight_ref, out_ref):
    real = column_ref[...].astype(F32) * weight_ref[...]
    imag = jnp.concatenate([-real[PAIRS:], real[:PAIRS]], axis=0)
    sides = []
    for side in (real, imag):
        top = side.astype(BF)
        sides.append((top, (side - top.astype(F32)).astype(BF)))
    for half, rows in ((core_ref[0], mine_ref[...]), (1 - core_ref[0], other_ref[...])):
        at = pl.ds(pl.multiple_of(half * GCHUNK, GCHUNK), GCHUNK)
        for part in range(2):
            total = None
            for piece in sides[part]:
                term = lax.dot_general(rows, piece, (((0,), (0,)), ((), ())), preferred_element_type=F32)
                total = term if total is None else total + term
            out_ref[part, at, :] = total


def chi_block(core, mine, other, column, weight):
    spec = pl.BlockSpec((128, GCHUNK), lambda i, k: (0, 0))
    return pl.pallas_call(
        chi_kernel,
        out_shape=jax.ShapeDtypeStruct((2, 2 * GCHUNK, GCHUNK), F32),
        grid_spec=pltpu.PrefetchScalarGridSpec(
            num_scalar_prefetch=1,
            grid=(1,),
            in_specs=[spec, spec, spec, pl.BlockSpec((128, 1), lambda i, k: (0, 0))],
            out_specs=pl.BlockSpec((2, 2 * GCHUNK, GCHUNK), lambda i, k: (0, 0, 0)),
        ),
        compiler_params=pltpu.CompilerParams(vmem_limit_bytes=8 * 2**20),
        name="chi",
    )(core, mine, other, column, weight)


def shards(valence, conduction, val_energy, cond_energy, cond_band, owners, gvectors):
    grid_pos = lax.axis_index("grid")
    band_pos = lax.axis_index("band")
    x_local = valence.shape[2]
    n_grid = lax.axis_size("grid")

    rows_all = x_local * LENGTH
    cond_wire = pack_cond(in_hbm(conduction.reshape(2, rows_all, LENGTH)), cond_band)
    cond_wire, core = lax.optimization_barrier((cond_wire, band_pos & 1))
    cond_wire = lax.all_to_all(cond_wire, "band", 0, 0, tiled=True)

    first, second = owners[0], owners[1]
    bands = in_hbm(valence.reshape(2, 2, rows_all, LENGTH))
    siblings = [(b, b ^ 1) for b in range(PARTS)]
    sibling = [
        lax.ppermute(pack_give(bands, (1 - core)[None], t), "band", siblings) for t in range(PARTS // PACK)
    ]
    here = (first >> 1) == (band_pos >> 1)
    own = jnp.where(here, first == band_pos, second == band_pos)
    val_wire = pack_choice(bands, core[None], own.astype(jnp.int32)[None], sibling)
    val_wire = lax.all_to_all(val_wire, "band", 0, 0, tiled=True)
    cond_wire, val_wire = lax.optimization_barrier((cond_wire, val_wire))

    ytab = plane_tables(band_pos & 3)

    def exchange_again(operands):
        bands, sibling = operands
        again = pack_choice(bands, core[None], (second == band_pos).astype(jnp.int32)[None], sibling)
        again = lax.all_to_all(again, "band", 0, 0, tiled=True)
        return lax.dynamic_slice_in_dim(again, (second >> 1) * 2, 2, 0)

    def nothing_more(operands):
        return jnp.zeros((2, WIRE, 128), BF)

    both = (first != second) & ((first >> 1) == (second >> 1))
    val_wire, both = lax.optimization_barrier((val_wire, both))
    again = lax.cond(both, exchange_again, nothing_more, (bands, sibling))
    where = jnp.stack([first >> 1, second >> 1, both.astype(jnp.int32)])
    plane = z_transform(where, val_wire, again, in_hbm(cond_wire), ytab)

    numbers = cond_wire[:, WIRE - 1, 127].astype(jnp.int32)
    order = jnp.arange(cond_energy.shape[0], dtype=jnp.int32)
    levels = jnp.sum(jnp.where(numbers[:, None] == order[None, :], cond_energy[None, :], 0.0), axis=1)
    val_index = (owners[:, None] * 2 + jnp.arange(2, dtype=jnp.int32)[None, :]).reshape(4)
    val_levels = val_energy[val_index]
    weight = (2.0 / (PAIRS * (val_levels[None, :] - levels[:, None]))).reshape(PAIRS)

    signed = (gvectors + GMAX) % LENGTH
    slot = jnp.where(signed[2] < SLOTS, signed[2] * SIDE, 256 + (signed[2] - SLOTS) * SIDE)
    index = (slot + signed[1]).reshape(PARTS // 2, 2, 1, GCHUNK)
    x_first = grid_pos * x_local + 5 * (band_pos >> 2) + (band_pos & 3)
    norm = float(LENGTH) ** (-1.5)
    waves = []
    for x in range(2):
        angle = (gvectors[0] * (x_first + x) % LENGTH).astype(F32) * (2.0 * math.pi / LENGTH)
        waves += [jnp.cos(angle), jnp.sin(angle)]
    phase = jnp.stack(waves).astype(BF).astype(F32) * norm
    phase = phase.reshape(4, PARTS, GCHUNK).transpose(1, 0, 2).reshape(PARTS // 2, 2, 4, GCHUNK)

    core = band_pos & 1
    away = g_elements((1 - core)[None], plane, index, phase, BF)
    come = lax.ppermute(away, "band", siblings)
    keep = g_elements(core[None], plane, index, phase, F32)
    parts = (keep + come.astype(F32)).astype(BF)
    parts = lax.all_to_all(parts, "grid", 0, 0, tiled=True)
    block = jnp.sum(parts.astype(F32), axis=0)
    block = block + lax.ppermute(block.astype(BF), "band", [(b, b ^ 2) for b in range(PARTS)]).astype(F32)
    narrow = block.astype(BF)
    for turn in (4, 8, 12):
        step = [(b, (b + turn) % PARTS) for b in range(PARTS)]
        block = block + lax.ppermute(narrow, "band", step).astype(F32)

    narrow = block.astype(BF)
    far = []
    for b in range(PARTS):
        for g in range(n_grid):
            far.append((b * n_grid + g, (2 * g + b % 2) * n_grid + b // 2))
    column = lax.ppermute(narrow, ("band", "grid"), far)
    other = lax.ppermute(narrow, "band", siblings)
    return chi_block(core[None], narrow, other, column, jnp.concatenate([weight, weight])[:, None])


def solution(mesh):
    return jax.shard_map(
        shards,
        mesh=mesh,
        in_specs=(
            P("band", None, "grid", None, None),
            P("band", None, "grid", None, None),
            P(),
            P(),
            P("band"),
            P(),
            P(),
        ),
        out_specs=P(None, "grid", "band"),
        check_vma=False,
    )
```

```python
import functools
import math

import jax
import jax.numpy as jnp
import numpy as np
from jax import lax
from jax.experimental import pallas as pl
from jax.experimental.pallas import tpu as pltpu
from jax.sharding import PartitionSpec as P

LENGTH = 160
GMAX = 10
SIDE = 2 * GMAX + 1
PARTS = 16
ROWS = 200
TAIL = 104
WIRE = 2 * ROWS + TAIL
PAIRS = 64
PACK = 8
CHIPS = 8
CONDS = 4
SLOTS = 12
KROWS = 24
GCHUNK = 256
BF = jnp.bfloat16
F32 = jnp.float32


def host_tables():
    freq = (np.arange(SIDE) - GMAX) % LENGTH
    pos = np.arange(LENGTH)
    angle = ((freq[:, None] * pos[None, :]) % LENGTH).astype(np.float32) * np.float32(2.0 * math.pi / LENGTH)
    rnd = lambda a: a.astype(np.float32).astype(jnp.bfloat16).astype(np.float32)
    return rnd(np.cos(angle)), rnd(np.sin(angle))


def z_table():
    cos, sin = host_tables()
    out = np.zeros((2 * KROWS, 384), np.float32)
    cm, sm, ct, st = cos[:, :128], sin[:, :128], cos[:, 128:], sin[:, 128:]
    out[:SIDE] = np.concatenate([cm, sm, ct, ct, st, -st], axis=1)
    out[KROWS : KROWS + SIDE] = np.concatenate([-sm, cm, -st, -st, ct, -ct], axis=1)
    return out.astype(jnp.bfloat16)


def y_tables():
    cos, sin = host_tables()
    out = np.zeros((4, 256, 4, 32), np.float32)
    for shift in range(4):
        for row in range(ROWS):
            flat = 40 * shift + row
            x, y = divmod(flat, LENGTH)
            out[shift, row, 2 * x, :SIDE] = cos[:, y]
            out[shift, row, 2 * x + 1, :SIDE] = sin[:, y]
    return out.reshape(4, 256, 128).astype(jnp.bfloat16)


def in_hbm(array):
    return pltpu.with_memory_space_constraint(array, pltpu.HBM)


def pack_band(src, out, fill):
    real, imag = src[0], src[1]
    out[0:ROWS] = real[:, :128]
    out[ROWS : 2 * ROWS] = imag[:, :128]
    tail = jnp.concatenate([real[:, 128:].astype(F32), imag[:, 128:].astype(F32)], axis=1)
    low = tail[:TAIL]
    high = jnp.concatenate([tail[TAIL:], jnp.full((2 * TAIL - ROWS, 64), 1.0, F32) * fill], axis=0)
    out[2 * ROWS :] = jnp.concatenate([low, high], axis=1).astype(BF)


def pack_cond_kernel(number_ref, cond_ref, out_ref):
    for t in range(PACK):
        rows = pl.ds(t * ROWS, ROWS)
        pack_band(cond_ref.at[:, rows], out_ref.at[t], number_ref[0].astype(F32))


def pack_cond(conduction, number):
    return pl.pallas_call(
        pack_cond_kernel,
        out_shape=pltpu.HBM((PARTS, WIRE, 128), BF),
        grid_spec=pltpu.PrefetchScalarGridSpec(
            num_scalar_prefetch=1,
            grid=(PARTS // PACK,),
            in_specs=[pl.BlockSpec((2, PACK * ROWS, LENGTH), lambda t, n: (0, t, 0))],
            out_specs=pl.BlockSpec((PACK, WIRE, 128), lambda t, n: (t, 0, 0)),
        ),
        cost_estimate=pl.CostEstimate(flops=0, transcendentals=0, bytes_accessed=6_000_000),
        compiler_params=pltpu.CompilerParams(vmem_limit_bytes=14 * 2**20),
        name="packcond",
    )(number, conduction)


def pack_give_kernel(place_ref, val_ref, out_ref):
    for s in range(CHIPS // 2):
        for band in range(2):
            pack_band(val_ref.at[band, :, s ^ (place_ref[1] & 3), 0], out_ref.at[s, band], 0.0)


def pack_give(valence, place, half):
    block = (2, 2, CHIPS // 2, 1, ROWS, LENGTH)
    return pl.pallas_call(
        pack_give_kernel,
        out_shape=jax.ShapeDtypeStruct((CHIPS // 2, 2, WIRE, 128), BF),
        grid_spec=pltpu.PrefetchScalarGridSpec(
            num_scalar_prefetch=1,
            grid=(1,),
            in_specs=[pl.BlockSpec(block, lambda i, p: (0, 0, half ^ (p[1] >> 2), 1 - p[0], 0, 0))],
            out_specs=pl.BlockSpec((CHIPS // 2, 2, WIRE, 128), lambda i, p: (0, 0, 0, 0)),
        ),
        cost_estimate=pl.CostEstimate(flops=0, transcendentals=0, bytes_accessed=3_000_000),
        compiler_params=pltpu.CompilerParams(vmem_limit_bytes=16 * 2**20),
        name="packgive",
    )(place, valence)


def pack_choice_kernel(place_ref, val_ref, *refs):
    others, outs = refs[:2], refs[2:]

    @pl.when(place_ref[2] == 1)
    def _():
        for s in range(CHIPS):
            for band in range(2):
                pack_band(val_ref.at[band, :, s ^ place_ref[1], 0], outs[s].at[band], 0.0)

    @pl.when(place_ref[2] == 0)
    def _():
        for s in range(CHIPS):
            outs[s][...] = others[s // 4][s % 4]


def pack_choice(valence, place, others):
    piece = (2, WIRE, 128)
    return pl.pallas_call(
        pack_choice_kernel,
        out_shape=[jax.ShapeDtypeStruct(piece, BF)] * CHIPS,
        grid_spec=pltpu.PrefetchScalarGridSpec(
            num_scalar_prefetch=1,
            grid=(1,),
            in_specs=[pl.BlockSpec((2, 2, CHIPS, 1, ROWS, LENGTH), lambda i, p: (0, 0, 0, p[0], 0, 0))]
            + [pl.BlockSpec((CHIPS // 2, 2, WIRE, 128), lambda i, p: (0, 0, 0, 0))] * 2,
            out_specs=[pl.BlockSpec(piece, lambda i, p: (0, 0, 0))] * CHIPS,
        ),
        cost_estimate=pl.CostEstimate(flops=0, transcendentals=0, bytes_accessed=8_000_000),
        compiler_params=pltpu.CompilerParams(vmem_limit_bytes=28 * 2**20),
        name="packchoice",
    )(place, valence, *others)


def send_to_chips(pieces):
    got = [pieces[0]]
    for s in range(1, CHIPS):
        got.append(lax.ppermute(pieces[s], "band", [(b, b ^ (2 * s)) for b in range(PARTS)]))
    return got


def unpack_tail(tail):
    return jnp.concatenate([tail[:, :64], tail[: ROWS - TAIL, 64:]], axis=0)


def plane_tables(shift):
    tab = lax.dynamic_index_in_dim(jnp.asarray(y_tables()), shift, 0, keepdims=False)
    tab = tab.reshape(256, 4, 32)[:, :, :SIDE].transpose(1, 0, 2)
    return jnp.pad(jnp.tile(tab, (1, 1, SLOTS)), ((0, 0), (0, 0), (0, 256 - SLOTS * SIDE)))


def z_kernel(where_ref, *refs):
    val_refs, again_ref = refs[:CHIPS], refs[CHIPS]
    cond_ref, table_ref, ytab_ref, out_ref, raw_ref, val_main, val_tail, low_ref, high_ref = refs[CHIPS + 1 :]
    step = pl.program_id(0)

    for s in range(CHIPS):
        for r in range(2):

            @pl.when((step == 0) & (where_ref[r] == s))
            def _():
                raw_ref[r] = val_refs[s][...]

    @pl.when((step == 0) & (where_ref[2] == 1))
    def _():
        raw_ref[1] = again_ref[...]

    @pl.when(step == 0)
    def _():
        for i in range(4):
            src = raw_ref.at[i // 2, i % 2]
            val_main[i, 0] = src[0:ROWS].astype(F32)
            val_main[i, 1] = src[ROWS : 2 * ROWS].astype(F32)
            both = unpack_tail(src[2 * ROWS :].astype(F32))
            val_tail[i] = jnp.concatenate([both, both], axis=1)
        high_ref[...] = jnp.zeros_like(high_ref)

    @pl.loop(0, CONDS, unroll=CONDS)
    def _(c):
        cre = cond_ref[c, 0:ROWS].astype(F32)
        cim = cond_ref[c, ROWS : 2 * ROWS].astype(F32)
        both = unpack_tail(cond_ref[c, 2 * ROWS :].astype(F32))
        ctail = jnp.concatenate([both, both[:, 32:], both[:, :32]], axis=1)
        first = (step * CONDS + c) * 4
        for i in range(0, 4, 2):
            density = []
            for j in (i, i + 1):
                vre, vim = val_main[j, 0], val_main[j, 1]
                density += [vre * cre + vim * cim, vre * cim - vim * cre, val_tail[j] * ctail]
            density = jnp.concatenate(density, axis=1).astype(BF)
            along = lax.dot_general(
                table_ref[...], density, (((1,), (1,)), ((), ())), preferred_element_type=F32
            )
            for j in range(2):
                for part in range(2):
                    start = part * PAIRS + first + i + j
                    at = (2 * j + part) * KROWS
                    piece = along[at : at + KROWS]
                    low_ref[pl.ds(start, KROWS, stride=128), :] = piece[:, :128]
                    high_ref[pl.ds(start, KROWS, stride=128), 0 : ROWS - 128] = piece[:, 128:]

    @pl.when(step == pl.num_programs(0) - 1)
    def _():
        lane = lax.broadcasted_iota(jnp.int32, (256, 256), 1)
        acc = [None] * 4
        for s in range(SLOTS):
            left = []
            for k in (s, s + SLOTS):
                rows = pl.ds(k * 128, 128)
                left.append(jnp.concatenate([low_ref[rows], high_ref[rows]], axis=1).astype(BF))
            left = jnp.concatenate(left, axis=0)
            keep = (lane >= s * SIDE) & (lane < (s + 1) * SIDE)
            for t in range(4):
                right = jnp.where(keep, ytab_ref[t], jnp.zeros((256, 256), BF))
                term = jnp.dot(left, right, preferred_element_type=F32)
                acc[t] = term if acc[t] is None else acc[t] + term
        for x in range(2):
            for tile in range(2):
                c = acc[2 * x][tile * 128 : (tile + 1) * 128]
                s = acc[2 * x + 1][tile * 128 : (tile + 1) * 128]
                lanes = pl.ds(tile * 256, 256)
                out_ref[x * 128 : x * 128 + PAIRS, lanes] = (c[:PAIRS] + s[PAIRS:]).astype(BF)
                out_ref[x * 128 + PAIRS : (x + 1) * 128, lanes] = (c[PAIRS:] - s[:PAIRS]).astype(BF)


def z_transform(where, val_pieces, again, cond_wire, ytab):
    single = z_table()
    table = np.zeros((4 * KROWS, 768), single.dtype)
    table[: 2 * KROWS, :384] = single
    table[2 * KROWS :, 384:] = single
    return pl.pallas_call(
        z_kernel,
        out_shape=jax.ShapeDtypeStruct((256, 512), BF),
        grid_spec=pltpu.PrefetchScalarGridSpec(
            num_scalar_prefetch=1,
            grid=(PARTS // CONDS,),
            in_specs=[
                *[pl.BlockSpec((2, WIRE, 128), lambda c, o: (0, 0, 0))] * (CHIPS + 1),
                pl.BlockSpec((CONDS, WIRE, 128), lambda c, o: (c, 0, 0)),
                pl.BlockSpec((4 * KROWS, 768), lambda c, o: (0, 0)),
                pl.BlockSpec((4, 256, 256), lambda c, o: (0, 0, 0)),
            ],
            out_specs=pl.BlockSpec((256, 512), lambda c, o: (0, 0)),
            scratch_shapes=[
                pltpu.VMEM((2, 2, WIRE, 128), BF),
                pltpu.VMEM((4, 2, ROWS, 128), F32),
                pltpu.VMEM((4, ROWS, 128), F32),
                pltpu.VMEM((KROWS * 128, 128), F32),
                pltpu.VMEM((KROWS * 128, 128), F32),
            ],
        ),
        compiler_params=pltpu.CompilerParams(vmem_limit_bytes=28 * 2**20),
        name="ztransform",
    )(where, *val_pieces, again, cond_wire, in_hbm(jnp.asarray(table)), ytab)


def g_kernel(parity_ref, plane_ref, index_ref, phase_ref, out_ref):
    row = lax.broadcasted_iota(jnp.int32, (512, GCHUNK), 0)
    for chunk in range(out_ref.shape[0]):
        pick = jnp.where(row == index_ref[chunk, 0], 1.0, 0.0).astype(BF)
        at = jnp.dot(plane_ref[...], pick, preferred_element_type=F32)
        real = jnp.zeros((PAIRS, GCHUNK), F32)
        imag = jnp.zeros((PAIRS, GCHUNK), F32)
        for x in range(2):
            c = phase_ref[chunk, 0, 2 * x : 2 * x + 1]
            s = phase_ref[chunk, 0, 2 * x + 1 : 2 * x + 2]
            re = at[x * 128 : x * 128 + PAIRS]
            im = at[x * 128 + PAIRS : (x + 1) * 128]
            real = real + re * c + im * s
            imag = imag + im * c - re * s
        out_ref[chunk, :PAIRS] = real.astype(out_ref.dtype)
        out_ref[chunk, PAIRS:] = imag.astype(out_ref.dtype)


def g_elements(parity, plane, index, phase, dtype):
    chips = index.shape[0]
    return pl.pallas_call(
        g_kernel,
        out_shape=jax.ShapeDtypeStruct((chips, 128, GCHUNK), dtype),
        grid_spec=pltpu.PrefetchScalarGridSpec(
            num_scalar_prefetch=1,
            grid=(1,),
            in_specs=[
                pl.BlockSpec((256, 512), lambda i, k: (0, 0)),
                pl.BlockSpec((chips, 1, 1, GCHUNK), lambda i, k: (0, k[0], 0, 0)),
                pl.BlockSpec((chips, 1, 4, GCHUNK), lambda i, k: (0, k[0], 0, 0)),
            ],
            out_specs=pl.BlockSpec((chips, 128, GCHUNK), lambda i, k: (0, 0, 0)),
        ),
        compiler_params=pltpu.CompilerParams(vmem_limit_bytes=10 * 2**20),
        cost_estimate=pl.CostEstimate(flops=2 * 10**9, transcendentals=0, bytes_accessed=12_000_000),
        name="gelements",
    )(parity, plane, index, phase)


def chi_kernel(core_ref, mine_ref, other_ref, column_ref, weight_ref, out_ref):
    real = column_ref[...].astype(F32) * weight_ref[...]
    imag = jnp.concatenate([-real[PAIRS:], real[:PAIRS]], axis=0)
    sides = []
    for side in (real, imag):
        top = side.astype(BF)
        sides.append((top, (side - top.astype(F32)).astype(BF)))
    for half, rows in ((core_ref[0], mine_ref[...]), (1 - core_ref[0], other_ref[...])):
        at = pl.ds(pl.multiple_of(half * GCHUNK, GCHUNK), GCHUNK)
        for part in range(2):
            total = None
            for piece in sides[part]:
                term = lax.dot_general(rows, piece, (((0,), (0,)), ((), ())), preferred_element_type=F32)
                total = term if total is None else total + term
            out_ref[part, at, :] = total


def chi_block(core, mine, other, column, weight):
    spec = pl.BlockSpec((128, GCHUNK), lambda i, k: (0, 0))
    return pl.pallas_call(
        chi_kernel,
        out_shape=jax.ShapeDtypeStruct((2, 2 * GCHUNK, GCHUNK), F32),
        grid_spec=pltpu.PrefetchScalarGridSpec(
            num_scalar_prefetch=1,
            grid=(1,),
            in_specs=[spec, spec, spec, pl.BlockSpec((128, 1), lambda i, k: (0, 0))],
            out_specs=pl.BlockSpec((2, 2 * GCHUNK, GCHUNK), lambda i, k: (0, 0, 0)),
        ),
        compiler_params=pltpu.CompilerParams(vmem_limit_bytes=8 * 2**20),
        name="chi",
    )(core, mine, other, column, weight)


def shards(valence, conduction, val_energy, cond_energy, cond_band, owners, gvectors):
    grid_pos = lax.axis_index("grid")
    band_pos = lax.axis_index("band")
    x_local = valence.shape[2]
    n_grid = lax.axis_size("grid")

    rows_all = x_local * LENGTH
    cond_wire = pack_cond(in_hbm(conduction.reshape(2, rows_all, LENGTH)), cond_band)
    cond_wire, core = lax.optimization_barrier((cond_wire, band_pos & 1))
    cond_wire = lax.all_to_all(cond_wire, "band", 0, 0, tiled=True)

    first, second = owners[0], owners[1]
    chip = band_pos >> 1
    siblings = [(b, b ^ 1) for b in range(PARTS)]
    bands = in_hbm(valence.reshape(2, 2, CHIPS, 2, ROWS, LENGTH))
    place = jnp.stack([core, chip])
    sibling = [lax.ppermute(pack_give(bands, place, half), "band", siblings) for half in range(2)]
    here = (first >> 1) == chip
    own = jnp.where(here, first == band_pos, second == band_pos)
    place = jnp.stack([core, chip, own.astype(jnp.int32)])
    pieces = send_to_chips(pack_choice(bands, place, sibling))
    ytab = plane_tables(band_pos & 3)

    def exchange_again(operands):
        bands, sibling = operands
        place = jnp.stack([core, chip, (second == band_pos).astype(jnp.int32)])
        again = send_to_chips(pack_choice(bands, place, sibling))
        found = again[0]
        for s in range(1, CHIPS):
            found = jnp.where((second >> 1) == chip ^ s, again[s], found)
        return found

    def nothing_more(operands):
        return jnp.zeros((2, WIRE, 128), BF)

    both = (first != second) & ((first >> 1) == (second >> 1))
    cond_wire, both, pieces = lax.optimization_barrier((cond_wire, both, pieces))
    again = lax.cond(both, exchange_again, nothing_more, (bands, sibling))
    where = jnp.stack([(first >> 1) ^ chip, (second >> 1) ^ chip, both.astype(jnp.int32)])
    plane = z_transform(where, pieces, again, in_hbm(cond_wire), ytab)

    numbers = cond_wire[:, WIRE - 1, 127].astype(jnp.int32)
    order = jnp.arange(cond_energy.shape[0], dtype=jnp.int32)
    levels = jnp.sum(jnp.where(numbers[:, None] == order[None, :], cond_energy[None, :], 0.0), axis=1)
    val_index = (owners[:, None] * 2 + jnp.arange(2, dtype=jnp.int32)[None, :]).reshape(4)
    val_levels = val_energy[val_index]
    weight = (2.0 / (PAIRS * (val_levels[None, :] - levels[:, None]))).reshape(PAIRS)

    signed = (gvectors + GMAX) % LENGTH
    slot = jnp.where(signed[2] < SLOTS, signed[2] * SIDE, 256 + (signed[2] - SLOTS) * SIDE)
    index = (slot + signed[1]).reshape(PARTS // 2, 2, 1, GCHUNK)
    x_first = grid_pos * x_local + 5 * (band_pos >> 2) + (band_pos & 3)
    norm = float(LENGTH) ** (-1.5)
    waves = []
    for x in range(2):
        angle = (gvectors[0] * (x_first + x) % LENGTH).astype(F32) * (2.0 * math.pi / LENGTH)
        waves += [jnp.cos(angle), jnp.sin(angle)]
    phase = jnp.stack(waves).astype(BF).astype(F32) * norm
    phase = phase.reshape(4, PARTS, GCHUNK).transpose(1, 0, 2).reshape(PARTS // 2, 2, 4, GCHUNK)

    core = band_pos & 1
    away = g_elements((1 - core)[None], plane, index, phase, BF)
    come = lax.ppermute(away, "band", siblings)
    keep = g_elements(core[None], plane, index, phase, F32)
    parts = (keep + come.astype(F32)).astype(BF)
    parts = lax.all_to_all(parts, "grid", 0, 0, tiled=True)
    block = jnp.sum(parts.astype(F32), axis=0)
    block = block + lax.ppermute(block.astype(BF), "band", [(b, b ^ 2) for b in range(PARTS)]).astype(F32)
    narrow = block.astype(BF)
    for turn in (4, 8, 12):
        step = [(b, (b + turn) % PARTS) for b in range(PARTS)]
        block = block + lax.ppermute(narrow, "band", step).astype(F32)

    narrow = block.astype(BF)
    far = []
    for b in range(PARTS):
        for g in range(n_grid):
            x, zl, y, zh = b >> 2, (b >> 1) & 1, g >> 1, g & 1
            to_x, to_zl, to_y, to_zh = y, zh, (2 * y + 2 - x) % 4, zl
            to_b = to_x * 4 + to_zl * 2 + (b & 1)
            far.append((b * n_grid + g, to_b * n_grid + to_y * 2 + to_zh))
    column = lax.ppermute(narrow, ("band", "grid"), far)
    other = lax.ppermute(narrow, "band", siblings)
    return chi_block(core[None], narrow, other, column, jnp.concatenate([weight, weight])[:, None])


def solution(mesh):
    return jax.shard_map(
        shards,
        mesh=mesh,
        in_specs=(
            P("band", None, "grid", None, None),
            P("band", None, "grid", None, None),
            P(),
            P(),
            P("band"),
            P(),
            P(),
        ),
        out_specs=P(None, "grid", "band"),
        check_vma=False,
    )
```

```python
import functools
import math

import jax
import jax.numpy as jnp
import numpy as np
from jax import lax
from jax.experimental import pallas as pl
from jax.experimental.pallas import tpu as pltpu
from jax.sharding import PartitionSpec as P

LENGTH = 160
GMAX = 10
SIDE = 2 * GMAX + 1
PARTS = 16
ROWS = 200
TAIL = 104
WIRE = 2 * ROWS + TAIL
PAIRS = 64
PACK = 8
CHIPS = 8
GIVE = 4
CONDS = 4
SLOTS = 12
KROWS = 24
GCHUNK = 256
BF = jnp.bfloat16
F32 = jnp.float32


def host_tables():
    freq = (np.arange(SIDE) - GMAX) % LENGTH
    pos = np.arange(LENGTH)
    angle = ((freq[:, None] * pos[None, :]) % LENGTH).astype(np.float32) * np.float32(2.0 * math.pi / LENGTH)
    rnd = lambda a: a.astype(np.float32).astype(jnp.bfloat16).astype(np.float32)
    return rnd(np.cos(angle)), rnd(np.sin(angle))


def z_table():
    cos, sin = host_tables()
    out = np.zeros((2 * KROWS, 384), np.float32)
    cm, sm, ct, st = cos[:, :128], sin[:, :128], cos[:, 128:], sin[:, 128:]
    out[:SIDE] = np.concatenate([cm, sm, ct, ct, st, -st], axis=1)
    out[KROWS : KROWS + SIDE] = np.concatenate([-sm, cm, -st, -st, ct, -ct], axis=1)
    return out.astype(jnp.bfloat16)


def y_tables():
    cos, sin = host_tables()
    out = np.zeros((4, 256, 4, 32), np.float32)
    for shift in range(4):
        for row in range(ROWS):
            flat = 40 * shift + row
            x, y = divmod(flat, LENGTH)
            out[shift, row, 2 * x, :SIDE] = cos[:, y]
            out[shift, row, 2 * x + 1, :SIDE] = sin[:, y]
    return out.reshape(4, 256, 128).astype(jnp.bfloat16)


def in_hbm(array):
    return pltpu.with_memory_space_constraint(array, pltpu.HBM)


def pack_band(src, out, fill):
    real, imag = src[0], src[1]
    out[0:ROWS] = real[:, :128]
    out[ROWS : 2 * ROWS] = imag[:, :128]
    tail = jnp.concatenate([real[:, 128:].astype(F32), imag[:, 128:].astype(F32)], axis=1)
    low = tail[:TAIL]
    high = jnp.concatenate([tail[TAIL:], jnp.full((2 * TAIL - ROWS, 64), 1.0, F32) * fill], axis=0)
    out[2 * ROWS :] = jnp.concatenate([low, high], axis=1).astype(BF)


def pack_cond_kernel(number_ref, cond_ref, out_ref):
    for t in range(PACK):
        rows = pl.ds(t * ROWS, ROWS)
        pack_band(cond_ref.at[:, rows], out_ref.at[t], number_ref[0].astype(F32))


def pack_cond(conduction, number):
    return pl.pallas_call(
        pack_cond_kernel,
        out_shape=pltpu.HBM((PARTS, WIRE, 128), BF),
        grid_spec=pltpu.PrefetchScalarGridSpec(
            num_scalar_prefetch=1,
            grid=(PARTS // PACK,),
            in_specs=[pl.BlockSpec((2, PACK * ROWS, LENGTH), lambda t, n: (0, t, 0))],
            out_specs=pl.BlockSpec((PACK, WIRE, 128), lambda t, n: (t, 0, 0)),
        ),
        cost_estimate=pl.CostEstimate(flops=0, transcendentals=0, bytes_accessed=6_000_000),
        compiler_params=pltpu.CompilerParams(vmem_limit_bytes=14 * 2**20),
        name="packcond",
    )(number, conduction)


def pack_give_kernel(place_ref, val_ref, out_ref):
    for s in range(GIVE):
        for band in range(2):
            pack_band(val_ref.at[band, :, s ^ (place_ref[1] & (GIVE - 1)), 0], out_ref.at[s, band], 0.0)


def pack_give(valence, place, t):
    block = (2, 2, GIVE, 1, ROWS, LENGTH)
    return pl.pallas_call(
        pack_give_kernel,
        out_shape=jax.ShapeDtypeStruct((GIVE, 2, WIRE, 128), BF),
        grid_spec=pltpu.PrefetchScalarGridSpec(
            num_scalar_prefetch=1,
            grid=(1,),
            in_specs=[pl.BlockSpec(block, lambda i, p: (0, 0, t ^ (p[1] // GIVE), 1 - p[0], 0, 0))],
            out_specs=pl.BlockSpec((GIVE, 2, WIRE, 128), lambda i, p: (0, 0, 0, 0)),
        ),
        cost_estimate=pl.CostEstimate(flops=0, transcendentals=0, bytes_accessed=3_000_000),
        compiler_params=pltpu.CompilerParams(vmem_limit_bytes=16 * 2**20),
        name="packgive",
    )(place, valence)


def pack_choice_kernel(place_ref, val_ref, *refs):
    others, outs = refs[: CHIPS // GIVE], refs[CHIPS // GIVE :]

    @pl.when(place_ref[2] == 1)
    def _():
        for s in range(CHIPS):
            for band in range(2):
                pack_band(val_ref.at[band, :, s ^ place_ref[1], 0], outs[s].at[band], 0.0)

    @pl.when(place_ref[2] == 0)
    def _():
        for s in range(CHIPS):
            outs[s][...] = others[s // GIVE][s % GIVE]


def pack_choice(valence, place, others):
    piece = (2, WIRE, 128)
    return pl.pallas_call(
        pack_choice_kernel,
        out_shape=[jax.ShapeDtypeStruct(piece, BF)] * CHIPS,
        grid_spec=pltpu.PrefetchScalarGridSpec(
            num_scalar_prefetch=1,
            grid=(1,),
            in_specs=[pl.BlockSpec((2, 2, CHIPS, 1, ROWS, LENGTH), lambda i, p: (0, 0, 0, p[0], 0, 0))]
            + [pl.BlockSpec((GIVE, 2, WIRE, 128), lambda i, p: (0, 0, 0, 0))] * (CHIPS // GIVE),
            out_specs=[pl.BlockSpec(piece, lambda i, p: (0, 0, 0))] * CHIPS,
        ),
        cost_estimate=pl.CostEstimate(flops=0, transcendentals=0, bytes_accessed=8_000_000),
        compiler_params=pltpu.CompilerParams(vmem_limit_bytes=28 * 2**20),
        name="packchoice",
    )(place, valence, *others)


def send_to_chips(pieces):
    got = [pieces[0]]
    for s in range(1, CHIPS):
        got.append(lax.ppermute(pieces[s], "band", [(b, b ^ (2 * s)) for b in range(PARTS)]))
    return got


def unpack_tail(tail):
    return jnp.concatenate([tail[:, :64], tail[: ROWS - TAIL, 64:]], axis=0)


def plane_tables(shift):
    tab = lax.dynamic_index_in_dim(jnp.asarray(y_tables()), shift, 0, keepdims=False)
    tab = tab.reshape(256, 4, 32)[:, :, :SIDE].transpose(1, 0, 2)
    return jnp.pad(jnp.tile(tab, (1, 1, SLOTS)), ((0, 0), (0, 0), (0, 256 - SLOTS * SIDE)))


def z_kernel(where_ref, *refs):
    val_refs, again_ref = refs[:CHIPS], refs[CHIPS]
    cond_ref, table_ref, ytab_ref, out_ref, raw_ref, val_main, val_tail, low_ref, high_ref = refs[CHIPS + 1 :]
    step = pl.program_id(0)

    for s in range(CHIPS):
        for r in range(2):

            @pl.when((step == 0) & (where_ref[r] == s))
            def _():
                raw_ref[r] = val_refs[s][...]

    @pl.when((step == 0) & (where_ref[2] == 1))
    def _():
        raw_ref[1] = again_ref[...]

    @pl.when(step == 0)
    def _():
        for i in range(4):
            src = raw_ref.at[i // 2, i % 2]
            val_main[i, 0] = src[0:ROWS].astype(F32)
            val_main[i, 1] = src[ROWS : 2 * ROWS].astype(F32)
            both = unpack_tail(src[2 * ROWS :].astype(F32))
            val_tail[i] = jnp.concatenate([both, both], axis=1)
        high_ref[...] = jnp.zeros_like(high_ref)

    @pl.loop(0, CONDS, unroll=CONDS)
    def _(c):
        cre = cond_ref[c, 0:ROWS].astype(F32)
        cim = cond_ref[c, ROWS : 2 * ROWS].astype(F32)
        both = unpack_tail(cond_ref[c, 2 * ROWS :].astype(F32))
        ctail = jnp.concatenate([both, both[:, 32:], both[:, :32]], axis=1)
        first = (step * CONDS + c) * 4
        for i in range(0, 4, 2):
            density = []
            for j in (i, i + 1):
                vre, vim = val_main[j, 0], val_main[j, 1]
                density += [vre * cre + vim * cim, vre * cim - vim * cre, val_tail[j] * ctail]
            density = jnp.concatenate(density, axis=1).astype(BF)
            along = lax.dot_general(
                table_ref[...], density, (((1,), (1,)), ((), ())), preferred_element_type=F32
            )
            for j in range(2):
                for part in range(2):
                    start = part * PAIRS + first + i + j
                    at = (2 * j + part) * KROWS
                    piece = along[at : at + KROWS]
                    low_ref[pl.ds(start, KROWS, stride=128), :] = piece[:, :128]
                    high_ref[pl.ds(start, KROWS, stride=128), 0 : ROWS - 128] = piece[:, 128:]

    @pl.when(step == pl.num_programs(0) - 1)
    def _():
        lane = lax.broadcasted_iota(jnp.int32, (256, 256), 1)
        acc = [None] * 4
        for s in range(SLOTS):
            left = []
            for k in (s, s + SLOTS):
                rows = pl.ds(k * 128, 128)
                left.append(jnp.concatenate([low_ref[rows], high_ref[rows]], axis=1).astype(BF))
            left = jnp.concatenate(left, axis=0)
            keep = (lane >= s * SIDE) & (lane < (s + 1) * SIDE)
            for t in range(4):
                right = jnp.where(keep, ytab_ref[t], jnp.zeros((256, 256), BF))
                term = jnp.dot(left, right, preferred_element_type=F32)
                acc[t] = term if acc[t] is None else acc[t] + term
        for x in range(2):
            for tile in range(2):
                c = acc[2 * x][tile * 128 : (tile + 1) * 128]
                s = acc[2 * x + 1][tile * 128 : (tile + 1) * 128]
                lanes = pl.ds(tile * 256, 256)
                out_ref[x * 128 : x * 128 + PAIRS, lanes] = (c[:PAIRS] + s[PAIRS:]).astype(BF)
                out_ref[x * 128 + PAIRS : (x + 1) * 128, lanes] = (c[PAIRS:] - s[:PAIRS]).astype(BF)


def z_transform(where, val_pieces, again, cond_wire, ytab):
    single = z_table()
    table = np.zeros((4 * KROWS, 768), single.dtype)
    table[: 2 * KROWS, :384] = single
    table[2 * KROWS :, 384:] = single
    return pl.pallas_call(
        z_kernel,
        out_shape=jax.ShapeDtypeStruct((256, 512), BF),
        grid_spec=pltpu.PrefetchScalarGridSpec(
            num_scalar_prefetch=1,
            grid=(PARTS // CONDS,),
            in_specs=[
                *[pl.BlockSpec((2, WIRE, 128), lambda c, o: (0, 0, 0))] * (CHIPS + 1),
                pl.BlockSpec((CONDS, WIRE, 128), lambda c, o: (c, 0, 0)),
                pl.BlockSpec((4 * KROWS, 768), lambda c, o: (0, 0)),
                pl.BlockSpec((4, 256, 256), lambda c, o: (0, 0, 0)),
            ],
            out_specs=pl.BlockSpec((256, 512), lambda c, o: (0, 0)),
            scratch_shapes=[
                pltpu.VMEM((2, 2, WIRE, 128), BF),
                pltpu.VMEM((4, 2, ROWS, 128), F32),
                pltpu.VMEM((4, ROWS, 128), F32),
                pltpu.VMEM((KROWS * 128, 128), F32),
                pltpu.VMEM((KROWS * 128, 128), F32),
            ],
        ),
        compiler_params=pltpu.CompilerParams(vmem_limit_bytes=28 * 2**20),
        name="ztransform",
    )(where, *val_pieces, again, cond_wire, in_hbm(jnp.asarray(table)), ytab)


def g_kernel(parity_ref, plane_ref, index_ref, phase_ref, out_ref):
    row = lax.broadcasted_iota(jnp.int32, (512, GCHUNK), 0)
    for s in range(out_ref.shape[0]):
        chunk = s ^ parity_ref[1]
        pick = jnp.where(row == index_ref[chunk, 0], 1.0, 0.0).astype(BF)
        at = jnp.dot(plane_ref[...], pick, preferred_element_type=F32)
        real = jnp.zeros((PAIRS, GCHUNK), F32)
        imag = jnp.zeros((PAIRS, GCHUNK), F32)
        for x in range(2):
            cos = phase_ref[chunk, 0, 2 * x : 2 * x + 1]
            sin = phase_ref[chunk, 0, 2 * x + 1 : 2 * x + 2]
            re = at[x * 128 : x * 128 + PAIRS]
            im = at[x * 128 + PAIRS : (x + 1) * 128]
            real = real + re * cos + im * sin
            imag = imag + im * cos - re * sin
        out_ref[s, :PAIRS] = real.astype(out_ref.dtype)
        out_ref[s, PAIRS:] = imag.astype(out_ref.dtype)


def g_elements(parity, plane, index, phase, dtype):
    chips = index.shape[0]
    return pl.pallas_call(
        g_kernel,
        out_shape=jax.ShapeDtypeStruct((chips, 128, GCHUNK), dtype),
        grid_spec=pltpu.PrefetchScalarGridSpec(
            num_scalar_prefetch=1,
            grid=(1,),
            in_specs=[
                pl.BlockSpec((256, 512), lambda i, k: (0, 0)),
                pl.BlockSpec((chips, 1, 1, GCHUNK), lambda i, k: (0, k[0], 0, 0)),
                pl.BlockSpec((chips, 1, 4, GCHUNK), lambda i, k: (0, k[0], 0, 0)),
            ],
            out_specs=pl.BlockSpec((chips, 128, GCHUNK), lambda i, k: (0, 0, 0)),
        ),
        compiler_params=pltpu.CompilerParams(vmem_limit_bytes=10 * 2**20),
        cost_estimate=pl.CostEstimate(flops=2 * 10**9, transcendentals=0, bytes_accessed=12_000_000),
        name="gelements",
    )(parity, plane, index, phase)


def merge_kernel(keep_ref, come_ref, *out_refs):
    for s, out_ref in enumerate(out_refs):
        out_ref[...] = (keep_ref[s] + come_ref[s].astype(F32)).astype(BF)


def merge(keep, come):
    blocks = keep.shape[0]
    whole = pl.BlockSpec((blocks, 128, GCHUNK), lambda i: (0, 0, 0))
    return pl.pallas_call(
        merge_kernel,
        out_shape=[jax.ShapeDtypeStruct((128, GCHUNK), BF)] * blocks,
        grid=(1,),
        in_specs=[whole, whole],
        out_specs=[pl.BlockSpec((128, GCHUNK), lambda i: (0, 0))] * blocks,
        compiler_params=pltpu.CompilerParams(vmem_limit_bytes=10 * 2**20),
        name="merge",
    )(keep, come)


def chi_kernel(core_ref, mine_ref, other_ref, column_ref, weight_ref, out_ref):
    real = column_ref[...].astype(F32) * weight_ref[...]
    imag = jnp.concatenate([-real[PAIRS:], real[:PAIRS]], axis=0)
    sides = []
    for side in (real, imag):
        top = side.astype(BF)
        sides.append((top, (side - top.astype(F32)).astype(BF)))
    for half, rows in ((core_ref[0], mine_ref[...]), (1 - core_ref[0], other_ref[...])):
        at = pl.ds(pl.multiple_of(half * GCHUNK, GCHUNK), GCHUNK)
        for part in range(2):
            total = None
            for piece in sides[part]:
                term = lax.dot_general(rows, piece, (((0,), (0,)), ((), ())), preferred_element_type=F32)
                total = term if total is None else total + term
            out_ref[part, at, :] = total


def chi_block(core, mine, other, column, weight):
    spec = pl.BlockSpec((128, GCHUNK), lambda i, k: (0, 0))
    return pl.pallas_call(
        chi_kernel,
        out_shape=jax.ShapeDtypeStruct((2, 2 * GCHUNK, GCHUNK), F32),
        grid_spec=pltpu.PrefetchScalarGridSpec(
            num_scalar_prefetch=1,
            grid=(1,),
            in_specs=[spec, spec, spec, pl.BlockSpec((128, 1), lambda i, k: (0, 0))],
            out_specs=pl.BlockSpec((2, 2 * GCHUNK, GCHUNK), lambda i, k: (0, 0, 0)),
        ),
        compiler_params=pltpu.CompilerParams(vmem_limit_bytes=8 * 2**20),
        name="chi",
    )(core, mine, other, column, weight)


def shards(valence, conduction, val_energy, cond_energy, cond_band, owners, gvectors):
    grid_pos = lax.axis_index("grid")
    band_pos = lax.axis_index("band")
    x_local = valence.shape[2]
    n_grid = lax.axis_size("grid")

    rows_all = x_local * LENGTH
    cond_wire = pack_cond(in_hbm(conduction.reshape(2, rows_all, LENGTH)), cond_band)
    cond_wire, core = lax.optimization_barrier((cond_wire, band_pos & 1))
    cond_wire = lax.all_to_all(cond_wire, "band", 0, 0, tiled=True)

    first, second = owners[0], owners[1]
    chip = band_pos >> 1
    siblings = [(b, b ^ 1) for b in range(PARTS)]
    bands = in_hbm(valence.reshape(2, 2, CHIPS, 2, ROWS, LENGTH))
    place = jnp.stack([core, chip])
    sibling = [lax.ppermute(pack_give(bands, place, t), "band", siblings) for t in range(CHIPS // GIVE)]
    here = (first >> 1) == chip
    own = jnp.where(here, first == band_pos, second == band_pos)
    place = jnp.stack([core, chip, own.astype(jnp.int32)])
    pieces = send_to_chips(pack_choice(bands, place, sibling))
    ytab = plane_tables(band_pos & 3)

    def exchange_again(operands):
        bands, sibling = operands
        place = jnp.stack([core, chip, (second == band_pos).astype(jnp.int32)])
        again = send_to_chips(pack_choice(bands, place, sibling))
        found = again[0]
        for s in range(1, CHIPS):
            found = jnp.where((second >> 1) == chip ^ s, again[s], found)
        return found

    def nothing_more(operands):
        return jnp.zeros((2, WIRE, 128), BF)

    both = (first != second) & ((first >> 1) == (second >> 1))
    cond_wire, both, pieces = lax.optimization_barrier((cond_wire, both, pieces))
    again = lax.cond(both, exchange_again, nothing_more, (bands, sibling))
    where = jnp.stack([(first >> 1) ^ chip, (second >> 1) ^ chip, both.astype(jnp.int32)])
    plane = z_transform(where, pieces, again, in_hbm(cond_wire), ytab)

    numbers = cond_wire[:, WIRE - 1, 127].astype(jnp.int32)
    order = jnp.arange(cond_energy.shape[0], dtype=jnp.int32)
    levels = jnp.sum(jnp.where(numbers[:, None] == order[None, :], cond_energy[None, :], 0.0), axis=1)
    val_index = (owners[:, None] * 2 + jnp.arange(2, dtype=jnp.int32)[None, :]).reshape(4)
    val_levels = val_energy[val_index]
    weight = (2.0 / (PAIRS * (val_levels[None, :] - levels[:, None]))).reshape(PAIRS)

    signed = (gvectors + GMAX) % LENGTH
    slot = jnp.where(signed[2] < SLOTS, signed[2] * SIDE, 256 + (signed[2] - SLOTS) * SIDE)
    index = (slot + signed[1]).reshape(PARTS // 2, 2, 1, GCHUNK)
    x_first = grid_pos * x_local + 5 * (band_pos >> 2) + (band_pos & 3)
    norm = float(LENGTH) ** (-1.5)
    waves = []
    for x in range(2):
        angle = (gvectors[0] * (x_first + x) % LENGTH).astype(F32) * (2.0 * math.pi / LENGTH)
        waves += [jnp.cos(angle), jnp.sin(angle)]
    phase = jnp.stack(waves).astype(BF).astype(F32) * norm
    phase = phase.reshape(4, PARTS, GCHUNK).transpose(1, 0, 2).reshape(PARTS // 2, 2, 4, GCHUNK)

    core = band_pos & 1
    away = g_elements(jnp.stack([1 - core, grid_pos]), plane, index, phase, BF)
    come = lax.ppermute(away, "band", siblings)
    keep = g_elements(jnp.stack([core, grid_pos]), plane, index, phase, F32)
    parts = merge(keep, come)
    block = parts[0].astype(F32)
    for s in range(1, n_grid):
        block = block + lax.ppermute(parts[s], "grid", [(g, g ^ s) for g in range(n_grid)]).astype(F32)
    block = block + lax.ppermute(block.astype(BF), "band", [(b, b ^ 2) for b in range(PARTS)]).astype(F32)
    narrow = block.astype(BF)
    for turn in (4, 8, 12):
        step = [(b, (b + turn) % PARTS) for b in range(PARTS)]
        block = block + lax.ppermute(narrow, "band", step).astype(F32)

    narrow = block.astype(BF)
    far = []
    for b in range(PARTS):
        for g in range(n_grid):
            x, zl, y, zh = b >> 2, (b >> 1) & 1, g >> 1, g & 1
            to_x, to_zl, to_y, to_zh = y, zh, (2 * y + 2 - x) % 4, zl
            to_b = to_x * 4 + to_zl * 2 + (b & 1)
            far.append((b * n_grid + g, to_b * n_grid + to_y * 2 + to_zh))
    column = lax.ppermute(narrow, ("band", "grid"), far)
    other = lax.ppermute(narrow, "band", siblings)
    return chi_block(core[None], narrow, other, column, jnp.concatenate([weight, weight])[:, None])


def solution(mesh):
    return jax.shard_map(
        shards,
        mesh=mesh,
        in_specs=(
            P("band", None, "grid", None, None),
            P("band", None, "grid", None, None),
            P(),
            P(),
            P("band"),
            P(),
            P(),
        ),
        out_specs=P(None, "grid", "band"),
        check_vma=False,
    )
```

```python
import functools
import math

import jax
import jax.numpy as jnp
import numpy as np
from jax import lax
from jax.experimental import pallas as pl
from jax.experimental.pallas import tpu as pltpu
from jax.sharding import PartitionSpec as P

LENGTH = 160
GMAX = 10
SIDE = 2 * GMAX + 1
PARTS = 16
ROWS = 200
TAIL = 104
WIRE = 2 * ROWS + TAIL
PAIRS = 64
PACK = 8
CHIPS = 8
ORDER = (0, 2, 6, 4, 1, 3, 7, 5)
CONDS = 4
SLOTS = 12
KROWS = 24
GCHUNK = 256
BF = jnp.bfloat16
F32 = jnp.float32


def host_tables():
    freq = (np.arange(SIDE) - GMAX) % LENGTH
    pos = np.arange(LENGTH)
    angle = ((freq[:, None] * pos[None, :]) % LENGTH).astype(np.float32) * np.float32(2.0 * math.pi / LENGTH)
    rnd = lambda a: a.astype(np.float32).astype(jnp.bfloat16).astype(np.float32)
    return rnd(np.cos(angle)), rnd(np.sin(angle))


def z_table():
    cos, sin = host_tables()
    out = np.zeros((2 * KROWS, 384), np.float32)
    cm, sm, ct, st = cos[:, :128], sin[:, :128], cos[:, 128:], sin[:, 128:]
    out[:SIDE] = np.concatenate([cm, sm, ct, ct, st, -st], axis=1)
    out[KROWS : KROWS + SIDE] = np.concatenate([-sm, cm, -st, -st, ct, -ct], axis=1)
    return out.astype(jnp.bfloat16)


def y_tables():
    cos, sin = host_tables()
    out = np.zeros((4, 256, 4, 32), np.float32)
    for shift in range(4):
        for row in range(ROWS):
            flat = 40 * shift + row
            x, y = divmod(flat, LENGTH)
            out[shift, row, 2 * x, :SIDE] = cos[:, y]
            out[shift, row, 2 * x + 1, :SIDE] = sin[:, y]
    return out.reshape(4, 256, 128).astype(jnp.bfloat16)


def in_hbm(array):
    return pltpu.with_memory_space_constraint(array, pltpu.HBM)


def pack_band(src, out, fill):
    real, imag = src[0], src[1]
    out[0:ROWS] = real[:, :128]
    out[ROWS : 2 * ROWS] = imag[:, :128]
    tail = jnp.concatenate([real[:, 128:].astype(F32), imag[:, 128:].astype(F32)], axis=1)
    low = tail[:TAIL]
    high = jnp.concatenate([tail[TAIL:], jnp.full((2 * TAIL - ROWS, 64), 1.0, F32) * fill], axis=0)
    out[2 * ROWS :] = jnp.concatenate([low, high], axis=1).astype(BF)


def pack_cond_kernel(number_ref, cond_ref, out_ref):
    for t in range(PACK):
        rows = pl.ds(t * ROWS, ROWS)
        pack_band(cond_ref.at[:, rows], out_ref.at[t], number_ref[0].astype(F32))


def pack_cond(conduction, number):
    return pl.pallas_call(
        pack_cond_kernel,
        out_shape=pltpu.HBM((PARTS, WIRE, 128), BF),
        grid_spec=pltpu.PrefetchScalarGridSpec(
            num_scalar_prefetch=1,
            grid=(PARTS // PACK,),
            in_specs=[pl.BlockSpec((2, PACK * ROWS, LENGTH), lambda t, n: (0, t, 0))],
            out_specs=pl.BlockSpec((PACK, WIRE, 128), lambda t, n: (t, 0, 0)),
        ),
        cost_estimate=pl.CostEstimate(flops=0, transcendentals=0, bytes_accessed=6_000_000),
        compiler_params=pltpu.CompilerParams(vmem_limit_bytes=14 * 2**20),
        name="packcond",
    )(number, conduction)


def pack_give_kernel(place_ref, val_ref, out_ref):
    for s in range(CHIPS // 2):
        for band in range(2):
            pack_band(val_ref.at[band, :, s ^ (place_ref[1] & 3), 0], out_ref.at[s, band], 0.0)


def pack_give(valence, place, half):
    block = (2, 2, CHIPS // 2, 1, ROWS, LENGTH)
    return pl.pallas_call(
        pack_give_kernel,
        out_shape=jax.ShapeDtypeStruct((CHIPS // 2, 2, WIRE, 128), BF),
        grid_spec=pltpu.PrefetchScalarGridSpec(
            num_scalar_prefetch=1,
            grid=(1,),
            in_specs=[pl.BlockSpec(block, lambda i, p: (0, 0, half ^ (p[1] >> 2), 1 - p[0], 0, 0))],
            out_specs=pl.BlockSpec((CHIPS // 2, 2, WIRE, 128), lambda i, p: (0, 0, 0, 0)),
        ),
        cost_estimate=pl.CostEstimate(flops=0, transcendentals=0, bytes_accessed=3_000_000),
        compiler_params=pltpu.CompilerParams(vmem_limit_bytes=16 * 2**20),
        name="packgive",
    )(place, valence)


def pack_choice_kernel(place_ref, val_ref, *refs):
    others, outs = refs[:2], refs[2:]

    @pl.when(place_ref[2] == 1)
    def _():
        for s in range(CHIPS):
            for band in range(2):
                pack_band(val_ref.at[band, :, s ^ place_ref[1], 0], outs[s].at[band], 0.0)

    @pl.when(place_ref[2] == 0)
    def _():
        for s in range(CHIPS):
            outs[s][...] = others[s // 4][s % 4]


def pack_choice(valence, place, others):
    piece = (2, WIRE, 128)
    return pl.pallas_call(
        pack_choice_kernel,
        out_shape=[jax.ShapeDtypeStruct(piece, BF)] * CHIPS,
        grid_spec=pltpu.PrefetchScalarGridSpec(
            num_scalar_prefetch=1,
            grid=(1,),
            in_specs=[pl.BlockSpec((2, 2, CHIPS, 1, ROWS, LENGTH), lambda i, p: (0, 0, 0, p[0], 0, 0))]
            + [pl.BlockSpec((CHIPS // 2, 2, WIRE, 128), lambda i, p: (0, 0, 0, 0))] * 2,
            out_specs=[pl.BlockSpec(piece, lambda i, p: (0, 0, 0))] * CHIPS,
        ),
        cost_estimate=pl.CostEstimate(flops=0, transcendentals=0, bytes_accessed=8_000_000),
        compiler_params=pltpu.CompilerParams(vmem_limit_bytes=28 * 2**20),
        name="packchoice",
    )(place, valence, *others)


def send_to_chips(pieces):
    got = [pieces[0]]
    for s in ORDER[1:]:
        got.append(lax.ppermute(pieces[s], "band", [(b, b ^ (2 * s)) for b in range(PARTS)]))
    return got


def unpack_tail(tail):
    return jnp.concatenate([tail[:, :64], tail[: ROWS - TAIL, 64:]], axis=0)


def plane_tables(shift):
    tab = lax.dynamic_index_in_dim(jnp.asarray(y_tables()), shift, 0, keepdims=False)
    tab = tab.reshape(256, 4, 32)[:, :, :SIDE].transpose(1, 0, 2)
    return jnp.pad(jnp.tile(tab, (1, 1, SLOTS)), ((0, 0), (0, 0), (0, 256 - SLOTS * SIDE)))


def z_kernel(where_ref, *refs):
    val_refs, again_ref = refs[:CHIPS], refs[CHIPS]
    cond_ref, table_ref, ytab_ref, out_ref, raw_ref, val_main, val_tail, low_ref, high_ref = refs[CHIPS + 1 :]
    step = pl.program_id(0)

    for slot, s in enumerate(ORDER):
        for r in range(2):

            @pl.when((step == 0) & (where_ref[r] == s))
            def _():
                raw_ref[r] = val_refs[slot][...]

    @pl.when((step == 0) & (where_ref[2] == 1))
    def _():
        raw_ref[1] = again_ref[...]

    @pl.when(step == 0)
    def _():
        for i in range(4):
            src = raw_ref.at[i // 2, i % 2]
            val_main[i, 0] = src[0:ROWS].astype(F32)
            val_main[i, 1] = src[ROWS : 2 * ROWS].astype(F32)
            both = unpack_tail(src[2 * ROWS :].astype(F32))
            val_tail[i] = jnp.concatenate([both, both], axis=1)
        high_ref[...] = jnp.zeros_like(high_ref)

    @pl.loop(0, CONDS, unroll=CONDS)
    def _(c):
        cre = cond_ref[c, 0:ROWS].astype(F32)
        cim = cond_ref[c, ROWS : 2 * ROWS].astype(F32)
        both = unpack_tail(cond_ref[c, 2 * ROWS :].astype(F32))
        ctail = jnp.concatenate([both, both[:, 32:], both[:, :32]], axis=1)
        first = (step * CONDS + c) * 4
        for i in range(0, 4, 2):
            density = []
            for j in (i, i + 1):
                vre, vim = val_main[j, 0], val_main[j, 1]
                density += [vre * cre + vim * cim, vre * cim - vim * cre, val_tail[j] * ctail]
            density = jnp.concatenate(density, axis=1).astype(BF)
            along = lax.dot_general(
                table_ref[...], density, (((1,), (1,)), ((), ())), preferred_element_type=F32
            )
            for j in range(2):
                for part in range(2):
                    start = part * PAIRS + first + i + j
                    at = (2 * j + part) * KROWS
                    piece = along[at : at + KROWS]
                    low_ref[pl.ds(start, KROWS, stride=128), :] = piece[:, :128]
                    high_ref[pl.ds(start, KROWS, stride=128), 0 : ROWS - 128] = piece[:, 128:]

    @pl.when(step == pl.num_programs(0) - 1)
    def _():
        lane = lax.broadcasted_iota(jnp.int32, (256, 256), 1)
        acc = [None] * 4
        for s in range(SLOTS):
            left = []
            for k in (s, s + SLOTS):
                rows = pl.ds(k * 128, 128)
                left.append(jnp.concatenate([low_ref[rows], high_ref[rows]], axis=1).astype(BF))
            left = jnp.concatenate(left, axis=0)
            keep = (lane >= s * SIDE) & (lane < (s + 1) * SIDE)
            for t in range(4):
                right = jnp.where(keep, ytab_ref[t], jnp.zeros((256, 256), BF))
                term = jnp.dot(left, right, preferred_element_type=F32)
                acc[t] = term if acc[t] is None else acc[t] + term
        for x in range(2):
            for tile in range(2):
                c = acc[2 * x][tile * 128 : (tile + 1) * 128]
                s = acc[2 * x + 1][tile * 128 : (tile + 1) * 128]
                lanes = pl.ds(tile * 256, 256)
                out_ref[x * 128 : x * 128 + PAIRS, lanes] = (c[:PAIRS] + s[PAIRS:]).astype(BF)
                out_ref[x * 128 + PAIRS : (x + 1) * 128, lanes] = (c[PAIRS:] - s[:PAIRS]).astype(BF)


def z_transform(where, val_pieces, again, cond_wire, ytab):
    single = z_table()
    table = np.zeros((4 * KROWS, 768), single.dtype)
    table[: 2 * KROWS, :384] = single
    table[2 * KROWS :, 384:] = single
    return pl.pallas_call(
        z_kernel,
        out_shape=jax.ShapeDtypeStruct((256, 512), BF),
        grid_spec=pltpu.PrefetchScalarGridSpec(
            num_scalar_prefetch=1,
            grid=(PARTS // CONDS,),
            in_specs=[
                *[pl.BlockSpec((2, WIRE, 128), lambda c, o: (0, 0, 0))] * (CHIPS + 1),
                pl.BlockSpec((CONDS, WIRE, 128), lambda c, o: (c, 0, 0)),
                pl.BlockSpec((4 * KROWS, 768), lambda c, o: (0, 0)),
                pl.BlockSpec((4, 256, 256), lambda c, o: (0, 0, 0)),
            ],
            out_specs=pl.BlockSpec((256, 512), lambda c, o: (0, 0)),
            scratch_shapes=[
                pltpu.VMEM((2, 2, WIRE, 128), BF),
                pltpu.VMEM((4, 2, ROWS, 128), F32),
                pltpu.VMEM((4, ROWS, 128), F32),
                pltpu.VMEM((KROWS * 128, 128), F32),
                pltpu.VMEM((KROWS * 128, 128), F32),
            ],
        ),
        compiler_params=pltpu.CompilerParams(vmem_limit_bytes=28 * 2**20),
        name="ztransform",
    )(where, *val_pieces, again, cond_wire, in_hbm(jnp.asarray(table)), ytab)


def g_kernel(parity_ref, plane_ref, index_ref, phase_ref, out_ref):
    row = lax.broadcasted_iota(jnp.int32, (512, GCHUNK), 0)
    for chunk in range(out_ref.shape[0]):
        pick = jnp.where(row == index_ref[chunk, 0], 1.0, 0.0).astype(BF)
        at = jnp.dot(plane_ref[...], pick, preferred_element_type=F32)
        real = jnp.zeros((PAIRS, GCHUNK), F32)
        imag = jnp.zeros((PAIRS, GCHUNK), F32)
        for x in range(2):
            c = phase_ref[chunk, 0, 2 * x : 2 * x + 1]
            s = phase_ref[chunk, 0, 2 * x + 1 : 2 * x + 2]
            re = at[x * 128 : x * 128 + PAIRS]
            im = at[x * 128 + PAIRS : (x + 1) * 128]
            real = real + re * c + im * s
            imag = imag + im * c - re * s
        out_ref[chunk, :PAIRS] = real.astype(out_ref.dtype)
        out_ref[chunk, PAIRS:] = imag.astype(out_ref.dtype)


def g_elements(parity, plane, index, phase, dtype):
    chips = index.shape[0]
    return pl.pallas_call(
        g_kernel,
        out_shape=jax.ShapeDtypeStruct((chips, 128, GCHUNK), dtype),
        grid_spec=pltpu.PrefetchScalarGridSpec(
            num_scalar_prefetch=1,
            grid=(1,),
            in_specs=[
                pl.BlockSpec((256, 512), lambda i, k: (0, 0)),
                pl.BlockSpec((chips, 1, 1, GCHUNK), lambda i, k: (0, k[0], 0, 0)),
                pl.BlockSpec((chips, 1, 4, GCHUNK), lambda i, k: (0, k[0], 0, 0)),
            ],
            out_specs=pl.BlockSpec((chips, 128, GCHUNK), lambda i, k: (0, 0, 0)),
        ),
        compiler_params=pltpu.CompilerParams(vmem_limit_bytes=10 * 2**20),
        cost_estimate=pl.CostEstimate(flops=2 * 10**9, transcendentals=0, bytes_accessed=12_000_000),
        name="gelements",
    )(parity, plane, index, phase)


def chi_kernel(core_ref, mine_ref, other_ref, column_ref, weight_ref, out_ref):
    real = column_ref[...].astype(F32) * weight_ref[...]
    imag = jnp.concatenate([-real[PAIRS:], real[:PAIRS]], axis=0)
    sides = []
    for side in (real, imag):
        top = side.astype(BF)
        sides.append((top, (side - top.astype(F32)).astype(BF)))
    for half, rows in ((core_ref[0], mine_ref[...]), (1 - core_ref[0], other_ref[...])):
        at = pl.ds(pl.multiple_of(half * GCHUNK, GCHUNK), GCHUNK)
        for part in range(2):
            total = None
            for piece in sides[part]:
                term = lax.dot_general(rows, piece, (((0,), (0,)), ((), ())), preferred_element_type=F32)
                total = term if total is None else total + term
            out_ref[part, at, :] = total


def chi_block(core, mine, other, column, weight):
    spec = pl.BlockSpec((128, GCHUNK), lambda i, k: (0, 0))
    return pl.pallas_call(
        chi_kernel,
        out_shape=jax.ShapeDtypeStruct((2, 2 * GCHUNK, GCHUNK), F32),
        grid_spec=pltpu.PrefetchScalarGridSpec(
            num_scalar_prefetch=1,
            grid=(1,),
            in_specs=[spec, spec, spec, pl.BlockSpec((128, 1), lambda i, k: (0, 0))],
            out_specs=pl.BlockSpec((2, 2 * GCHUNK, GCHUNK), lambda i, k: (0, 0, 0)),
        ),
        compiler_params=pltpu.CompilerParams(vmem_limit_bytes=8 * 2**20),
        name="chi",
    )(core, mine, other, column, weight)


def shards(valence, conduction, val_energy, cond_energy, cond_band, owners, gvectors):
    grid_pos = lax.axis_index("grid")
    band_pos = lax.axis_index("band")
    x_local = valence.shape[2]
    n_grid = lax.axis_size("grid")

    rows_all = x_local * LENGTH
    cond_wire = pack_cond(in_hbm(conduction.reshape(2, rows_all, LENGTH)), cond_band)
    cond_wire, core = lax.optimization_barrier((cond_wire, band_pos & 1))
    cond_wire = lax.all_to_all(cond_wire, "band", 0, 0, tiled=True)

    first, second = owners[0], owners[1]
    chip = band_pos >> 1
    siblings = [(b, b ^ 1) for b in range(PARTS)]
    bands = in_hbm(valence.reshape(2, 2, CHIPS, 2, ROWS, LENGTH))
    place = jnp.stack([core, chip])
    sibling = [lax.ppermute(pack_give(bands, place, half), "band", siblings) for half in range(2)]
    here = (first >> 1) == chip
    own = jnp.where(here, first == band_pos, second == band_pos)
    place = jnp.stack([core, chip, own.astype(jnp.int32)])
    pieces = send_to_chips(pack_choice(bands, place, sibling))
    ytab = plane_tables(band_pos & 3)

    def exchange_again(operands):
        bands, sibling = operands
        place = jnp.stack([core, chip, (second == band_pos).astype(jnp.int32)])
        again = send_to_chips(pack_choice(bands, place, sibling))
        found = again[0]
        for slot, s in enumerate(ORDER[1:], 1):
            found = jnp.where((second >> 1) == chip ^ s, again[slot], found)
        return found

    def nothing_more(operands):
        return jnp.zeros((2, WIRE, 128), BF)

    both = (first != second) & ((first >> 1) == (second >> 1))
    cond_wire, both, pieces = lax.optimization_barrier((cond_wire, both, pieces))
    again = lax.cond(both, exchange_again, nothing_more, (bands, sibling))
    where = jnp.stack([(first >> 1) ^ chip, (second >> 1) ^ chip, both.astype(jnp.int32)])
    plane = z_transform(where, pieces, again, in_hbm(cond_wire), ytab)

    numbers = cond_wire[:, WIRE - 1, 127].astype(jnp.int32)
    order = jnp.arange(cond_energy.shape[0], dtype=jnp.int32)
    levels = jnp.sum(jnp.where(numbers[:, None] == order[None, :], cond_energy[None, :], 0.0), axis=1)
    val_index = (owners[:, None] * 2 + jnp.arange(2, dtype=jnp.int32)[None, :]).reshape(4)
    val_levels = val_energy[val_index]
    weight = (2.0 / (PAIRS * (val_levels[None, :] - levels[:, None]))).reshape(PAIRS)

    signed = (gvectors + GMAX) % LENGTH
    slot = jnp.where(signed[2] < SLOTS, signed[2] * SIDE, 256 + (signed[2] - SLOTS) * SIDE)
    index = (slot + signed[1]).reshape(PARTS // 2, 2, 1, GCHUNK)
    x_first = grid_pos * x_local + 5 * (band_pos >> 2) + (band_pos & 3)
    norm = float(LENGTH) ** (-1.5)
    waves = []
    for x in range(2):
        angle = (gvectors[0] * (x_first + x) % LENGTH).astype(F32) * (2.0 * math.pi / LENGTH)
        waves += [jnp.cos(angle), jnp.sin(angle)]
    phase = jnp.stack(waves).astype(BF).astype(F32) * norm
    phase = phase.reshape(4, PARTS, GCHUNK).transpose(1, 0, 2).reshape(PARTS // 2, 2, 4, GCHUNK)

    core = band_pos & 1
    away = g_elements((1 - core)[None], plane, index, phase, BF)
    come = lax.ppermute(away, "band", siblings)
    keep = g_elements(core[None], plane, index, phase, F32)
    parts = (keep + come.astype(F32)).astype(BF)
    parts = lax.all_to_all(parts, "grid", 0, 0, tiled=True)
    block = jnp.sum(parts.astype(F32), axis=0)
    block = block + lax.ppermute(block.astype(BF), "band", [(b, b ^ 2) for b in range(PARTS)]).astype(F32)
    narrow = block.astype(BF)
    for turn in (4, 8, 12):
        step = [(b, (b + turn) % PARTS) for b in range(PARTS)]
        block = block + lax.ppermute(narrow, "band", step).astype(F32)

    narrow = block.astype(BF)
    far = []
    for b in range(PARTS):
        for g in range(n_grid):
            x, zl, y, zh = b >> 2, (b >> 1) & 1, g >> 1, g & 1
            to_x, to_zl, to_y, to_zh = y, zh, (2 * y + 2 - x) % 4, zl
            to_b = to_x * 4 + to_zl * 2 + (b & 1)
            far.append((b * n_grid + g, to_b * n_grid + to_y * 2 + to_zh))
    column = lax.ppermute(narrow, ("band", "grid"), far)
    other = lax.ppermute(narrow, "band", siblings)
    return chi_block(core[None], narrow, other, column, jnp.concatenate([weight, weight])[:, None])


def solution(mesh):
    return jax.shard_map(
        shards,
        mesh=mesh,
        in_specs=(
            P("band", None, "grid", None, None),
            P("band", None, "grid", None, None),
            P(),
            P(),
            P("band"),
            P(),
            P(),
        ),
        out_specs=P(None, "grid", "band"),
        check_vma=False,
    )
```

```python
import functools
import math

import jax
import jax.numpy as jnp
import numpy as np
from jax import lax
from jax.experimental import pallas as pl
from jax.experimental.pallas import tpu as pltpu
from jax.sharding import PartitionSpec as P

LENGTH = 160
GMAX = 10
SIDE = 2 * GMAX + 1
PARTS = 16
ROWS = 200
TAIL = 104
WIRE = 2 * ROWS + TAIL
PAIRS = 64
PACK = 8
CHIPS = 8
ORDER = (0, 2, 6, 4, 1, 3, 7, 5)
CONDS = 4
SLOTS = 12
KROWS = 24
GCHUNK = 256
BF = jnp.bfloat16
F32 = jnp.float32


def host_tables():
    freq = (np.arange(SIDE) - GMAX) % LENGTH
    pos = np.arange(LENGTH)
    angle = ((freq[:, None] * pos[None, :]) % LENGTH).astype(np.float32) * np.float32(2.0 * math.pi / LENGTH)
    rnd = lambda a: a.astype(np.float32).astype(jnp.bfloat16).astype(np.float32)
    return rnd(np.cos(angle)), rnd(np.sin(angle))


def z_table():
    cos, sin = host_tables()
    out = np.zeros((2 * KROWS, 384), np.float32)
    cm, sm, ct, st = cos[:, :128], sin[:, :128], cos[:, 128:], sin[:, 128:]
    out[:SIDE] = np.concatenate([cm, sm, ct, ct, st, -st], axis=1)
    out[KROWS : KROWS + SIDE] = np.concatenate([-sm, cm, -st, -st, ct, -ct], axis=1)
    return out.astype(jnp.bfloat16)


def y_tables():
    cos, sin = host_tables()
    out = np.zeros((4, 256, 4, 32), np.float32)
    for shift in range(4):
        for row in range(ROWS):
            flat = 40 * shift + row
            x, y = divmod(flat, LENGTH)
            out[shift, row, 2 * x, :SIDE] = cos[:, y]
            out[shift, row, 2 * x + 1, :SIDE] = sin[:, y]
    return out.reshape(4, 256, 128).astype(jnp.bfloat16)


def in_hbm(array):
    return pltpu.with_memory_space_constraint(array, pltpu.HBM)


def pack_band(src, out, fill):
    real, imag = src[0], src[1]
    out[0:ROWS] = real[:, :128]
    out[ROWS : 2 * ROWS] = imag[:, :128]
    tail = jnp.concatenate([real[:, 128:].astype(F32), imag[:, 128:].astype(F32)], axis=1)
    low = tail[:TAIL]
    high = jnp.concatenate([tail[TAIL:], jnp.full((2 * TAIL - ROWS, 64), 1.0, F32) * fill], axis=0)
    out[2 * ROWS :] = jnp.concatenate([low, high], axis=1).astype(BF)


def pack_cond_kernel(number_ref, cond_ref, out_ref):
    for t in range(PACK):
        rows = pl.ds(t * ROWS, ROWS)
        pack_band(cond_ref.at[:, rows], out_ref.at[t], number_ref[0].astype(F32))


def pack_cond(conduction, number):
    return pl.pallas_call(
        pack_cond_kernel,
        out_shape=pltpu.HBM((PARTS, WIRE, 128), BF),
        grid_spec=pltpu.PrefetchScalarGridSpec(
            num_scalar_prefetch=1,
            grid=(PARTS // PACK,),
            in_specs=[pl.BlockSpec((2, PACK * ROWS, LENGTH), lambda t, n: (0, t, 0))],
            out_specs=pl.BlockSpec((PACK, WIRE, 128), lambda t, n: (t, 0, 0)),
        ),
        cost_estimate=pl.CostEstimate(flops=0, transcendentals=0, bytes_accessed=6_000_000),
        compiler_params=pltpu.CompilerParams(vmem_limit_bytes=14 * 2**20),
        name="packcond",
    )(number, conduction)


def pack_give_kernel(place_ref, val_ref, out_ref):
    for s in range(CHIPS // 2):
        for band in range(2):
            pack_band(val_ref.at[band, :, s ^ (place_ref[1] & 3), 0], out_ref.at[s, band], 0.0)


def pack_give(valence, place, half):
    block = (2, 2, CHIPS // 2, 1, ROWS, LENGTH)
    return pl.pallas_call(
        pack_give_kernel,
        out_shape=jax.ShapeDtypeStruct((CHIPS // 2, 2, WIRE, 128), BF),
        grid_spec=pltpu.PrefetchScalarGridSpec(
            num_scalar_prefetch=1,
            grid=(1,),
            in_specs=[pl.BlockSpec(block, lambda i, p: (0, 0, half ^ (p[1] >> 2), 1 - p[0], 0, 0))],
            out_specs=pl.BlockSpec((CHIPS // 2, 2, WIRE, 128), lambda i, p: (0, 0, 0, 0)),
        ),
        cost_estimate=pl.CostEstimate(flops=0, transcendentals=0, bytes_accessed=3_000_000),
        compiler_params=pltpu.CompilerParams(vmem_limit_bytes=16 * 2**20),
        name="packgive",
    )(place, valence)


def pack_choice_kernel(place_ref, val_ref, *refs):
    others, outs = refs[:2], refs[2:]

    @pl.when(place_ref[2] == 1)
    def _():
        for s in range(CHIPS):
            for band in range(2):
                pack_band(val_ref.at[band, :, s ^ place_ref[1], 0], outs[s].at[band], 0.0)

    @pl.when(place_ref[2] == 0)
    def _():
        for s in range(CHIPS):
            outs[s][...] = others[s // 4][s % 4]


def pack_choice(valence, place, others):
    piece = (2, WIRE, 128)
    return pl.pallas_call(
        pack_choice_kernel,
        out_shape=[jax.ShapeDtypeStruct(piece, BF)] * CHIPS,
        grid_spec=pltpu.PrefetchScalarGridSpec(
            num_scalar_prefetch=1,
            grid=(1,),
            in_specs=[pl.BlockSpec((2, 2, CHIPS, 1, ROWS, LENGTH), lambda i, p: (0, 0, 0, p[0], 0, 0))]
            + [pl.BlockSpec((CHIPS // 2, 2, WIRE, 128), lambda i, p: (0, 0, 0, 0))] * 2,
            out_specs=[pl.BlockSpec(piece, lambda i, p: (0, 0, 0))] * CHIPS,
        ),
        cost_estimate=pl.CostEstimate(flops=0, transcendentals=0, bytes_accessed=8_000_000),
        compiler_params=pltpu.CompilerParams(vmem_limit_bytes=28 * 2**20),
        name="packchoice",
    )(place, valence, *others)


def send_to_chips(pieces):
    got = [pieces[0]]
    for s in ORDER[1:]:
        got.append(lax.ppermute(pieces[s], "band", [(b, b ^ (2 * s)) for b in range(PARTS)]))
    return got


def unpack_tail(tail):
    return jnp.concatenate([tail[:, :64], tail[: ROWS - TAIL, 64:]], axis=0)


def plane_tables(shift):
    tab = lax.dynamic_index_in_dim(jnp.asarray(y_tables()), shift, 0, keepdims=False)
    tab = tab.reshape(256, 4, 32)[:, :, :SIDE].transpose(1, 0, 2)
    return jnp.pad(jnp.tile(tab, (1, 1, SLOTS)), ((0, 0), (0, 0), (0, 256 - SLOTS * SIDE)))


def z_kernel(where_ref, *refs):
    val_refs, again_ref = refs[:CHIPS], refs[CHIPS]
    cond_ref, table_ref, ytab_ref, out_ref, raw_ref, val_main, val_tail, low_ref, high_ref = refs[CHIPS + 1 :]
    step = pl.program_id(0)

    for slot, s in enumerate(ORDER):
        for r in range(2):

            @pl.when((step == 0) & (where_ref[r] == s))
            def _():
                raw_ref[r] = val_refs[slot][...]

    @pl.when((step == 0) & (where_ref[2] == 1))
    def _():
        raw_ref[1] = again_ref[...]

    @pl.when(step == 0)
    def _():
        for i in range(4):
            src = raw_ref.at[i // 2, i % 2]
            val_main[i, 0] = src[0:ROWS].astype(F32)
            val_main[i, 1] = src[ROWS : 2 * ROWS].astype(F32)
            both = unpack_tail(src[2 * ROWS :].astype(F32))
            val_tail[i] = jnp.concatenate([both, both], axis=1)
        high_ref[...] = jnp.zeros_like(high_ref)

    @pl.loop(0, CONDS, unroll=CONDS)
    def _(c):
        cre = cond_ref[c, 0:ROWS].astype(F32)
        cim = cond_ref[c, ROWS : 2 * ROWS].astype(F32)
        both = unpack_tail(cond_ref[c, 2 * ROWS :].astype(F32))
        ctail = jnp.concatenate([both, both[:, 32:], both[:, :32]], axis=1)
        first = (step * CONDS + c) * 4
        for i in range(0, 4, 2):
            density = []
            for j in (i, i + 1):
                vre, vim = val_main[j, 0], val_main[j, 1]
                density += [vre * cre + vim * cim, vre * cim - vim * cre, val_tail[j] * ctail]
            density = jnp.concatenate(density, axis=1).astype(BF)
            along = lax.dot_general(
                table_ref[...], density, (((1,), (1,)), ((), ())), preferred_element_type=F32
            )
            for j in range(2):
                for part in range(2):
                    start = part * PAIRS + first + i + j
                    at = (2 * j + part) * KROWS
                    piece = along[at : at + KROWS]
                    low_ref[pl.ds(start, KROWS, stride=128), :] = piece[:, :128]
                    high_ref[pl.ds(start, KROWS, stride=128), 0 : ROWS - 128] = piece[:, 128:]

    @pl.when(step == pl.num_programs(0) - 1)
    def _():
        lane = lax.broadcasted_iota(jnp.int32, (256, 256), 1)
        acc = [None] * 4
        for s in range(SLOTS):
            left = []
            for k in (s, s + SLOTS):
                rows = pl.ds(k * 128, 128)
                left.append(jnp.concatenate([low_ref[rows], high_ref[rows]], axis=1).astype(BF))
            left = jnp.concatenate(left, axis=0)
            keep = (lane >= s * SIDE) & (lane < (s + 1) * SIDE)
            for t in range(4):
                right = jnp.where(keep, ytab_ref[t], jnp.zeros((256, 256), BF))
                term = jnp.dot(left, right, preferred_element_type=F32)
                acc[t] = term if acc[t] is None else acc[t] + term
        for x in range(2):
            for tile in range(2):
                c = acc[2 * x][tile * 128 : (tile + 1) * 128]
                s = acc[2 * x + 1][tile * 128 : (tile + 1) * 128]
                lanes = pl.ds(tile * 256, 256)
                out_ref[x * 128 : x * 128 + PAIRS, lanes] = (c[:PAIRS] + s[PAIRS:]).astype(BF)
                out_ref[x * 128 + PAIRS : (x + 1) * 128, lanes] = (c[PAIRS:] - s[:PAIRS]).astype(BF)


def z_transform(where, val_pieces, again, cond_wire, ytab):
    single = z_table()
    table = np.zeros((4 * KROWS, 768), single.dtype)
    table[: 2 * KROWS, :384] = single
    table[2 * KROWS :, 384:] = single
    return pl.pallas_call(
        z_kernel,
        out_shape=jax.ShapeDtypeStruct((256, 512), BF),
        grid_spec=pltpu.PrefetchScalarGridSpec(
            num_scalar_prefetch=1,
            grid=(PARTS // CONDS,),
            in_specs=[
                *[pl.BlockSpec((2, WIRE, 128), lambda c, o: (0, 0, 0))] * (CHIPS + 1),
                pl.BlockSpec((CONDS, WIRE, 128), lambda c, o: (c, 0, 0)),
                pl.BlockSpec((4 * KROWS, 768), lambda c, o: (0, 0)),
                pl.BlockSpec((4, 256, 256), lambda c, o: (0, 0, 0)),
            ],
            out_specs=pl.BlockSpec((256, 512), lambda c, o: (0, 0)),
            scratch_shapes=[
                pltpu.VMEM((2, 2, WIRE, 128), BF),
                pltpu.VMEM((4, 2, ROWS, 128), F32),
                pltpu.VMEM((4, ROWS, 128), F32),
                pltpu.VMEM((KROWS * 128, 128), F32),
                pltpu.VMEM((KROWS * 128, 128), F32),
            ],
        ),
        compiler_params=pltpu.CompilerParams(vmem_limit_bytes=28 * 2**20),
        name="ztransform",
    )(where, *val_pieces, again, cond_wire, in_hbm(jnp.asarray(table)), ytab)


def g_kernel(parity_ref, plane_ref, index_ref, phase_ref, out_ref):
    row = lax.broadcasted_iota(jnp.int32, (512, GCHUNK), 0)
    for chunk in range(out_ref.shape[0]):
        pick = jnp.where(row == index_ref[chunk, 0], 1.0, 0.0).astype(BF)
        at = jnp.dot(plane_ref[...], pick, preferred_element_type=F32)
        real = jnp.zeros((PAIRS, GCHUNK), F32)
        imag = jnp.zeros((PAIRS, GCHUNK), F32)
        for x in range(2):
            c = phase_ref[chunk, 0, 2 * x : 2 * x + 1]
            s = phase_ref[chunk, 0, 2 * x + 1 : 2 * x + 2]
            re = at[x * 128 : x * 128 + PAIRS]
            im = at[x * 128 + PAIRS : (x + 1) * 128]
            real = real + re * c + im * s
            imag = imag + im * c - re * s
        out_ref[chunk, :PAIRS] = real.astype(out_ref.dtype)
        out_ref[chunk, PAIRS:] = imag.astype(out_ref.dtype)


def g_elements(parity, plane, index, phase, dtype):
    chips = index.shape[0]
    return pl.pallas_call(
        g_kernel,
        out_shape=jax.ShapeDtypeStruct((chips, 128, GCHUNK), dtype),
        grid_spec=pltpu.PrefetchScalarGridSpec(
            num_scalar_prefetch=1,
            grid=(1,),
            in_specs=[
                pl.BlockSpec((256, 512), lambda i, k: (0, 0)),
                pl.BlockSpec((chips, 1, 1, GCHUNK), lambda i, k: (0, k[0], 0, 0)),
                pl.BlockSpec((chips, 1, 4, GCHUNK), lambda i, k: (0, k[0], 0, 0)),
            ],
            out_specs=pl.BlockSpec((chips, 128, GCHUNK), lambda i, k: (0, 0, 0)),
        ),
        compiler_params=pltpu.CompilerParams(vmem_limit_bytes=10 * 2**20),
        cost_estimate=pl.CostEstimate(flops=2 * 10**9, transcendentals=0, bytes_accessed=12_000_000),
        name="gelements",
    )(parity, plane, index, phase)


def chi_kernel(core_ref, mine_ref, column_ref, other_ref, weight_ref, out_ref):
    real = column_ref[...].astype(F32) * weight_ref[...]
    imag = jnp.concatenate([-real[PAIRS:], real[:PAIRS]], axis=0)
    sides = []
    for side in (real, imag):
        top = side.astype(BF)
        sides.append((top, (side - top.astype(F32)).astype(BF)))
    for half, rows in ((core_ref[0], mine_ref[...]), (1 - core_ref[0], other_ref[...])):
        at = pl.ds(pl.multiple_of(half * GCHUNK, GCHUNK), GCHUNK)
        for part in range(2):
            total = None
            for piece in sides[part]:
                term = lax.dot_general(rows, piece, (((0,), (0,)), ((), ())), preferred_element_type=F32)
                total = term if total is None else total + term
            out_ref[part, at, :] = total


def chi_block(core, mine, other, column, weight):
    spec = pl.BlockSpec((128, GCHUNK), lambda i, k: (0, 0))
    return pl.pallas_call(
        chi_kernel,
        out_shape=jax.ShapeDtypeStruct((2, 2 * GCHUNK, GCHUNK), F32),
        grid_spec=pltpu.PrefetchScalarGridSpec(
            num_scalar_prefetch=1,
            grid=(1,),
            in_specs=[spec, spec, spec, pl.BlockSpec((128, 1), lambda i, k: (0, 0))],
            out_specs=pl.BlockSpec((2, 2 * GCHUNK, GCHUNK), lambda i, k: (0, 0, 0)),
        ),
        compiler_params=pltpu.CompilerParams(vmem_limit_bytes=8 * 2**20),
        name="chi",
    )(core, mine, column, other, weight)


def shards(valence, conduction, val_energy, cond_energy, cond_band, owners, gvectors):
    grid_pos = lax.axis_index("grid")
    band_pos = lax.axis_index("band")
    x_local = valence.shape[2]
    n_grid = lax.axis_size("grid")

    rows_all = x_local * LENGTH
    cond_wire = pack_cond(in_hbm(conduction.reshape(2, rows_all, LENGTH)), cond_band)
    cond_wire, core = lax.optimization_barrier((cond_wire, band_pos & 1))
    cond_wire = lax.all_to_all(cond_wire, "band", 0, 0, tiled=True)

    first, second = owners[0], owners[1]
    chip = band_pos >> 1
    siblings = [(b, b ^ 1) for b in range(PARTS)]
    bands = in_hbm(valence.reshape(2, 2, CHIPS, 2, ROWS, LENGTH))
    place = jnp.stack([core, chip])
    sibling = [lax.ppermute(pack_give(bands, place, half), "band", siblings) for half in range(2)]
    here = (first >> 1) == chip
    own = jnp.where(here, first == band_pos, second == band_pos)
    place = jnp.stack([core, chip, own.astype(jnp.int32)])
    pieces = send_to_chips(pack_choice(bands, place, sibling))
    ytab = plane_tables(band_pos & 3)

    def exchange_again(operands):
        bands, sibling = operands
        place = jnp.stack([core, chip, (second == band_pos).astype(jnp.int32)])
        again = send_to_chips(pack_choice(bands, place, sibling))
        found = again[0]
        for slot, s in enumerate(ORDER[1:], 1):
            found = jnp.where((second >> 1) == chip ^ s, again[slot], found)
        return found

    def nothing_more(operands):
        return jnp.zeros((2, WIRE, 128), BF)

    both = (first != second) & ((first >> 1) == (second >> 1))
    cond_wire, both, pieces = lax.optimization_barrier((cond_wire, both, pieces))
    again = lax.cond(both, exchange_again, nothing_more, (bands, sibling))
    where = jnp.stack([(first >> 1) ^ chip, (second >> 1) ^ chip, both.astype(jnp.int32)])
    plane = z_transform(where, pieces, again, in_hbm(cond_wire), ytab)

    numbers = cond_wire[:, WIRE - 1, 127].astype(jnp.int32)
    order = jnp.arange(cond_energy.shape[0], dtype=jnp.int32)
    levels = jnp.sum(jnp.where(numbers[:, None] == order[None, :], cond_energy[None, :], 0.0), axis=1)
    val_index = (owners[:, None] * 2 + jnp.arange(2, dtype=jnp.int32)[None, :]).reshape(4)
    val_levels = val_energy[val_index]
    weight = (2.0 / (PAIRS * (val_levels[None, :] - levels[:, None]))).reshape(PAIRS)

    signed = (gvectors + GMAX) % LENGTH
    slot = jnp.where(signed[2] < SLOTS, signed[2] * SIDE, 256 + (signed[2] - SLOTS) * SIDE)
    index = (slot + signed[1]).reshape(PARTS // 2, 2, 1, GCHUNK)
    x_first = grid_pos * x_local + 5 * (band_pos >> 2) + (band_pos & 3)
    norm = float(LENGTH) ** (-1.5)
    waves = []
    for x in range(2):
        angle = (gvectors[0] * (x_first + x) % LENGTH).astype(F32) * (2.0 * math.pi / LENGTH)
        waves += [jnp.cos(angle), jnp.sin(angle)]
    phase = jnp.stack(waves).astype(BF).astype(F32) * norm
    phase = phase.reshape(4, PARTS, GCHUNK).transpose(1, 0, 2).reshape(PARTS // 2, 2, 4, GCHUNK)

    core = band_pos & 1
    away = g_elements((1 - core)[None], plane, index, phase, BF)
    come = lax.ppermute(away, "band", siblings)
    keep = g_elements(core[None], plane, index, phase, F32)
    parts = (keep + come.astype(F32)).astype(BF)
    parts = lax.all_to_all(parts, "grid", 0, 0, tiled=True)
    block = jnp.sum(parts.astype(F32), axis=0)
    block = block + lax.ppermute(block.astype(BF), "band", [(b, b ^ 2) for b in range(PARTS)]).astype(F32)
    narrow = block.astype(BF)
    for turn in (4, 8, 12):
        step = [(b, (b + turn) % PARTS) for b in range(PARTS)]
        block = block + lax.ppermute(narrow, "band", step).astype(F32)

    narrow = block.astype(BF)
    far = []
    for b in range(PARTS):
        for g in range(n_grid):
            x, zl, y, zh = b >> 2, (b >> 1) & 1, g >> 1, g & 1
            to_x, to_zl, to_y, to_zh = y, zh, (2 * y + 2 - x) % 4, zl
            to_b = to_x * 4 + to_zl * 2 + (b & 1)
            far.append((b * n_grid + g, to_b * n_grid + to_y * 2 + to_zh))
    column = lax.ppermute(narrow, ("band", "grid"), far)
    other = lax.ppermute(narrow, "band", siblings)
    return chi_block(core[None], narrow, other, column, jnp.concatenate([weight, weight])[:, None])


def solution(mesh):
    return jax.shard_map(
        shards,
        mesh=mesh,
        in_specs=(
            P("band", None, "grid", None, None),
            P("band", None, "grid", None, None),
            P(),
            P(),
            P("band"),
            P(),
            P(),
        ),
        out_specs=P(None, "grid", "band"),
        check_vma=False,
    )
```

```python
import functools
import math

import jax
import jax.numpy as jnp
import numpy as np
from jax import lax
from jax.experimental import pallas as pl
from jax.experimental.pallas import tpu as pltpu
from jax.sharding import PartitionSpec as P

LENGTH = 160
GMAX = 10
SIDE = 2 * GMAX + 1
PARTS = 16
ROWS = 200
TAIL = 104
WIRE = 2 * ROWS + TAIL
PAIRS = 64
PACK = 8
CHIPS = 8
ORDER = (0, 2, 6, 4, 1, 3, 7, 5)
CONDS = 8
SLOTS = 12
KROWS = 24
GCHUNK = 256
BF = jnp.bfloat16
F32 = jnp.float32


def host_tables():
    freq = (np.arange(SIDE) - GMAX) % LENGTH
    pos = np.arange(LENGTH)
    angle = ((freq[:, None] * pos[None, :]) % LENGTH).astype(np.float32) * np.float32(2.0 * math.pi / LENGTH)
    rnd = lambda a: a.astype(np.float32).astype(jnp.bfloat16).astype(np.float32)
    return rnd(np.cos(angle)), rnd(np.sin(angle))


def z_table():
    cos, sin = host_tables()
    out = np.zeros((2 * KROWS, 384), np.float32)
    cm, sm, ct, st = cos[:, :128], sin[:, :128], cos[:, 128:], sin[:, 128:]
    out[:SIDE] = np.concatenate([cm, sm, ct, ct, st, -st], axis=1)
    out[KROWS : KROWS + SIDE] = np.concatenate([-sm, cm, -st, -st, ct, -ct], axis=1)
    return out.astype(jnp.bfloat16)


def y_tables():
    cos, sin = host_tables()
    out = np.zeros((4, 256, 4, 32), np.float32)
    for shift in range(4):
        for row in range(ROWS):
            flat = 40 * shift + row
            x, y = divmod(flat, LENGTH)
            out[shift, row, 2 * x, :SIDE] = cos[:, y]
            out[shift, row, 2 * x + 1, :SIDE] = sin[:, y]
    return out.reshape(4, 256, 128).astype(jnp.bfloat16)


def in_hbm(array):
    return pltpu.with_memory_space_constraint(array, pltpu.HBM)


def pack_band(src, out, fill):
    real, imag = src[0], src[1]
    out[0:ROWS] = real[:, :128]
    out[ROWS : 2 * ROWS] = imag[:, :128]
    tail = jnp.concatenate([real[:, 128:].astype(F32), imag[:, 128:].astype(F32)], axis=1)
    low = tail[:TAIL]
    high = jnp.concatenate([tail[TAIL:], jnp.full((2 * TAIL - ROWS, 64), 1.0, F32) * fill], axis=0)
    out[2 * ROWS :] = jnp.concatenate([low, high], axis=1).astype(BF)


def pack_cond_kernel(number_ref, cond_ref, out_ref):
    for t in range(PACK):
        rows = pl.ds(t * ROWS, ROWS)
        pack_band(cond_ref.at[:, rows], out_ref.at[t], number_ref[0].astype(F32))


def pack_cond(conduction, number):
    return pl.pallas_call(
        pack_cond_kernel,
        out_shape=pltpu.HBM((PARTS, WIRE, 128), BF),
        grid_spec=pltpu.PrefetchScalarGridSpec(
            num_scalar_prefetch=1,
            grid=(PARTS // PACK,),
            in_specs=[pl.BlockSpec((2, PACK * ROWS, LENGTH), lambda t, n: (0, t, 0))],
            out_specs=pl.BlockSpec((PACK, WIRE, 128), lambda t, n: (t, 0, 0)),
        ),
        cost_estimate=pl.CostEstimate(flops=0, transcendentals=0, bytes_accessed=6_000_000),
        compiler_params=pltpu.CompilerParams(vmem_limit_bytes=14 * 2**20),
        name="packcond",
    )(number, conduction)


def pack_give_kernel(place_ref, val_ref, out_ref):
    for s in range(CHIPS // 2):
        for band in range(2):
            pack_band(val_ref.at[band, :, s ^ (place_ref[1] & 3), 0], out_ref.at[s, band], 0.0)


def pack_give(valence, place, half):
    block = (2, 2, CHIPS // 2, 1, ROWS, LENGTH)
    return pl.pallas_call(
        pack_give_kernel,
        out_shape=jax.ShapeDtypeStruct((CHIPS // 2, 2, WIRE, 128), BF),
        grid_spec=pltpu.PrefetchScalarGridSpec(
            num_scalar_prefetch=1,
            grid=(1,),
            in_specs=[pl.BlockSpec(block, lambda i, p: (0, 0, half ^ (p[1] >> 2), 1 - p[0], 0, 0))],
            out_specs=pl.BlockSpec((CHIPS // 2, 2, WIRE, 128), lambda i, p: (0, 0, 0, 0)),
        ),
        cost_estimate=pl.CostEstimate(flops=0, transcendentals=0, bytes_accessed=3_000_000),
        compiler_params=pltpu.CompilerParams(vmem_limit_bytes=16 * 2**20),
        name="packgive",
    )(place, valence)


def pack_choice_kernel(place_ref, val_ref, *refs):
    others, outs = refs[:2], refs[2:]

    @pl.when(place_ref[2] == 1)
    def _():
        for s in range(CHIPS):
            for band in range(2):
                pack_band(val_ref.at[band, :, s ^ place_ref[1], 0], outs[s].at[band], 0.0)

    @pl.when(place_ref[2] == 0)
    def _():
        for s in range(CHIPS):
            outs[s][...] = others[s // 4][s % 4]


def pack_choice(valence, place, others):
    piece = (2, WIRE, 128)
    return pl.pallas_call(
        pack_choice_kernel,
        out_shape=[jax.ShapeDtypeStruct(piece, BF)] * CHIPS,
        grid_spec=pltpu.PrefetchScalarGridSpec(
            num_scalar_prefetch=1,
            grid=(1,),
            in_specs=[pl.BlockSpec((2, 2, CHIPS, 1, ROWS, LENGTH), lambda i, p: (0, 0, 0, p[0], 0, 0))]
            + [pl.BlockSpec((CHIPS // 2, 2, WIRE, 128), lambda i, p: (0, 0, 0, 0))] * 2,
            out_specs=[pl.BlockSpec(piece, lambda i, p: (0, 0, 0))] * CHIPS,
        ),
        cost_estimate=pl.CostEstimate(flops=0, transcendentals=0, bytes_accessed=8_000_000),
        compiler_params=pltpu.CompilerParams(vmem_limit_bytes=28 * 2**20),
        name="packchoice",
    )(place, valence, *others)


def send_to_chips(pieces):
    got = [pieces[0]]
    for s in ORDER[1:]:
        got.append(lax.ppermute(pieces[s], "band", [(b, b ^ (2 * s)) for b in range(PARTS)]))
    return got


def unpack_tail(tail):
    return jnp.concatenate([tail[:, :64], tail[: ROWS - TAIL, 64:]], axis=0)


def plane_tables(shift):
    tab = lax.dynamic_index_in_dim(jnp.asarray(y_tables()), shift, 0, keepdims=False)
    tab = tab.reshape(256, 4, 32)[:, :, :SIDE].transpose(1, 0, 2)
    return jnp.pad(jnp.tile(tab, (1, 1, SLOTS)), ((0, 0), (0, 0), (0, 256 - SLOTS * SIDE)))


def z_kernel(where_ref, *refs):
    val_refs, again_ref = refs[:CHIPS], refs[CHIPS]
    cond_ref, table_ref, ytab_ref, out_ref, raw_ref, val_main, val_tail, low_ref, high_ref = refs[CHIPS + 1 :]
    step = pl.program_id(0)

    for slot, s in enumerate(ORDER):
        for r in range(2):

            @pl.when((step == 0) & (where_ref[r] == s))
            def _():
                raw_ref[r] = val_refs[slot][...]

    @pl.when((step == 0) & (where_ref[2] == 1))
    def _():
        raw_ref[1] = again_ref[...]

    @pl.when(step == 0)
    def _():
        for i in range(4):
            src = raw_ref.at[i // 2, i % 2]
            val_main[i, 0] = src[0:ROWS].astype(F32)
            val_main[i, 1] = src[ROWS : 2 * ROWS].astype(F32)
            both = unpack_tail(src[2 * ROWS :].astype(F32))
            val_tail[i] = jnp.concatenate([both, both], axis=1)
        high_ref[...] = jnp.zeros_like(high_ref)

    @pl.loop(0, CONDS, unroll=CONDS)
    def _(c):
        cre = cond_ref[c, 0:ROWS].astype(F32)
        cim = cond_ref[c, ROWS : 2 * ROWS].astype(F32)
        both = unpack_tail(cond_ref[c, 2 * ROWS :].astype(F32))
        ctail = jnp.concatenate([both, both[:, 32:], both[:, :32]], axis=1)
        first = (step * CONDS + c) * 4
        for i in range(0, 4, 2):
            density = []
            for j in (i, i + 1):
                vre, vim = val_main[j, 0], val_main[j, 1]
                density += [vre * cre + vim * cim, vre * cim - vim * cre, val_tail[j] * ctail]
            density = jnp.concatenate(density, axis=1).astype(BF)
            along = lax.dot_general(
                table_ref[...], density, (((1,), (1,)), ((), ())), preferred_element_type=F32
            )
            for j in range(2):
                for part in range(2):
                    start = part * PAIRS + first + i + j
                    at = (2 * j + part) * KROWS
                    piece = along[at : at + KROWS]
                    low_ref[pl.ds(start, KROWS, stride=128), :] = piece[:, :128]
                    high_ref[pl.ds(start, KROWS, stride=128), 0 : ROWS - 128] = piece[:, 128:]

    @pl.when(step == pl.num_programs(0) - 1)
    def _():
        lane = lax.broadcasted_iota(jnp.int32, (256, 256), 1)
        acc = [None] * 4
        for s in range(SLOTS):
            left = []
            for k in (s, s + SLOTS):
                rows = pl.ds(k * 128, 128)
                left.append(jnp.concatenate([low_ref[rows], high_ref[rows]], axis=1).astype(BF))
            left = jnp.concatenate(left, axis=0)
            keep = (lane >= s * SIDE) & (lane < (s + 1) * SIDE)
            for t in range(4):
                right = jnp.where(keep, ytab_ref[t], jnp.zeros((256, 256), BF))
                term = jnp.dot(left, right, preferred_element_type=F32)
                acc[t] = term if acc[t] is None else acc[t] + term
        for x in range(2):
            for tile in range(2):
                c = acc[2 * x][tile * 128 : (tile + 1) * 128]
                s = acc[2 * x + 1][tile * 128 : (tile + 1) * 128]
                lanes = pl.ds(tile * 256, 256)
                out_ref[x * 128 : x * 128 + PAIRS, lanes] = (c[:PAIRS] + s[PAIRS:]).astype(BF)
                out_ref[x * 128 + PAIRS : (x + 1) * 128, lanes] = (c[PAIRS:] - s[:PAIRS]).astype(BF)


def z_transform(where, val_pieces, again, cond_wire, ytab):
    single = z_table()
    table = np.zeros((4 * KROWS, 768), single.dtype)
    table[: 2 * KROWS, :384] = single
    table[2 * KROWS :, 384:] = single
    return pl.pallas_call(
        z_kernel,
        out_shape=jax.ShapeDtypeStruct((256, 512), BF),
        grid_spec=pltpu.PrefetchScalarGridSpec(
            num_scalar_prefetch=1,
            grid=(PARTS // CONDS,),
            in_specs=[
                *[pl.BlockSpec((2, WIRE, 128), lambda c, o: (0, 0, 0))] * (CHIPS + 1),
                pl.BlockSpec((CONDS, WIRE, 128), lambda c, o: (c, 0, 0)),
                pl.BlockSpec((4 * KROWS, 768), lambda c, o: (0, 0)),
                pl.BlockSpec((4, 256, 256), lambda c, o: (0, 0, 0)),
            ],
            out_specs=pl.BlockSpec((256, 512), lambda c, o: (0, 0)),
            scratch_shapes=[
                pltpu.VMEM((2, 2, WIRE, 128), BF),
                pltpu.VMEM((4, 2, ROWS, 128), F32),
                pltpu.VMEM((4, ROWS, 128), F32),
                pltpu.VMEM((KROWS * 128, 128), F32),
                pltpu.VMEM((KROWS * 128, 128), F32),
            ],
        ),
        compiler_params=pltpu.CompilerParams(vmem_limit_bytes=28 * 2**20),
        name="ztransform",
    )(where, *val_pieces, again, cond_wire, in_hbm(jnp.asarray(table)), ytab)


def g_kernel(parity_ref, plane_ref, index_ref, phase_ref, out_ref):
    row = lax.broadcasted_iota(jnp.int32, (512, GCHUNK), 0)
    for chunk in range(out_ref.shape[0]):
        pick = jnp.where(row == index_ref[chunk, 0], 1.0, 0.0).astype(BF)
        at = jnp.dot(plane_ref[...], pick, preferred_element_type=F32)
        real = jnp.zeros((PAIRS, GCHUNK), F32)
        imag = jnp.zeros((PAIRS, GCHUNK), F32)
        for x in range(2):
            c = phase_ref[chunk, 0, 2 * x : 2 * x + 1]
            s = phase_ref[chunk, 0, 2 * x + 1 : 2 * x + 2]
            re = at[x * 128 : x * 128 + PAIRS]
            im = at[x * 128 + PAIRS : (x + 1) * 128]
            real = real + re * c + im * s
            imag = imag + im * c - re * s
        out_ref[chunk, :PAIRS] = real.astype(out_ref.dtype)
        out_ref[chunk, PAIRS:] = imag.astype(out_ref.dtype)


def g_elements(parity, plane, index, phase, dtype):
    chips = index.shape[0]
    return pl.pallas_call(
        g_kernel,
        out_shape=jax.ShapeDtypeStruct((chips, 128, GCHUNK), dtype),
        grid_spec=pltpu.PrefetchScalarGridSpec(
            num_scalar_prefetch=1,
            grid=(1,),
            in_specs=[
                pl.BlockSpec((256, 512), lambda i, k: (0, 0)),
                pl.BlockSpec((chips, 1, 1, GCHUNK), lambda i, k: (0, k[0], 0, 0)),
                pl.BlockSpec((chips, 1, 4, GCHUNK), lambda i, k: (0, k[0], 0, 0)),
            ],
            out_specs=pl.BlockSpec((chips, 128, GCHUNK), lambda i, k: (0, 0, 0)),
        ),
        compiler_params=pltpu.CompilerParams(vmem_limit_bytes=10 * 2**20),
        cost_estimate=pl.CostEstimate(flops=2 * 10**9, transcendentals=0, bytes_accessed=12_000_000),
        name="gelements",
    )(parity, plane, index, phase)


def chi_kernel(core_ref, mine_ref, column_ref, other_ref, weight_ref, out_ref):
    real = column_ref[...].astype(F32) * weight_ref[...]
    imag = jnp.concatenate([-real[PAIRS:], real[:PAIRS]], axis=0)
    sides = []
    for side in (real, imag):
        top = side.astype(BF)
        sides.append((top, (side - top.astype(F32)).astype(BF)))
    for half, rows in ((core_ref[0], mine_ref[...]), (1 - core_ref[0], other_ref[...])):
        at = pl.ds(pl.multiple_of(half * GCHUNK, GCHUNK), GCHUNK)
        for part in range(2):
            total = None
            for piece in sides[part]:
                term = lax.dot_general(rows, piece, (((0,), (0,)), ((), ())), preferred_element_type=F32)
                total = term if total is None else total + term
            out_ref[part, at, :] = total


def chi_block(core, mine, other, column, weight):
    spec = pl.BlockSpec((128, GCHUNK), lambda i, k: (0, 0))
    return pl.pallas_call(
        chi_kernel,
        out_shape=jax.ShapeDtypeStruct((2, 2 * GCHUNK, GCHUNK), F32),
        grid_spec=pltpu.PrefetchScalarGridSpec(
            num_scalar_prefetch=1,
            grid=(1,),
            in_specs=[spec, spec, spec, pl.BlockSpec((128, 1), lambda i, k: (0, 0))],
            out_specs=pl.BlockSpec((2, 2 * GCHUNK, GCHUNK), lambda i, k: (0, 0, 0)),
        ),
        compiler_params=pltpu.CompilerParams(vmem_limit_bytes=8 * 2**20),
        name="chi",
    )(core, mine, column, other, weight)


def shards(valence, conduction, val_energy, cond_energy, cond_band, owners, gvectors):
    grid_pos = lax.axis_index("grid")
    band_pos = lax.axis_index("band")
    x_local = valence.shape[2]
    n_grid = lax.axis_size("grid")

    rows_all = x_local * LENGTH
    cond_wire = pack_cond(in_hbm(conduction.reshape(2, rows_all, LENGTH)), cond_band)
    cond_wire, core = lax.optimization_barrier((cond_wire, band_pos & 1))
    cond_wire = lax.all_to_all(cond_wire, "band", 0, 0, tiled=True)

    first, second = owners[0], owners[1]
    chip = band_pos >> 1
    siblings = [(b, b ^ 1) for b in range(PARTS)]
    bands = in_hbm(valence.reshape(2, 2, CHIPS, 2, ROWS, LENGTH))
    place = jnp.stack([core, chip])
    sibling = [lax.ppermute(pack_give(bands, place, half), "band", siblings) for half in range(2)]
    here = (first >> 1) == chip
    own = jnp.where(here, first == band_pos, second == band_pos)
    place = jnp.stack([core, chip, own.astype(jnp.int32)])
    pieces = send_to_chips(pack_choice(bands, place, sibling))
    ytab = plane_tables(band_pos & 3)

    def exchange_again(operands):
        bands, sibling = operands
        place = jnp.stack([core, chip, (second == band_pos).astype(jnp.int32)])
        again = send_to_chips(pack_choice(bands, place, sibling))
        found = again[0]
        for slot, s in enumerate(ORDER[1:], 1):
            found = jnp.where((second >> 1) == chip ^ s, again[slot], found)
        return found

    def nothing_more(operands):
        return jnp.zeros((2, WIRE, 128), BF)

    both = (first != second) & ((first >> 1) == (second >> 1))
    cond_wire, both, pieces = lax.optimization_barrier((cond_wire, both, pieces))
    again = lax.cond(both, exchange_again, nothing_more, (bands, sibling))
    where = jnp.stack([(first >> 1) ^ chip, (second >> 1) ^ chip, both.astype(jnp.int32)])
    plane = z_transform(where, pieces, again, in_hbm(cond_wire), ytab)

    numbers = cond_wire[:, WIRE - 1, 127].astype(jnp.int32)
    order = jnp.arange(cond_energy.shape[0], dtype=jnp.int32)
    levels = jnp.sum(jnp.where(numbers[:, None] == order[None, :], cond_energy[None, :], 0.0), axis=1)
    val_index = (owners[:, None] * 2 + jnp.arange(2, dtype=jnp.int32)[None, :]).reshape(4)
    val_levels = val_energy[val_index]
    weight = (2.0 / (PAIRS * (val_levels[None, :] - levels[:, None]))).reshape(PAIRS)

    signed = (gvectors + GMAX) % LENGTH
    slot = jnp.where(signed[2] < SLOTS, signed[2] * SIDE, 256 + (signed[2] - SLOTS) * SIDE)
    index = (slot + signed[1]).reshape(PARTS // 2, 2, 1, GCHUNK)
    x_first = grid_pos * x_local + 5 * (band_pos >> 2) + (band_pos & 3)
    norm = float(LENGTH) ** (-1.5)
    waves = []
    for x in range(2):
        angle = (gvectors[0] * (x_first + x) % LENGTH).astype(F32) * (2.0 * math.pi / LENGTH)
        waves += [jnp.cos(angle), jnp.sin(angle)]
    phase = jnp.stack(waves).astype(BF).astype(F32) * norm
    phase = phase.reshape(4, PARTS, GCHUNK).transpose(1, 0, 2).reshape(PARTS // 2, 2, 4, GCHUNK)

    core = band_pos & 1
    away = g_elements((1 - core)[None], plane, index, phase, BF)
    come = lax.ppermute(away, "band", siblings)
    keep = g_elements(core[None], plane, index, phase, F32)
    parts = (keep + come.astype(F32)).astype(BF)
    parts = lax.all_to_all(parts, "grid", 0, 0, tiled=True)
    block = jnp.sum(parts.astype(F32), axis=0)
    block = block + lax.ppermute(block.astype(BF), "band", [(b, b ^ 2) for b in range(PARTS)]).astype(F32)
    narrow = block.astype(BF)
    for turn in (4, 8, 12):
        step = [(b, (b + turn) % PARTS) for b in range(PARTS)]
        block = block + lax.ppermute(narrow, "band", step).astype(F32)

    narrow = block.astype(BF)
    far = []
    for b in range(PARTS):
        for g in range(n_grid):
            x, zl, y, zh = b >> 2, (b >> 1) & 1, g >> 1, g & 1
            to_x, to_zl, to_y, to_zh = y, zh, (2 * y + 2 - x) % 4, zl
            to_b = to_x * 4 + to_zl * 2 + (b & 1)
            far.append((b * n_grid + g, to_b * n_grid + to_y * 2 + to_zh))
    column = lax.ppermute(narrow, ("band", "grid"), far)
    other = lax.ppermute(narrow, "band", siblings)
    return chi_block(core[None], narrow, other, column, jnp.concatenate([weight, weight])[:, None])


def solution(mesh):
    return jax.shard_map(
        shards,
        mesh=mesh,
        in_specs=(
            P("band", None, "grid", None, None),
            P("band", None, "grid", None, None),
            P(),
            P(),
            P("band"),
            P(),
            P(),
        ),
        out_specs=P(None, "grid", "band"),
        check_vma=False,
    )
```
